32 devices in a mesh: dp: 2 (over y), seq: 16 (over z, x, core).
Axes of the slice: x: 2, y: 2, z: 4, core: 2. Of those that a mesh axis runs over, the one named last changes fastest.
Arguments:
- inputs: bfloat16 [2, 2, 1024, 1024], P(None, 'dp', 'seq'), may hold values from -6 to 6
- teacher: bfloat16 [2, 2, 1024, 1024], P(None, 'dp', 'seq')
- valid_mask: int32 [2, 2, 1024], P(None, 'dp', 'seq'), may hold values from 0 to 1
- prefix: int32 [2, 2], P(None, 'dp'), may hold values from 1 to 512, as said below
- attn_in: bfloat16 [3072, 1024], P(('dp', 'seq')), may hold values from -0.1875 to 0.1875
- attn_out: bfloat16 [1024, 1024], P(('dp', 'seq')), may hold values from -2.5 to 2.5
- mlp_in: bfloat16 [8192, 1024], P(('dp', 'seq')), may hold values from -0.1875 to 0.1875
- mlp_out: bfloat16 [4096, 1024], P(('dp', 'seq')), may hold values from -0.09375 to 0.09375
- norm_gains: float32 [2, 1024], replicated, may hold values from 0.1 to 1.9
Outputs:
- output: bfloat16 [2, 2, 1024, 1024], P(None, 'dp', 'seq')
- losses: float32 [2], replicated
- input_grad: float32 [2, 2, 1024, 1024], P(None, 'dp', 'seq')
- attn_in_grad: float32 [3072, 1024], P(('dp', 'seq'))
- attn_out_grad: float32 [1024, 1024], P(('dp', 'seq'))
- mlp_in_grad: float32 [8192, 1024], P(('dp', 'seq'))
- mlp_out_grad: float32 [4096, 1024], P(('dp', 'seq'))
- gain_grad: float32 [2, 1024], replicated
The draws below stay inside these ranges and needn't reach their ends.
Inputs may be any that keep to these rules, and one draw needn't show every extreme that they name: Each sequence's prefix length is drawn evenly from 1 to 512, and one sequence has a prefix of exactly 512.
All inputs are finite; a program needn't handle non-finite values.
Results may differ from the reference program's by a relative error of at most 0.017.
Values may be sent and summed in bfloat16 or wider, within the bound.
No kernel may reach another device: no remote copies, remote signals or barrier semaphores. Data moves between devices by JAX's collectives and lax.ppermute only.
A program may use at most 256 MiB of HBM per device.

```python
import jax
import jax.numpy as jnp
from jax import lax

D = 1024
HEADS = 16
HEAD_DIM = 64
FF = 4096
MB = 2
PAIR = 2
SEQ_LEN = 1024


def draw_prefix(key, part):
    first, second = jax.random.split(jax.random.fold_in(key, 11))
    drawn = jax.random.randint(first, (MB, PAIR), 1, SEQ_LEN // 2 + 1, dtype=jnp.int32)
    chosen = jax.random.randint(second, (), 0, MB * PAIR, dtype=jnp.int32)
    flat_index = jnp.arange(MB * PAIR, dtype=jnp.int32).reshape(MB, PAIR)
    return jnp.where(flat_index == chosen, SEQ_LEN // 2, drawn).astype(jnp.int32)


def draw_valid_mask(key, part):
    position = jnp.arange(SEQ_LEN, dtype=jnp.int32)
    drawn = jax.random.randint(jax.random.fold_in(key, 23), (MB, PAIR, SEQ_LEN), 0, 4 * SEQ_LEN, dtype=jnp.int32)
    return (drawn < SEQ_LEN + 2 * position[None, None, :]).astype(jnp.int32)


def draw_teacher(key, part):
    position = jnp.arange(SEQ_LEN, dtype=jnp.float32) / SEQ_LEN
    rising = (0.5 + position)[None, None, :, None]
    noise = jax.random.normal(jax.random.fold_in(key, 37), (MB, PAIR, SEQ_LEN, D), jnp.float32)
    return (noise * rising).astype(jnp.bfloat16)


def block_scale(rng, extent, cuts, least, largest):
    loudness = 1.0
    for dim, blocks in cuts:
        steps = jax.random.uniform(jax.random.fold_in(jax.random.fold_in(rng, 6), dim), (blocks,), jnp.float32, least / len(cuts), largest / len(cuts))
        loudness = loudness * jnp.repeat(jnp.exp(steps), extent[dim] // blocks).reshape((-1,) + (1,) * (len(extent) - 1 - dim))
    return loudness


def normal_values(rng, shape, deviation, limit, cuts=(), held_as=jnp.bfloat16):
    loudness = block_scale(rng, shape, cuts, -0.22, 0.18) if cuts else 1.0
    values = jax.random.normal(rng, shape, jnp.float32) * deviation * loudness
    return jnp.minimum(jnp.maximum(values, -limit), limit).astype(held_as)


def setup_inputs(seed: int = 0) -> dict:
    key_list = jax.random.split(jax.random.key(seed), 10)
    return {
        "inputs": normal_values(key_list[0], (MB, PAIR, SEQ_LEN, D), 1.0, 6.0, ((1, 2), (2, 16))),
        "teacher": draw_teacher(jax.random.fold_in(key_list[9], 71), 0),
        "valid_mask": draw_valid_mask(jax.random.fold_in(key_list[9], 71), 0),
        "prefix": draw_prefix(jax.random.fold_in(key_list[9], 71), 0),
        "attn_in": normal_values(key_list[4], (3 * D, D), D ** -0.5, 0.1875, ((0, 32),)),
        "attn_out": normal_values(key_list[5], (D, D), (max(1, 5 * D // SEQ_LEN)) ** -0.5, 2.5, ((0, 32),)),
        "mlp_in": normal_values(key_list[6], (2 * FF, D), D ** -0.5, 0.1875, ((0, 32),)),
        "mlp_out": normal_values(key_list[7], (FF, D), FF ** -0.5, 0.09375, ((0, 32),)),
        "norm_gains": jnp.clip(1.0 + 0.18 * jax.random.normal(key_list[8], (2, D), jnp.float32), 0.1, 1.9),
    }


EPS = 1e-05
NEG = -1e+30
HIGH = lax.Precision.HIGHEST

@jax.custom_vjp
def low(v):
    return lax.optimization_barrier(v.astype(jnp.bfloat16)).astype(jnp.float32)

@jax.custom_vjp
def low_back(v):
    return v

def low_keep(v):
    return (low(v), None)

def low_pass(kept, grad):
    return (grad,)

def back_keep(v):
    return (v, None)

def back_low(kept, grad):
    return (low(grad),)
low.defvjp(low_keep, low_pass)
low_back.defvjp(back_keep, back_low)

def matmul(left, right):
    return jnp.dot(left, right, precision=HIGH, preferred_element_type=jnp.float32)

def rms_scale(rows):
    return lax.rsqrt(lax.optimization_barrier(jnp.mean(rows * rows, axis=-1, keepdims=True)) + EPS)

def attend(queries, key_heads, value_heads, prefix_len):
    seq_rows = queries.shape[0]
    block_rows = min(512, seq_rows)
    key_pos = jnp.arange(seq_rows, dtype=jnp.int32)
    score_scale = HEAD_DIM ** (-0.5)

    def one_block(first_row):
        query_block = lax.dynamic_slice_in_dim(queries, first_row, block_rows, 0)
        query_pos = first_row + jnp.arange(block_rows, dtype=jnp.int32)
        scores = low_back(jnp.einsum('qhd,khd->hqk', query_block, key_heads, precision=HIGH) * score_scale)
        allowed = (key_pos[None, :] <= query_pos[:, None]) | (key_pos[None, :] < prefix_len)
        scores = jnp.where(allowed[None], scores, NEG)
        weights_p = low(jax.nn.softmax(scores, axis=-1))
        return jnp.einsum('hqk,khd->qhd', weights_p, value_heads, precision=HIGH)
    starts = jnp.arange(0, seq_rows, block_rows, dtype=jnp.int32)
    blocks = lax.map(jax.checkpoint(one_block), starts)
    return blocks.reshape(seq_rows, queries.shape[1], queries.shape[2])

def block_forward(source, target, weight_rows, prefix_len, attn_in, attn_out, mlp_in, mlp_out, norm_gains):
    seq_rows = source.shape[0]
    normed_one = source * rms_scale(source)
    first_in = low(normed_one * norm_gains[0])
    mixed = low_back(low(matmul(first_in, attn_in.T)))
    queries = mixed[:, :D].reshape(seq_rows, HEADS, HEAD_DIM)
    key_heads = mixed[:, D:2 * D].reshape(seq_rows, HEADS, HEAD_DIM)
    value_heads = mixed[:, 2 * D:].reshape(seq_rows, HEADS, HEAD_DIM)
    attended = attend(queries, key_heads, value_heads, prefix_len).reshape(seq_rows, D)
    attended = low_back(low(attended))
    middle = source + low_back(matmul(attended, attn_out))
    normed_two = middle * rms_scale(middle)
    second_in = low(normed_two * norm_gains[1])
    gate_up = low_back(matmul(second_in, mlp_in.T))
    hidden = low(jax.nn.silu(gate_up[:, :FF]) * gate_up[:, FF:])
    result = middle + low_back(matmul(hidden, mlp_out))
    error = weight_rows * (result - target)
    return (0.5 * jnp.sum(error * error), result)

def reference(inputs, teacher, valid_mask, prefix, attn_in, attn_out, mlp_in, mlp_out, norm_gains):
    weights = tuple((weight.astype(jnp.float32) for weight in (attn_in, attn_out, mlp_in, mlp_out, norm_gains)))
    seq_count = MB * PAIR
    sources = inputs.astype(jnp.float32).reshape(seq_count, SEQ_LEN, D)
    targets = teacher.astype(jnp.float32).reshape(seq_count, SEQ_LEN, D)
    rows_weight = valid_mask.astype(jnp.float32).reshape(seq_count, SEQ_LEN, 1)
    prefixes = prefix.reshape(seq_count).astype(jnp.int32)

    def one_sequence(totals, seq_items):
        source, target, weight_rows, prefix_len = seq_items

        def objective(source_in, first_w, second_w, third_w, fourth_w, gain_w):
            return block_forward(source_in, target, weight_rows, prefix_len, first_w, second_w, third_w, fourth_w, gain_w)
        half_error, pullback, result = jax.vjp(objective, source, *weights, has_aux=True)
        gradients = pullback(jnp.ones_like(half_error))
        totals = tuple((total + grad for total, grad in zip(totals, gradients[1:])))
        return (totals, (result.astype(jnp.bfloat16), gradients[0], 2.0 * half_error))
    start_sums = tuple((jnp.zeros_like(weight) for weight in weights))
    totals, (results, input_grads, error_sums) = lax.scan(one_sequence, start_sums, (sources, targets, rows_weight, prefixes))
    losses = lax.optimization_barrier(jnp.sum(error_sums.reshape(MB, PAIR), axis=1)) / (D * jnp.sum(rows_weight))
    return (results.reshape(MB, PAIR, SEQ_LEN, D), losses, input_grads.reshape(MB, PAIR, SEQ_LEN, D), totals[0], totals[1], totals[2], totals[3], totals[4])
```

```python
import functools

import jax
import jax.numpy as jnp
from jax import lax
from jax.experimental import pallas as pl
from jax.experimental.pallas import tpu as pltpu
from jax.sharding import PartitionSpec as P

HEADS = 16
HEAD_DIM = 64
PAIR_DIM = 2 * HEAD_DIM
EPS = 1e-05
NEG = -1e30
F32 = jnp.float32
BF16 = jnp.bfloat16
BOTH = ("dp", "seq")
BLOCK = 256


def rms_scale(rows):
    return lax.rsqrt(jnp.mean(rows * rows, axis=-1, keepdims=True) + EPS)


def nt(left, right):
    return lax.dot_general(left, right, (((1,), (1,)), ((), ())), preferred_element_type=F32)


def tn(left, right):
    return lax.dot_general(left, right, (((0,), (0,)), ((), ())), preferred_element_type=F32)


def nn(left, right):
    return jnp.dot(left, right, preferred_element_type=F32)


def norm_back(grad_norm, normed, scale_rows, gain):
    scaled = grad_norm * gain
    return scale_rows * (scaled - normed * jnp.mean(scaled * normed, axis=-1, keepdims=True))


def swap_seq(value, bits, n_seq):
    return lax.ppermute(value, "seq", [(i, i ^ bits) for i in range(n_seq)])


def swap_dp(value):
    return lax.ppermute(value, "dp", [(0, 1), (1, 0)])


def cube_gather(own, n_seq):
    half = own.shape[0] // 2
    by_x = swap_seq(own, 2, n_seq)
    by_dp = swap_dp(own)
    by_core = swap_seq(own, 1, n_seq)
    far = jnp.concatenate([swap_seq(by_dp[:half], 2, n_seq), swap_dp(by_x[half:])], 0)
    others = [swap_seq(v, 1, n_seq) for v in (by_x, by_dp, far)]
    return jnp.concatenate([own, by_x, by_dp, far, by_core] + others, 0)


def cube_reduce(parts, n_seq):
    rows = parts.shape[1]
    half = rows // 2
    got = swap_seq(parts[4:].astype(BF16), 1, n_seq).astype(F32)
    here, for_x, for_dp, for_far = (parts[i] + got[i] for i in range(4))
    far_low = for_far.astype(BF16)
    via_x = swap_seq(far_low[:half], 2, n_seq).astype(F32)
    via_dp = swap_dp(far_low[half:]).astype(F32)
    for_dp = jnp.concatenate([for_dp[:half] + via_x, for_dp[half:]], 0)
    for_x = jnp.concatenate([for_x[:half], for_x[half:] + via_dp], 0)
    from_x = swap_seq(for_x.astype(BF16), 2, n_seq).astype(F32)
    from_dp = swap_dp(for_dp.astype(BF16)).astype(F32)
    return here + from_x + from_dp


def micro_gather(rows, core, n_seq):
    keep = jnp.where(core == 0, rows[0], rows[1])
    send = jnp.where(core == 0, rows[1], rows[0])
    got = swap_seq(send, 1, n_seq)
    own = jnp.where(core == 0, jnp.concatenate([keep, got], 0), jnp.concatenate([got, keep], 0))
    lines = [own] + [swap_seq(own, 4 * j, n_seq) for j in range(1, n_seq // 4)]
    blocks = []
    for value in lines:
        blocks += [value, swap_seq(value, 2, n_seq)]
    return blocks


def matchings(edges, count):
    left = list(edges)
    rounds = []
    for _ in range(count):
        by_source = {}
        for edge in left:
            by_source.setdefault(edge[0], []).append(edge)
        taken = {}

        def place(source, seen):
            for edge in by_source[source]:
                if edge[1] in seen:
                    continue
                seen.add(edge[1])
                if edge[1] not in taken or place(taken[edge[1]][0], seen):
                    taken[edge[1]] = edge
                    return True
            return False

        for source in sorted(by_source):
            place(source, set())
        chosen = sorted(taken.values())
        rounds.append(chosen)
        for edge in chosen:
            left.remove(edge)
    return rounds


def spans(rows_q, rows_k):
    for start in range(0, rows_q, BLOCK):
        if rows_q == rows_k:
            yield start, max(start + BLOCK, rows_k // 2)
        else:
            yield start, rows_k


def attend_kernel(where_ref, *refs):
    n_blocks = len(refs) - 5
    x_refs = refs[:n_blocks]
    w_ref, gain_ref, first_ref, mixed_ref, att_ref = refs[n_blocks:]
    my_block, first_query, prefix_len = where_ref[0], where_ref[1], where_ref[2]
    rows = x_refs[0].shape[0]
    for j in range(n_blocks):
        at = pl.multiple_of((my_block ^ j) * rows, rows)
        source = x_refs[j][...].astype(F32)
        first = (source * rms_scale(source) * gain_ref[...]).astype(BF16)
        first_ref[pl.ds(at, rows), :] = first
        mixed_ref[pl.ds(at, rows), :] = nt(first, w_ref[...]).astype(BF16)
    rows_q, rows_k = att_ref.shape[0], mixed_ref.shape[0]
    lanes = lax.broadcasted_iota(jnp.int32, (BLOCK, PAIR_DIM), 1)
    for start, width in spans(rows_q, rows_k):
        at = pl.multiple_of(first_query + start, BLOCK)
        query = mixed_ref[pl.ds(at, BLOCK), 0:PAIR_DIM]
        keys = mixed_ref[0:width, PAIR_DIM : 2 * PAIR_DIM]
        values = mixed_ref[0:width, 2 * PAIR_DIM :]
        key_pos = lax.broadcasted_iota(jnp.int32, (BLOCK, width), 1)
        query_pos = at + lax.broadcasted_iota(jnp.int32, (BLOCK, width), 0)
        allowed = (key_pos <= query_pos) | (key_pos < prefix_len)
        outs = []
        for head in range(2):
            mine = (lanes // HEAD_DIM) == head
            scores = nt(jnp.where(mine, query, jnp.zeros_like(query)), keys) * HEAD_DIM**-0.5
            scores = jnp.where(allowed, scores, NEG)
            top = jnp.max(scores, axis=-1, keepdims=True)
            weights = jnp.exp(scores - top)
            total = jnp.sum(weights, axis=-1, keepdims=True)
            probs = (weights / total).astype(BF16)
            outs.append(nn(probs, values))
        att_ref[start : start + BLOCK, :] = jnp.where(lanes < HEAD_DIM, outs[0], outs[1]).astype(BF16)


def attend(where, blocks, weights, gain, rows_q):
    rows_k = blocks[0].shape[0] * len(blocks)
    width = blocks[0].shape[1]
    n_in = len(blocks) + 2
    return pl.pallas_call(
        attend_kernel,
        out_shape=(
            jax.ShapeDtypeStruct((rows_k, width), BF16),
            jax.ShapeDtypeStruct((rows_k, 3 * PAIR_DIM), BF16),
            jax.ShapeDtypeStruct((rows_q, PAIR_DIM), BF16),
        ),
        in_specs=[pl.BlockSpec(memory_space=pltpu.SMEM)] + [pl.BlockSpec(memory_space=pltpu.VMEM)] * n_in,
        out_specs=(pl.BlockSpec(memory_space=pltpu.VMEM),) * 3,
        compiler_params=pltpu.CompilerParams(vmem_limit_bytes=56 << 20),
        cost_estimate=pl.CostEstimate(
            flops=2 * rows_k * width * 3 * PAIR_DIM + 4 * rows_q * rows_k * PAIR_DIM,
            bytes_accessed=4 * rows_k * width,
            transcendentals=2 * rows_q * rows_k,
        ),
    )(where, *blocks, weights, gain)


def attend_back_kernel(where_ref, mixed_ref, grad_ref, gq_ref, gk_ref, gv_ref):
    first_query, prefix_len = where_ref[1], where_ref[2]
    rows_q, rows_k = grad_ref.shape[0], mixed_ref.shape[0]
    lanes = lax.broadcasted_iota(jnp.int32, (BLOCK, PAIR_DIM), 1)
    gk_ref[...] = jnp.zeros_like(gk_ref)
    gv_ref[...] = jnp.zeros_like(gv_ref)
    for start, width in spans(rows_q, rows_k):
        at = pl.multiple_of(first_query + start, BLOCK)
        query = mixed_ref[pl.ds(at, BLOCK), 0:PAIR_DIM]
        grad = grad_ref[start : start + BLOCK, :]
        keys = mixed_ref[0:width, PAIR_DIM : 2 * PAIR_DIM]
        values = mixed_ref[0:width, 2 * PAIR_DIM :]
        key_pos = lax.broadcasted_iota(jnp.int32, (width, BLOCK), 0)
        query_pos = at + lax.broadcasted_iota(jnp.int32, (width, BLOCK), 1)
        allowed = (key_pos <= query_pos) | (key_pos < prefix_len)
        outs = []
        for head in range(2):
            mine = (lanes // HEAD_DIM) == head
            own_query = jnp.where(mine, query, jnp.zeros_like(query))
            own_grad = jnp.where(mine, grad, jnp.zeros_like(grad))
            scores = nt(keys, own_query) * HEAD_DIM**-0.5
            scores = jnp.where(allowed, scores, NEG)
            top = jnp.max(scores, axis=0, keepdims=True)
            weights = jnp.exp(scores - top)
            probs = weights / jnp.sum(weights, axis=0, keepdims=True)
            grad_probs = nt(values, own_grad)
            delta = jnp.sum(probs * grad_probs, axis=0, keepdims=True)
            grad_scores = (probs * (grad_probs - delta)).astype(BF16)
            gv_ref[0:width, :] += nn(probs.astype(BF16), own_grad)
            gk_ref[0:width, :] += nn(grad_scores, own_query) * HEAD_DIM**-0.5
            outs.append(tn(grad_scores, keys) * HEAD_DIM**-0.5)
        gq_ref[start : start + BLOCK, :] = jnp.where(lanes < HEAD_DIM, outs[0], outs[1])


def attend_back(where, mixed, grad):
    rows_q, rows_k = grad.shape[0], mixed.shape[0]
    return pl.pallas_call(
        attend_back_kernel,
        out_shape=(
            jax.ShapeDtypeStruct((rows_q, PAIR_DIM), F32),
            jax.ShapeDtypeStruct((rows_k, PAIR_DIM), F32),
            jax.ShapeDtypeStruct((rows_k, PAIR_DIM), F32),
        ),
        in_specs=[pl.BlockSpec(memory_space=pltpu.SMEM)] + [pl.BlockSpec(memory_space=pltpu.VMEM)] * 2,
        out_specs=(pl.BlockSpec(memory_space=pltpu.VMEM),) * 3,
        compiler_params=pltpu.CompilerParams(vmem_limit_bytes=56 << 20),
        cost_estimate=pl.CostEstimate(
            flops=10 * rows_q * rows_k * PAIR_DIM,
            bytes_accessed=8 * rows_k * PAIR_DIM * 4,
            transcendentals=2 * rows_q * rows_k,
        ),
    )(where, mixed, grad)


def shards(n_dp, n_seq, inputs, teacher, valid_mask, prefix, attn_in, attn_out, mlp_in, mlp_out, norm_gains):
    n_micro, _, tok_rows, width = inputs.shape
    rows = n_micro * tok_rows
    dp = lax.axis_index("dp")
    seq = lax.axis_index("seq")
    me = dp * n_seq + seq
    core = seq % 2
    n_dev = n_dp * n_seq
    n_pairs = HEADS // 2
    group = n_micro * n_pairs
    n_parts = n_seq // group
    part = seq // group
    n_line = n_seq // 4
    seq_len = n_seq * tok_rows
    rows_q = seq_len // n_parts
    part_groups = [[p * group + g for p in range(n_parts)] for g in range(group)]
    in_groups = [[p * group + g for g in range(group)] for p in range(n_parts)] if n_parts > 1 else None
    gain_one = norm_gains[0:1]
    gain_two = norm_gains[1:2]

    x_blocks = micro_gather(inputs[:, 0], core, n_seq)

    unit = attn_in.shape[0] // 3
    n_share = PAIR_DIM // unit
    edges = []
    for block in range(3 * n_dev):
        third, rest = divmod(block, n_pairs * n_share)
        pair, share = divmod(rest, n_share)
        to_dp, rest = divmod(share, 2 * n_parts)
        to_part, to_core = divmod(rest, 2)
        to_seq = to_part * group + 2 * pair + to_core
        edges.append((block // 3, to_dp * n_seq + to_seq, block % 3, third))
    rounds = matchings(edges, 3)
    own_units = attn_in.reshape(3, unit, width)
    arrived = []
    for chosen in rounds:
        slot = jnp.array([edge[2] for edge in chosen], jnp.int32)[me]
        value = lax.dynamic_index_in_dim(own_units, slot, 0, keepdims=False)
        arrived.append(lax.ppermute(value, BOTH, [(edge[0], edge[1]) for edge in chosen]))
    thirds = []
    for chosen in rounds:
        order = sorted((edge[1], edge[3]) for edge in chosen)
        thirds.append(jnp.array([third for _, third in order], jnp.int32)[me])
    my_thirds = jnp.stack(
        [
            jnp.where(thirds[0] == third, arrived[0], jnp.where(thirds[1] == third, arrived[1], arrived[2]))
            for third in range(3)
        ]
    )
    got = swap_seq(my_thirds, 1, n_seq)
    both = jnp.where(core == 0, jnp.stack([my_thirds, got], 1), jnp.stack([got, my_thirds], 1))
    if n_parts > 1:
        both = lax.all_gather(both, "seq", axis=1, axis_index_groups=part_groups, tiled=True)
    got = swap_dp(both)
    pair_weights = jnp.where(dp == 0, jnp.stack([both, got], 1), jnp.stack([got, both], 1))
    pair_weights = pair_weights.reshape(3 * PAIR_DIM, width)

    attn_out_full = lax.all_gather(attn_out, BOTH, axis=0, tiled=True)
    attn_in_full = lax.all_gather(attn_in, BOTH, axis=0, tiled=True)

    ff_half = mlp_in.shape[0] // 2
    given = swap_dp(jnp.where(dp == 0, mlp_in[ff_half:], mlp_in[:ff_half]))
    gate_rows = jnp.where(dp == 0, mlp_in[:ff_half], given)
    up_rows = jnp.where(dp == 0, given, mlp_in[ff_half:])
    down_rows = lax.ppermute(mlp_out, BOTH, [(b, (b % 2) * n_seq + b // 2) for b in range(n_dev)])
    line_own = jnp.concatenate([gate_rows, up_rows, down_rows], 0)
    line = jnp.stack([line_own] + [swap_seq(line_own, 4 * j, n_seq) for j in range(1, n_line)])
    gate_w = line[:, :ff_half].reshape(n_line * ff_half, width)
    up_w = line[:, ff_half : 2 * ff_half].reshape(n_line * ff_half, width)
    down_w = line[:, 2 * ff_half :].reshape(n_line * ff_half, width)

    prefix_len = jnp.where(core == 0, prefix[0, 0], prefix[1, 0])
    where = jnp.stack([seq // 2, part * rows_q, prefix_len]).astype(jnp.int32)
    first_in, mixed, attended = attend(where, x_blocks, pair_weights, gain_one, rows_q)

    def to_rows(by_device, n_kinds):
        moved = lax.all_to_all(by_device, "seq", 0, 0, axis_index_groups=in_groups)
        moved = moved.reshape(n_pairs, n_micro, tok_rows, n_kinds, PAIR_DIM)
        return moved.transpose(1, 2, 3, 0, 4).reshape(rows, n_kinds * width)

    attended_low = to_rows(attended.reshape(group, tok_rows, PAIR_DIM), 1)

    source = inputs[:, 0].reshape(rows, width).astype(F32)
    target = teacher[:, 0].reshape(rows, width).astype(F32)
    row_mask = valid_mask[:, 0].reshape(rows, 1).astype(F32)
    middle = source + nn(attended_low, attn_out_full)
    scale_two = rms_scale(middle)
    normed_two = middle * scale_two
    second_in = cube_gather((normed_two * gain_two).astype(BF16), n_seq)

    gate = nt(second_in, gate_w)
    up_part = nt(second_in, up_w)
    sigmoid_gate = jax.nn.sigmoid(gate)
    silu_gate = gate * sigmoid_gate
    hidden = (silu_gate * up_part).astype(BF16)
    result = middle + cube_reduce(nn(hidden, down_w).reshape(8, rows, width), n_seq)
    output = result.astype(BF16).reshape(n_micro, 1, tok_rows, width)
    error = row_mask * (result - target)
    error_low = cube_gather(error.astype(BF16), n_seq)
    grad_hidden = nt(error_low, down_w)
    grad_gate = (grad_hidden * up_part * sigmoid_gate * (1.0 + gate * (1.0 - sigmoid_gate))).astype(BF16)
    grad_up = (grad_hidden * silu_gate).astype(BF16)
    grad_second = cube_reduce((nn(grad_gate, gate_w) + nn(grad_up, up_w)).reshape(8, rows, width), n_seq)

    terms = jnp.concatenate(
        [
            tn(grad_gate, second_in).astype(BF16).reshape(n_line, ff_half, width),
            tn(grad_up, second_in).astype(BF16).reshape(n_line, ff_half, width),
            tn(hidden, error_low).astype(BF16).reshape(n_line, ff_half, width),
        ],
        1,
    )
    line_sum = terms[0].astype(F32)
    for j in range(1, n_line):
        line_sum = line_sum + swap_seq(terms[j], 4 * j, n_seq).astype(F32)
    gate_sum, up_sum, down_sum = line_sum[:ff_half], line_sum[ff_half : 2 * ff_half], line_sum[2 * ff_half :]
    given = swap_dp(jnp.where(dp == 0, up_sum, gate_sum))
    mlp_in_grad = jnp.where(
        dp == 0, jnp.concatenate([gate_sum, given], 0), jnp.concatenate([given, up_sum], 0)
    )
    mlp_out_grad = lax.ppermute(down_sum, BOTH, [((b % 2) * n_seq + b // 2, b) for b in range(n_dev)])

    gain_two_term = jnp.sum(grad_second * normed_two, axis=0)
    grad_middle = error + norm_back(grad_second, normed_two, scale_two, gain_two)
    middle_low = grad_middle.astype(BF16)
    grad_att = nt(middle_low, attn_out_full).astype(BF16)
    grad_att = grad_att.reshape(n_micro, tok_rows, n_pairs, PAIR_DIM).transpose(2, 0, 1, 3)
    grad_att = lax.all_to_all(
        grad_att.reshape(group, tok_rows, PAIR_DIM), "seq", 0, 0, axis_index_groups=in_groups
    ).reshape(rows_q, PAIR_DIM)
    middle_blocks = micro_gather(middle_low.reshape(n_micro, tok_rows, width), core, n_seq)

    grad_q, grad_k, grad_v = attend_back(where, mixed, grad_att)
    first_part = first_in
    if n_parts > 1:
        grad_k, grad_v = (
            lax.psum_scatter(v, "seq", scatter_dimension=0, axis_index_groups=part_groups, tiled=True)
            for v in (grad_k, grad_v)
        )
        first_part = lax.dynamic_slice_in_dim(first_in, part * rows_q, rows_q, 0)
    grad_mixed = jnp.concatenate([grad_q, grad_k, grad_v], 1).astype(BF16)
    pair_grad = tn(grad_mixed, first_part)
    own_grad_mixed = to_rows(grad_mixed.reshape(group, tok_rows, 3 * PAIR_DIM), 3)

    gain_one_term = jnp.sum(pair_grad * pair_weights.astype(F32), axis=0) / gain_one[0]
    n_blocks = len(middle_blocks)
    stacked = jnp.stack(middle_blocks)
    order = (jnp.arange(n_blocks, dtype=jnp.int32) ^ (seq // 2)).astype(jnp.int32)
    middle_rows = stacked[order].reshape(seq_len, width)
    middle_part = middle_rows
    if n_parts > 1:
        middle_part = lax.dynamic_slice_in_dim(middle_rows, part * rows_q, rows_q, 0)
    out_grad = tn(attended, middle_part)
    all_grad = jnp.concatenate([pair_grad, out_grad], 0).reshape(4, n_dp, n_parts, 2, unit, width)
    keep = jnp.where(core == 0, all_grad[:, :, :, 0], all_grad[:, :, :, 1])
    give = jnp.where(core == 0, all_grad[:, :, :, 1], all_grad[:, :, :, 0])
    all_grad = keep + swap_seq(give, 1, n_seq)
    if n_parts > 1:
        all_grad = lax.psum_scatter(
            all_grad, "seq", scatter_dimension=2, axis_index_groups=part_groups, tiled=True
        )
    all_grad = all_grad[:, :, 0]
    keep = jnp.where(dp == 0, all_grad[:, 0], all_grad[:, 1])
    give = jnp.where(dp == 0, all_grad[:, 1], all_grad[:, 0])
    all_grad = keep + swap_dp(give)
    returned = []
    for chosen in rounds:
        order = sorted((edge[1], edge[3]) for edge in chosen)
        third = jnp.array([t for _, t in order], jnp.int32)[me]
        value = lax.dynamic_index_in_dim(all_grad[:3], third, 0, keepdims=False)
        returned.append(lax.ppermute(value, BOTH, [(edge[1], edge[0]) for edge in chosen]))
    slots = [jnp.array([edge[2] for edge in chosen], jnp.int32)[me] for chosen in rounds]
    attn_in_grad = jnp.stack(
        [
            jnp.where(slots[0] == slot, returned[0], jnp.where(slots[1] == slot, returned[1], returned[2]))
            for slot in range(3)
        ]
    ).reshape(3 * unit, width)
    moves = []
    for block in range(n_dev):
        pair, share = divmod(block, n_share)
        to_dp, rest = divmod(share, 2 * n_parts)
        to_part, to_core = divmod(rest, 2)
        moves.append((to_dp * n_seq + to_part * group + 2 * pair + to_core, block))
    attn_out_grad = lax.ppermute(all_grad[3], BOTH, moves)

    scale_one = rms_scale(source)
    normed_one = source * scale_one
    grad_first = nn(own_grad_mixed, attn_in_full)
    input_grad = grad_middle + norm_back(grad_first, normed_one, scale_one, gain_one)

    squares = jnp.sum((error * error).reshape(n_micro, tok_rows * width), axis=1)
    count = jnp.sum(row_mask)
    scalars = jnp.zeros((width,), F32).at[0:2].set(squares).at[2].set(count)
    sums = jnp.stack([gain_one_term, gain_two_term, scalars])
    bits = 1
    while bits < n_seq:
        sums = sums + swap_seq(sums, bits, n_seq)
        bits *= 2
    sums = sums + swap_dp(sums)
    losses = sums[2, 0:2] / (width * sums[2, 2])
    return (
        output,
        losses,
        input_grad.reshape(n_micro, 1, tok_rows, width),
        attn_in_grad,
        attn_out_grad,
        mlp_in_grad,
        mlp_out_grad,
        sums[0:2],
    )


def solution(mesh):
    n_dp, n_seq = mesh.shape["dp"], mesh.shape["seq"]
    placed = (
        P(None, "dp", "seq", None),
        P(None, "dp", "seq", None),
        P(None, "dp", "seq"),
        P(None, "dp"),
        P(BOTH, None),
        P(BOTH, None),
        P(BOTH, None),
        P(BOTH, None),
        P(),
    )
    return jax.shard_map(
        functools.partial(shards, n_dp, n_seq),
        mesh=mesh,
        in_specs=placed,
        out_specs=(
            P(None, "dp", "seq", None),
            P(),
            P(None, "dp", "seq", None),
            P(BOTH, None),
            P(BOTH, None),
            P(BOTH, None),
            P(BOTH, None),
            P(),
        ),
        check_vma=False,
    )
```

```python
import functools

import jax
import jax.numpy as jnp
from jax import lax
from jax.experimental import pallas as pl
from jax.experimental.pallas import tpu as pltpu
from jax.sharding import PartitionSpec as P

HEADS = 16
HEAD_DIM = 64
PAIR_DIM = 2 * HEAD_DIM
EPS = 1e-05
NEG = -1e30
F32 = jnp.float32
BF16 = jnp.bfloat16
BOTH = ("dp", "seq")
BLOCK = 256


def rms_scale(rows):
    return lax.rsqrt(jnp.mean(rows * rows, axis=-1, keepdims=True) + EPS)


def nt(left, right):
    return lax.dot_general(left, right, (((1,), (1,)), ((), ())), preferred_element_type=F32)


def tn(left, right):
    return lax.dot_general(left, right, (((0,), (0,)), ((), ())), preferred_element_type=F32)


def nn(left, right):
    return jnp.dot(left, right, preferred_element_type=F32)


def norm_back(grad_norm, normed, scale_rows, gain):
    scaled = grad_norm * gain
    return scale_rows * (scaled - normed * jnp.mean(scaled * normed, axis=-1, keepdims=True))


def swap_seq(value, bits, n_seq):
    return lax.ppermute(value, "seq", [(i, i ^ bits) for i in range(n_seq)])


def swap_dp(value):
    return lax.ppermute(value, "dp", [(0, 1), (1, 0)])


def cube_gather(own, n_seq):
    half = own.shape[0] // 2
    by_one = swap_seq(own, 2, n_seq)
    by_two = swap_seq(own, 4, n_seq)
    by_core = swap_seq(own, 1, n_seq)
    across = jnp.concatenate([swap_seq(by_two[:half], 2, n_seq), swap_seq(by_one[half:], 4, n_seq)], 0)
    others = [swap_seq(v, 1, n_seq) for v in (by_one, by_two, across)]
    return jnp.concatenate([own, by_one, by_two, across, by_core] + others, 0)


def cube_reduce(parts, n_seq):
    half = parts.shape[1] // 2
    got = swap_seq(parts[4:].astype(BF16), 1, n_seq).astype(F32)
    here, for_one, for_two, for_across = (parts[i] + got[i] for i in range(4))
    low = for_across.astype(BF16)
    via_one = swap_seq(low[:half], 2, n_seq).astype(F32)
    via_two = swap_seq(low[half:], 4, n_seq).astype(F32)
    for_two = jnp.concatenate([for_two[:half] + via_one, for_two[half:]], 0)
    for_one = jnp.concatenate([for_one[:half], for_one[half:] + via_two], 0)
    from_one = swap_seq(for_one.astype(BF16), 2, n_seq).astype(F32)
    from_two = swap_seq(for_two.astype(BF16), 4, n_seq).astype(F32)
    return here + from_one + from_two, got


def joint(*trees):
    leaves, shape = jax.tree.flatten(trees)
    return jax.tree.unflatten(shape, lax.optimization_barrier(tuple(leaves)))


def after(value, *others):
    return joint(value, *others)[0]


def micro_pair(rows, core, n_seq):
    keep = jnp.where(core == 0, rows[0], rows[1])
    send = jnp.where(core == 0, rows[1], rows[0])
    got = swap_seq(send, 1, n_seq)
    return jnp.where(core == 0, jnp.concatenate([keep, got], 0), jnp.concatenate([got, keep], 0))


def ones_of(number):
    return bin(number).count("1")


def spread(blocks, ones, unit_bits, count, n_seq):
    for j in range(1, count):
        if ones_of(j) == ones:
            blocks[j] = swap_seq(blocks[j & (j - 1)], unit_bits * (j & -j), n_seq)


def far_reduce(terms, gates, n_seq):
    bits = 8
    while terms.shape[0] > 1:
        pairs = terms.reshape((terms.shape[0] // 2, 2) + terms.shape[1:])
        got = swap_seq(pairs[:, 1].astype(BF16), bits, n_seq)
        terms = pairs[:, 0] + after(got, gates[0]).astype(F32)
        gates = gates[1:] or gates
        bits *= 2
    return terms[0]


def halve(terms, extra, mine, exchange):
    keep = jnp.where(mine == 0, terms[0], terms[1])
    give = jnp.where(mine == 0, terms[1], terms[0]).astype(BF16)
    high = extra.astype(BF16)
    low = (extra - high.astype(F32)).astype(BF16)
    rows = give.reshape(-1, give.shape[-1])
    got = exchange(jnp.concatenate([rows, high, low], 0)).astype(F32)
    n = extra.shape[0]
    keep = keep + got[: rows.shape[0]].reshape(keep.shape)
    return keep, (high.astype(F32) + low.astype(F32)) + (got[-2 * n : -n] + got[-n:])


def halve_seq(terms, extra, bits, n_seq):
    shape = terms.shape
    pairs = terms.reshape(shape[:-3] + (shape[-3] // 2, 2) + shape[-2:])
    mine = (lax.axis_index("seq") // bits) % 2
    return halve(jnp.moveaxis(pairs, -3, 0), extra, mine, lambda v: swap_seq(v, bits, n_seq))


def matchings(edges, count):
    left = list(edges)
    rounds = []
    for _ in range(count):
        by_source = {}
        for edge in left:
            by_source.setdefault(edge[0], []).append(edge)
        taken = {}

        def place(source, seen):
            for edge in by_source[source]:
                if edge[1] in seen:
                    continue
                seen.add(edge[1])
                if edge[1] not in taken or place(taken[edge[1]][0], seen):
                    taken[edge[1]] = edge
                    return True
            return False

        for source in sorted(by_source):
            place(source, set())
        chosen = sorted(taken.values())
        rounds.append(chosen)
        for edge in chosen:
            left.remove(edge)
    return rounds


def spans(rows_q, rows_k):
    for start in range(0, rows_q, BLOCK):
        if rows_q == rows_k:
            yield start, max(start + BLOCK, rows_k // 2)
        else:
            yield start, rows_k


def attend_kernel(where_ref, *refs):
    n_blocks = len(refs) - 5
    x_refs = refs[:n_blocks]
    w_ref, gain_ref, first_ref, mixed_ref, att_ref = refs[n_blocks:]
    my_block, first_query, prefix_len = where_ref[0], where_ref[1], where_ref[2]
    rows = x_refs[0].shape[0]
    for j in range(n_blocks):
        at = pl.multiple_of((my_block ^ j) * rows, rows)
        source = x_refs[j][...].astype(F32)
        first = (source * rms_scale(source) * gain_ref[...]).astype(BF16)
        first_ref[pl.ds(at, rows), :] = first
        mixed_ref[pl.ds(at, rows), :] = nt(first, w_ref[...]).astype(BF16)
    rows_q, rows_k = att_ref.shape[0], mixed_ref.shape[0]
    lanes = lax.broadcasted_iota(jnp.int32, (BLOCK, PAIR_DIM), 1)
    for start, width in spans(rows_q, rows_k):
        at = pl.multiple_of(first_query + start, BLOCK)
        query = mixed_ref[pl.ds(at, BLOCK), 0:PAIR_DIM]
        keys = mixed_ref[0:width, PAIR_DIM : 2 * PAIR_DIM]
        values = mixed_ref[0:width, 2 * PAIR_DIM :]
        key_pos = lax.broadcasted_iota(jnp.int32, (BLOCK, width), 1)
        query_pos = at + lax.broadcasted_iota(jnp.int32, (BLOCK, width), 0)
        allowed = (key_pos <= query_pos) | (key_pos < prefix_len)
        outs = []
        for head in range(2):
            mine = (lanes // HEAD_DIM) == head
            scores = nt(jnp.where(mine, query, jnp.zeros_like(query)), keys) * HEAD_DIM**-0.5
            scores = jnp.where(allowed, scores, NEG)
            top = jnp.max(scores, axis=-1, keepdims=True)
            weights = jnp.exp(scores - top)
            total = jnp.sum(weights, axis=-1, keepdims=True)
            probs = (weights / total).astype(BF16)
            outs.append(nn(probs, values))
        att_ref[start : start + BLOCK, :] = jnp.where(lanes < HEAD_DIM, outs[0], outs[1]).astype(BF16)


def attend(where, blocks, weights, gain, rows_q):
    rows_k = blocks[0].shape[0] * len(blocks)
    width = blocks[0].shape[1]
    n_in = len(blocks) + 2
    return pl.pallas_call(
        attend_kernel,
        out_shape=(
            jax.ShapeDtypeStruct((rows_k, width), BF16),
            jax.ShapeDtypeStruct((rows_k, 3 * PAIR_DIM), BF16),
            jax.ShapeDtypeStruct((rows_q, PAIR_DIM), BF16),
        ),
        in_specs=[pl.BlockSpec(memory_space=pltpu.SMEM)] + [pl.BlockSpec(memory_space=pltpu.VMEM)] * n_in,
        out_specs=(pl.BlockSpec(memory_space=pltpu.VMEM),) * 3,
        compiler_params=pltpu.CompilerParams(vmem_limit_bytes=56 << 20),
        cost_estimate=pl.CostEstimate(
            flops=2 * rows_k * width * 3 * PAIR_DIM + 4 * rows_q * rows_k * PAIR_DIM,
            bytes_accessed=4 * rows_k * width,
            transcendentals=2 * rows_q * rows_k,
        ),
    )(where, *blocks, weights, gain)


def attend_back_kernel(where_ref, mixed_ref, grad_ref, out_ref, gk_ref, gv_ref):
    first_query, prefix_len = where_ref[1], where_ref[2]
    rows_q, rows_k = grad_ref.shape[0], mixed_ref.shape[0]
    lanes = lax.broadcasted_iota(jnp.int32, (BLOCK, PAIR_DIM), 1)
    gk_ref[...] = jnp.zeros_like(gk_ref)
    gv_ref[...] = jnp.zeros_like(gv_ref)
    for start, width in spans(rows_q, rows_k):
        at = pl.multiple_of(first_query + start, BLOCK)
        query = mixed_ref[pl.ds(at, BLOCK), 0:PAIR_DIM]
        grad = grad_ref[start : start + BLOCK, :]
        keys = mixed_ref[0:width, PAIR_DIM : 2 * PAIR_DIM]
        values = mixed_ref[0:width, 2 * PAIR_DIM :]
        key_pos = lax.broadcasted_iota(jnp.int32, (width, BLOCK), 0)
        query_pos = at + lax.broadcasted_iota(jnp.int32, (width, BLOCK), 1)
        allowed = (key_pos <= query_pos) | (key_pos < prefix_len)
        outs = []
        for head in range(2):
            mine = (lanes // HEAD_DIM) == head
            own_query = jnp.where(mine, query, jnp.zeros_like(query))
            own_grad = jnp.where(mine, grad, jnp.zeros_like(grad))
            scores = nt(keys, own_query) * HEAD_DIM**-0.5
            scores = jnp.where(allowed, scores, NEG)
            top = jnp.max(scores, axis=0, keepdims=True)
            weights = jnp.exp(scores - top)
            probs = weights / jnp.sum(weights, axis=0, keepdims=True)
            grad_probs = nt(values, own_grad)
            delta = jnp.sum(probs * grad_probs, axis=0, keepdims=True)
            grad_scores = (probs * (grad_probs - delta)).astype(BF16)
            gv_ref[0:width, :] += nn(probs.astype(BF16), own_grad)
            gk_ref[0:width, :] += nn(grad_scores, own_query) * HEAD_DIM**-0.5
            outs.append(tn(grad_scores, keys) * HEAD_DIM**-0.5)
        grad_q = jnp.where(lanes < HEAD_DIM, outs[0], outs[1])
        out_ref[start : start + BLOCK, 0:PAIR_DIM] = grad_q.astype(BF16)
    if out_ref.shape[1] > PAIR_DIM:
        out_ref[:, PAIR_DIM : 2 * PAIR_DIM] = gk_ref[...].astype(BF16)
        out_ref[:, 2 * PAIR_DIM :] = gv_ref[...].astype(BF16)


def attend_back(where, mixed, grad):
    rows_q, rows_k = grad.shape[0], mixed.shape[0]
    whole = rows_q == rows_k
    keys = jax.ShapeDtypeStruct((rows_k, PAIR_DIM), F32)
    vmem = pl.BlockSpec(memory_space=pltpu.VMEM)
    return pl.pallas_call(
        attend_back_kernel,
        out_shape=(jax.ShapeDtypeStruct((rows_q, (3 if whole else 1) * PAIR_DIM), BF16),) + (() if whole else (keys, keys)),
        in_specs=[pl.BlockSpec(memory_space=pltpu.SMEM), vmem, vmem],
        out_specs=(vmem,) if whole else (vmem,) * 3,
        scratch_shapes=[pltpu.VMEM(keys.shape, F32)] * (2 if whole else 0),
        compiler_params=pltpu.CompilerParams(vmem_limit_bytes=56 << 20),
        cost_estimate=pl.CostEstimate(
            flops=10 * rows_q * rows_k * PAIR_DIM,
            bytes_accessed=8 * rows_k * PAIR_DIM * 4,
            transcendentals=2 * rows_q * rows_k,
        ),
    )(where, mixed, grad)


def project_kernel(moved_ref, w_ref, x_ref, gain_ref, att_ref, middle_ref, second_ref):
    n_micro = att_ref.shape[0] // moved_ref.shape[1]
    tok = moved_ref.shape[1]
    for i in range(moved_ref.shape[0]):
        pair, micro = divmod(i, n_micro)
        att_ref[micro * tok : (micro + 1) * tok, pair * PAIR_DIM : (pair + 1) * PAIR_DIM] = moved_ref[i]
    middle = x_ref[...].astype(F32) + nn(att_ref[...], w_ref[...])
    middle_ref[...] = middle
    second_ref[...] = (middle * rms_scale(middle) * gain_ref[...]).astype(BF16)


def project(moved, weights, rows_in, gain):
    rows, width = rows_in.shape
    vmem = pl.BlockSpec(memory_space=pltpu.VMEM)
    return pl.pallas_call(
        project_kernel,
        out_shape=(
            jax.ShapeDtypeStruct((rows, width), BF16),
            jax.ShapeDtypeStruct((rows, width), F32),
            jax.ShapeDtypeStruct((rows, width), BF16),
        ),
        in_specs=[vmem] * 4,
        out_specs=(vmem,) * 3,
        compiler_params=pltpu.CompilerParams(vmem_limit_bytes=32 << 20),
        cost_estimate=pl.CostEstimate(flops=2 * rows * width * width, bytes_accessed=4 * width * width, transcendentals=rows),
    )(moved, weights, rows_in, gain)


def input_grad_kernel(moved_ref, w_ref, x_ref, grad_ref, gain_ref, out_ref, mixed_ref):
    n_micro = out_ref.shape[0] // moved_ref.shape[1]
    tok = moved_ref.shape[1]
    width = x_ref.shape[1]
    for i in range(moved_ref.shape[0]):
        pair, micro = divmod(i, n_micro)
        for kind in range(3):
            at = kind * width + pair * PAIR_DIM
            mixed_ref[micro * tok : (micro + 1) * tok, at : at + PAIR_DIM] = moved_ref[
                i, :, kind * PAIR_DIM : (kind + 1) * PAIR_DIM
            ]
    source = x_ref[...].astype(F32)
    scale = rms_scale(source)
    grad_first = nn(mixed_ref[...], w_ref[...])
    out_ref[...] = grad_ref[...] + norm_back(grad_first, source * scale, scale, gain_ref[...])


def input_gradient(moved, weights, rows_in, grad_middle, gain):
    rows, width = rows_in.shape
    vmem = pl.BlockSpec(memory_space=pltpu.VMEM)
    return pl.pallas_call(
        input_grad_kernel,
        out_shape=jax.ShapeDtypeStruct((rows, width), F32),
        in_specs=[vmem] * 5,
        out_specs=vmem,
        scratch_shapes=[pltpu.VMEM((rows, 3 * width), BF16)],
        compiler_params=pltpu.CompilerParams(vmem_limit_bytes=32 << 20),
        cost_estimate=pl.CostEstimate(flops=200 * rows * width * width, bytes_accessed=8 * width * width, transcendentals=rows),
    )(moved, weights, rows_in, grad_middle, gain)


def shards(n_dp, n_seq, inputs, teacher, valid_mask, prefix, attn_in, attn_out, mlp_in, mlp_out, norm_gains):
    n_micro, _, tok_rows, width = inputs.shape
    rows = n_micro * tok_rows
    dp = lax.axis_index("dp")
    seq = lax.axis_index("seq")
    me = dp * n_seq + seq
    core = seq % 2
    n_dev = n_dp * n_seq
    n_pairs = HEADS // 2
    group = n_micro * n_pairs
    n_parts = n_seq // group
    part = seq // group
    n_far = n_seq // 8
    seq_len = n_seq * tok_rows
    rows_q = seq_len // n_parts
    part_groups = [[p * group + g for p in range(n_parts)] for g in range(group)]
    in_groups = [[p * group + g for g in range(group)] for p in range(n_parts)] if n_parts > 1 else None
    gain_one = norm_gains[0:1]
    gain_two = norm_gains[1:2]

    unit = attn_in.shape[0] // 3
    n_share = PAIR_DIM // unit
    edges = []
    for block in range(3 * n_dev):
        third, rest = divmod(block, n_pairs * n_share)
        pair, share = divmod(rest, n_share)
        to_dp, rest = divmod(share, 2 * n_parts)
        to_part, to_core = divmod(rest, 2)
        to_seq = to_part * group + 2 * pair + to_core
        edges.append((block // 3, to_dp * n_seq + to_seq, block % 3, third))
    rounds = matchings(edges, 3)
    own_units = attn_in.reshape(3, unit, width)
    arrived = []
    for chosen in rounds:
        slot = jnp.array([edge[2] for edge in chosen], jnp.int32)[me]
        value = lax.dynamic_index_in_dim(own_units, slot, 0, keepdims=False)
        arrived.append(lax.ppermute(value, BOTH, [(edge[0], edge[1]) for edge in chosen]))
    thirds = []
    for chosen in rounds:
        order = sorted((edge[1], edge[3]) for edge in chosen)
        thirds.append(jnp.array([third for _, third in order], jnp.int32)[me])

    attn_out_full = lax.all_gather(attn_out, BOTH, axis=0, tiled=True)
    attn_in_full = lax.all_gather(attn_in, BOTH, axis=0, tiled=True)

    down_rows = lax.ppermute(mlp_out, BOTH, [(b, (b % 2) * n_seq + b // 2) for b in range(n_dev)])

    n_line = n_seq // 4
    near = {0: micro_pair(inputs[:, 0], core, n_seq)}
    far = {}
    near, arrived, down_rows = joint(near, arrived, down_rows)
    spread(near, 1, 4, n_line, n_seq)
    far[0] = swap_seq(near[0], 2, n_seq)
    my_thirds = jnp.stack(
        [
            jnp.where(thirds[0] == third, arrived[0], jnp.where(thirds[1] == third, arrived[1], arrived[2]))
            for third in range(3)
        ]
    )
    got = swap_seq(my_thirds, 1, n_seq)
    both = jnp.where(core == 0, jnp.stack([my_thirds, got], 1), jnp.stack([got, my_thirds], 1))
    if n_parts > 1:
        both = lax.all_gather(both, "seq", axis=1, axis_index_groups=part_groups, tiled=True)
    near, far, both, ffn_own = joint(near, far, both, jnp.concatenate([mlp_in, down_rows], 0))
    ffn_here, ffn_there = {0: ffn_own}, {}
    ones = 2
    while True:
        before = [j for j in near if ones_of(j) == ones - 1]
        if not before:
            break
        spread(near, ones, 4, n_line, n_seq)
        for j in before:
            far[j] = swap_seq(near[j], 2, n_seq)
        if ones == 2:
            got = swap_dp(both)
            ffn_there[0] = swap_dp(ffn_own)
        near, far, got, ffn_here = joint(near, far, got, ffn_here)
        ones += 1
    spread(ffn_here, 1, 8, n_far, n_seq)
    pair_weights = jnp.where(dp == 0, jnp.stack([both, got], 1), jnp.stack([got, both], 1))
    pair_weights = pair_weights.reshape(3 * PAIR_DIM, width)
    x_blocks = [value for j in range(n_line) for value in (near[j], far[j])]

    prefix_len = jnp.where(core == 0, prefix[0, 0], prefix[1, 0])
    where = jnp.stack([seq // 2, part * rows_q, prefix_len]).astype(jnp.int32)
    first_in, mixed, attended = attend(where, x_blocks, pair_weights, gain_one, rows_q)

    def exchange(by_device):
        return lax.all_to_all(by_device, "seq", 0, 0, axis_index_groups=in_groups)

    own_in = inputs[:, 0].reshape(rows, width)
    target = teacher[:, 0].reshape(rows, width).astype(F32)
    row_mask = valid_mask[:, 0].reshape(rows, 1).astype(F32)
    attended_low, middle, second_own = project(
        exchange(attended.reshape(group, tok_rows, PAIR_DIM)), attn_out_full, own_in, gain_two
    )
    scale_two = rms_scale(middle)
    normed_two = middle * scale_two
    second_in = cube_gather(second_own, n_seq)

    ffn_here = after(ffn_here, second_own)
    for ones in range(1, n_far.bit_length()):
        if ones > 1:
            spread(ffn_here, ones, 8, n_far, n_seq)
        for j in range(1, n_far):
            if ones_of(j) == ones:
                ffn_there[j] = swap_dp(ffn_here[j])
    in_rows = mlp_in.shape[0]
    here_w, there_w = (
        jnp.concatenate([blocks[j][:in_rows] for j in range(n_far)], 0) for blocks in (ffn_here, ffn_there)
    )
    downs = [(ffn_here[j][in_rows:], ffn_there[j][in_rows:]) for j in range(n_far)]
    down_w = jnp.where(
        dp == 0,
        jnp.concatenate([block for here, there in downs for block in (here, there)], 0),
        jnp.concatenate([block for here, there in downs for block in (there, here)], 0),
    )

    by_here = nt(second_in, here_w)
    by_there = nt(second_in, there_w)
    gate = jnp.where(dp == 0, by_here, by_there)
    up_part = jnp.where(dp == 0, by_there, by_here)
    sigmoid_gate = jax.nn.sigmoid(gate)
    silu_gate = gate * sigmoid_gate
    hidden = (silu_gate * up_part).astype(BF16)
    result = middle + cube_reduce(nn(hidden, down_w).reshape(8, rows, width), n_seq)[0]
    output = result.astype(BF16).reshape(n_micro, 1, tok_rows, width)
    error = row_mask * (result - target)
    error_low = cube_gather(error.astype(BF16), n_seq)
    grad_hidden = nt(error_low, down_w)
    grad_gate = grad_hidden * up_part * sigmoid_gate * (1.0 + gate * (1.0 - sigmoid_gate))
    grad_up = grad_hidden * silu_gate
    grad_here = jnp.where(dp == 0, grad_gate, grad_up).astype(BF16)
    grad_there = jnp.where(dp == 0, grad_up, grad_gate).astype(BF16)
    grad_second, begun = cube_reduce(
        (nn(grad_here, here_w) + nn(grad_there, there_w)).reshape(8, rows, width), n_seq
    )

    hidden_late, grad_here, grad_there = after((hidden, grad_here, grad_there), begun)
    down_terms = tn(hidden_late, error_low).reshape(n_far, 2, mlp_out.shape[0], width)
    in_terms = tn(grad_here, second_in).reshape(n_far, in_rows, width)
    down_got = swap_dp(jnp.where(dp == 0, down_terms[:, 1], down_terms[:, 0]).astype(BF16))
    in_got = swap_dp(tn(grad_there, second_in).astype(BF16).reshape(n_far, in_rows, width))
    down_terms = jnp.where(dp == 0, down_terms[:, 0], down_terms[:, 1])

    grad_middle = error + norm_back(grad_second, normed_two, scale_two, gain_two)
    middle_low = grad_middle.astype(BF16)
    grad_att = nt(middle_low, attn_out_full).astype(BF16)
    grad_att = grad_att.reshape(n_micro, tok_rows, n_pairs, PAIR_DIM).transpose(2, 0, 1, 3)
    grad_att = exchange(grad_att.reshape(group, tok_rows, PAIR_DIM)).reshape(rows_q, PAIR_DIM)

    squares = jnp.sum((error * error).reshape(n_micro, tok_rows * width), axis=1)
    scalars = jnp.zeros((width,), F32).at[0:2].set(squares).at[2].set(jnp.sum(row_mask))
    extra = jnp.stack([jnp.sum(grad_second * normed_two, axis=0), scalars])
    out_terms = tn(attended_low, middle_low).reshape(n_dp, n_seq, width // n_dev, width)
    out_terms, extra = halve_seq(out_terms, extra, 1, n_seq)
    out_terms, extra = halve_seq(out_terms, extra, 2, n_seq)
    out_terms, extra = halve(out_terms, extra, dp, swap_dp)

    down_terms = down_terms + after(down_got, grad_second).astype(F32)
    down_sum = far_reduce(down_terms, [grad_att], n_seq)
    mlp_out_grad = lax.ppermute(
        down_sum.astype(BF16), BOTH, [((b % 2) * n_seq + b // 2, b) for b in range(n_dev)]
    )
    in_terms = in_terms + after(in_got, grad_att).astype(F32)

    grads = attend_back(where, mixed, grad_att)
    first_part = first_in
    grad_mixed = grads[0]
    if n_parts > 1:
        grad_k, grad_v = (
            lax.psum_scatter(v, "seq", scatter_dimension=0, axis_index_groups=part_groups, tiled=True).astype(BF16)
            for v in grads[1:]
        )
        grad_mixed = jnp.concatenate([grad_mixed, grad_k, grad_v], 1)
        first_part = lax.dynamic_slice_in_dim(first_in, part * rows_q, rows_q, 0)
    own_grad_mixed = exchange(grad_mixed.reshape(group, tok_rows, 3 * PAIR_DIM))
    mlp_in_grad = far_reduce(in_terms, [own_grad_mixed], n_seq)
    mlp_out_grad = after(mlp_out_grad, own_grad_mixed).astype(F32)

    pair_grad = tn(grad_mixed, first_part)
    gain_term = (jnp.sum(pair_grad * pair_weights.astype(F32), axis=0) / gain_one[0]).reshape(8, width // 8)
    pair_grad = pair_grad.reshape(3, n_dp, n_parts, 2, unit, width)
    keep = jnp.where(core == 0, pair_grad[:, :, :, 0], pair_grad[:, :, :, 1])
    give = jnp.where(core == 0, pair_grad[:, :, :, 1], pair_grad[:, :, :, 0])
    pair_grad = keep + swap_seq(give.astype(BF16), 1, n_seq).astype(F32)
    if n_parts > 1:
        pair_grad = lax.psum_scatter(
            pair_grad, "seq", scatter_dimension=2, axis_index_groups=part_groups, tiled=True
        )
    pair_grad = pair_grad[:, :, 0]
    keep = jnp.where(dp == 0, pair_grad[:, 0], pair_grad[:, 1])
    give = jnp.where(dp == 0, pair_grad[:, 1], pair_grad[:, 0])
    pair_grad = (keep + swap_dp(give.astype(BF16)).astype(F32)).astype(BF16)
    returned = []
    for chosen in rounds:
        order = sorted((edge[1], edge[3]) for edge in chosen)
        third = jnp.array([t for _, t in order], jnp.int32)[me]
        value = lax.dynamic_index_in_dim(pair_grad, third, 0, keepdims=False)
        returned.append(lax.ppermute(value, BOTH, [(edge[1], edge[0]) for edge in chosen]))
    slots = [jnp.array([edge[2] for edge in chosen], jnp.int32)[me] for chosen in rounds]
    attn_in_grad = jnp.concatenate(
        [
            jnp.where(slots[0] == slot, returned[0], jnp.where(slots[1] == slot, returned[1], returned[2]))
            for slot in range(3)
        ],
        0,
    ).astype(F32)

    gain_term = gain_term + swap_seq(gain_term, 1, n_seq)
    gain_term = gain_term + swap_seq(gain_term, 2, n_seq)
    gain_term = gain_term + swap_dp(gain_term)
    extra = jnp.concatenate([extra, gain_term.reshape(1, width)], 0)
    bits = 4
    while bits < n_seq:
        out_terms, extra = halve_seq(out_terms, extra, bits, n_seq)
        bits *= 2
    attn_out_grad = out_terms.reshape(attn_out.shape)
    losses = extra[1, 0:2] / (width * extra[1, 2])
    gain_grad = jnp.stack([extra[2], extra[0]])

    input_grad = input_gradient(own_grad_mixed, attn_in_full, own_in, grad_middle, gain_one)
    return (
        output,
        losses,
        input_grad.reshape(n_micro, 1, tok_rows, width),
        attn_in_grad,
        attn_out_grad,
        mlp_in_grad,
        mlp_out_grad,
        gain_grad,
    )


def solution(mesh):
    n_dp, n_seq = mesh.shape["dp"], mesh.shape["seq"]
    placed = (
        P(None, "dp", "seq", None),
        P(None, "dp", "seq", None),
        P(None, "dp", "seq"),
        P(None, "dp"),
        P(BOTH, None),
        P(BOTH, None),
        P(BOTH, None),
        P(BOTH, None),
        P(),
    )
    return jax.shard_map(
        functools.partial(shards, n_dp, n_seq),
        mesh=mesh,
        in_specs=placed,
        out_specs=(
            P(None, "dp", "seq", None),
            P(),
            P(None, "dp", "seq", None),
            P(BOTH, None),
            P(BOTH, None),
            P(BOTH, None),
            P(BOTH, None),
            P(),
        ),
        check_vma=False,
    )
```

```python
import functools

import jax
import jax.numpy as jnp
from jax import lax
from jax.experimental import pallas as pl
from jax.experimental.pallas import tpu as pltpu
from jax.sharding import PartitionSpec as P

HEADS = 16
HEAD_DIM = 64
PAIR_DIM = 2 * HEAD_DIM
EPS = 1e-05
NEG = -1e30
F32 = jnp.float32
BF16 = jnp.bfloat16
BOTH = ("dp", "seq")
BLOCK = 256
CUBE = (0, 2, 4, 6, 1, 3, 5, 7)


def rms_scale(rows):
    return lax.rsqrt(jnp.mean(rows * rows, axis=-1, keepdims=True) + EPS)


def nt(left, right):
    return lax.dot_general(left, right, (((1,), (1,)), ((), ())), preferred_element_type=F32)


def tn(left, right):
    return lax.dot_general(left, right, (((0,), (0,)), ((), ())), preferred_element_type=F32)


def nn(left, right):
    return jnp.dot(left, right, preferred_element_type=F32)


def norm_back(grad_norm, normed, scale_rows, gain):
    scaled = grad_norm * gain
    return scale_rows * (scaled - normed * jnp.mean(scaled * normed, axis=-1, keepdims=True))


def swap_seq(value, bits, n_seq):
    return lax.ppermute(value, "seq", [(i, i ^ bits) for i in range(n_seq)])


def swap_dp(value):
    return lax.ppermute(value, "dp", [(0, 1), (1, 0)])


def cube_gather(own, n_seq):
    half = own.shape[0] // 2
    by_one = swap_seq(own, 2, n_seq)
    by_two = swap_seq(own, 4, n_seq)
    by_core = swap_seq(own, 1, n_seq)
    across = jnp.concatenate([swap_seq(by_two[:half], 2, n_seq), swap_seq(by_one[half:], 4, n_seq)], 0)
    others = [swap_seq(v, 1, n_seq) for v in (by_one, by_two, across)]
    return [own, by_one, by_two, across, by_core] + others


def cube_rows(own, n_seq):
    return jnp.concatenate(cube_gather(own, n_seq), 0)


def cube_reduce(product, left, n_seq, hold=()):
    cut = left.shape[0] // 2
    got = swap_seq(product(left[cut:]).astype(BF16), 1, n_seq)
    got, hold = joint(got, hold)
    sums = product(left[:cut]) + got.astype(F32)
    here, for_one, for_two, for_across = sums.reshape(4, cut // 4, -1)
    half = cut // 8
    low = for_across.astype(BF16)
    via_one = swap_seq(low[:half], 2, n_seq).astype(F32)
    via_two = swap_seq(low[half:], 4, n_seq).astype(F32)
    for_two = jnp.concatenate([for_two[:half] + via_one, for_two[half:]], 0)
    for_one = jnp.concatenate([for_one[:half], for_one[half:] + via_two], 0)
    from_one = swap_seq(for_one.astype(BF16), 2, n_seq).astype(F32)
    from_two = swap_seq(for_two.astype(BF16), 4, n_seq).astype(F32)
    return here + from_one + from_two, (via_one, via_two), hold


def joint(*trees):
    leaves, shape = jax.tree.flatten(trees)
    return jax.tree.unflatten(shape, lax.optimization_barrier(tuple(leaves)))


def after(value, *others):
    return joint(value, *others)[0]


def ones_of(number):
    return bin(number).count("1")


def far_spread(own, n_seq):
    here = {0: own}
    for ones in range(1, (n_seq // 8).bit_length()):
        for j in range(1, n_seq // 8):
            if ones_of(j) == ones:
                here[j] = swap_seq(here[j & (j - 1)], 8 * (j & -j), n_seq)
    return [here[j] for j in range(n_seq // 8)]


def far_reduce(terms, gates, n_seq, bits=8):
    while terms.shape[0] > 1:
        pairs = terms.reshape((terms.shape[0] // 2, 2) + terms.shape[1:])
        got = swap_seq(pairs[:, 1].astype(BF16), bits, n_seq)
        terms = pairs[:, 0] + after(got, gates[0]).astype(F32)
        gates = gates[1:] or gates
        bits *= 2
    return terms[0]


def spans(rows_q, rows_k):
    if rows_q != rows_k:
        return [(0, rows_q, rows_k)]
    half = rows_k // 2
    return [(0, half, half)] + [(start, start + BLOCK, start + BLOCK) for start in range(half, rows_q, BLOCK)]


def place(micro, member, half, slot, tok):
    bits = (slot % 4) * 2 + slot // 4
    return pl.multiple_of(((micro ^ half) * 8 + (member ^ bits)) * tok, tok)


def attend_kernel(where_ref, *refs):
    x_refs = refs[:-8]
    w_ref, gain_ref, first_ref, mixed_ref, keep_ref, give_ref, att_ref, x_ref = refs[-8:]
    micro, member, first_query, prefix_len = where_ref[0], where_ref[1], where_ref[2], where_ref[3]
    rows_q, rows_k = att_ref.shape[0], mixed_ref.shape[0]
    tok = rows_q // 16
    for piece, ref in enumerate(x_refs):
        x_ref[2 * tok * piece : 2 * tok * (piece + 1), :] = ref[...]

    @pl.loop(0, rows_k // (4 * tok))
    def _(pair):
        rows = pl.ds(pl.multiple_of(4 * tok * pair, 4 * tok), 4 * tok)
        source = x_ref[rows, :].astype(F32)
        first = (source * rms_scale(source) * gain_ref[...]).astype(BF16)
        mixed = nt(first, w_ref[...]).astype(BF16)
        for piece in range(2):
            part, slot = (2 * pair + piece) // 8, (2 * pair + piece) % 8
            for half in range(2):
                at = part * rows_q + place(micro, member, half, slot, tok)
                here = slice((2 * piece + half) * tok, (2 * piece + half + 1) * tok)
                first_ref[pl.ds(at, tok), :] = first[here]
                mixed_ref[pl.ds(at, tok), :] = mixed[here]

    att_ref[...] = jnp.zeros_like(att_ref)
    lanes = lax.broadcasted_iota(jnp.int32, (BLOCK, PAIR_DIM), 1)
    for begin, end, width in spans(rows_q, rows_k):

        @pl.loop(0, 2 * (end - begin) // BLOCK)
        def _(step, begin=begin, width=width):
            start = pl.multiple_of(begin + (step // 2) * BLOCK, BLOCK)
            at = pl.multiple_of(first_query + start, BLOCK)
            mine = (lanes // HEAD_DIM) == step % 2
            query = mixed_ref[pl.ds(at, BLOCK), 0:PAIR_DIM]
            keys = mixed_ref[0:width, PAIR_DIM : 2 * PAIR_DIM]
            values = mixed_ref[0:width, 2 * PAIR_DIM :]
            key_pos = lax.broadcasted_iota(jnp.int32, (BLOCK, width), 1)
            query_pos = at + lax.broadcasted_iota(jnp.int32, (BLOCK, width), 0)
            allowed = (key_pos <= query_pos) | (key_pos < prefix_len)
            scores = nt(jnp.where(mine, query, jnp.zeros_like(query)), keys) * HEAD_DIM**-0.5
            scores = jnp.where(allowed, scores, NEG)
            top = jnp.max(scores, axis=-1, keepdims=True)
            weights = jnp.exp(scores - top)
            total = jnp.sum(weights, axis=-1, keepdims=True)
            probs = (weights / total).astype(BF16)
            before = att_ref[pl.ds(start, BLOCK), :]
            att_ref[pl.ds(start, BLOCK), :] = jnp.where(mine, nn(probs, values).astype(BF16), before)
    for slot in range(8):
        here = slice(slot * tok, (slot + 1) * tok)
        keep_ref[here, :] = att_ref[pl.ds(place(micro, member, 0, slot, tok), tok), :]
        give_ref[here, :] = att_ref[pl.ds(place(micro, member, 1, slot, tok), tok), :]


def attend(where, blocks, weights, gain, rows_q):
    rows_k, width = blocks[0].shape[0] * len(blocks), blocks[0].shape[1]
    vmem = pl.BlockSpec(memory_space=pltpu.VMEM)
    return pl.pallas_call(
        attend_kernel,
        out_shape=(
            jax.ShapeDtypeStruct((rows_k, width), BF16),
            jax.ShapeDtypeStruct((rows_k, 3 * PAIR_DIM), BF16),
            jax.ShapeDtypeStruct((rows_q // 2, PAIR_DIM), BF16),
            jax.ShapeDtypeStruct((rows_q // 2, PAIR_DIM), BF16),
        ),
        in_specs=[pl.BlockSpec(memory_space=pltpu.SMEM)] + [vmem] * (len(blocks) + 2),
        out_specs=(vmem,) * 4,
        scratch_shapes=[pltpu.VMEM((rows_q, PAIR_DIM), BF16), pltpu.VMEM((rows_k, width), BF16)],
        compiler_params=pltpu.CompilerParams(vmem_limit_bytes=56 << 20),
        cost_estimate=pl.CostEstimate(
            flops=2 * rows_k * width * 3 * PAIR_DIM + 4 * rows_q * rows_k * PAIR_DIM,
            bytes_accessed=4 * rows_k * width,
            transcendentals=2 * rows_q * rows_k,
        ),
    )(where, *blocks, weights, gain)


def attend_back_kernel(where_ref, mixed_ref, own_ref, got_ref, gq_ref, *refs):
    micro, member, first_query, prefix_len = where_ref[0], where_ref[1], where_ref[2], where_ref[3]
    grad_ref = refs[-1]
    whole = len(refs) == 5
    keep_ref, give_ref, gk_ref, gv_ref = refs[:4] if whole else (None, None) + refs[:2]
    rows_q, rows_k = grad_ref.shape[0], mixed_ref.shape[0]
    tok = rows_q // 16
    for slot in range(8):
        here = slice(slot * tok, (slot + 1) * tok)
        grad_ref[pl.ds(place(micro, member, 0, slot, tok), tok), :] = own_ref[here, :]
        grad_ref[pl.ds(place(micro, member, 1, slot, tok), tok), :] = got_ref[here, :]
    lanes = lax.broadcasted_iota(jnp.int32, (BLOCK, PAIR_DIM), 1)
    gq_ref[...] = jnp.zeros_like(gq_ref)
    gk_ref[...] = jnp.zeros_like(gk_ref)
    gv_ref[...] = jnp.zeros_like(gv_ref)
    for begin, end, width in spans(rows_q, rows_k):

        @pl.loop(0, 2 * (end - begin) // BLOCK)
        def _(step, begin=begin, width=width):
            start = pl.multiple_of(begin + (step // 2) * BLOCK, BLOCK)
            at = pl.multiple_of(first_query + start, BLOCK)
            mine = (lanes // HEAD_DIM) == step % 2
            query = mixed_ref[pl.ds(at, BLOCK), 0:PAIR_DIM]
            grad = grad_ref[pl.ds(start, BLOCK), :]
            keys = mixed_ref[0:width, PAIR_DIM : 2 * PAIR_DIM]
            values = mixed_ref[0:width, 2 * PAIR_DIM :]
            key_pos = lax.broadcasted_iota(jnp.int32, (width, BLOCK), 0)
            query_pos = at + lax.broadcasted_iota(jnp.int32, (width, BLOCK), 1)
            allowed = (key_pos <= query_pos) | (key_pos < prefix_len)
            own_query = jnp.where(mine, query, jnp.zeros_like(query))
            own_grad = jnp.where(mine, grad, jnp.zeros_like(grad))
            scores = nt(keys, own_query) * HEAD_DIM**-0.5
            scores = jnp.where(allowed, scores, NEG)
            top = jnp.max(scores, axis=0, keepdims=True)
            weights = jnp.exp(scores - top)
            probs = weights / jnp.sum(weights, axis=0, keepdims=True)
            grad_probs = nt(values, own_grad)
            delta = jnp.sum(probs * grad_probs, axis=0, keepdims=True)
            grad_scores = (probs * (grad_probs - delta)).astype(BF16)
            gv_ref[0:width, :] += nn(probs.astype(BF16), own_grad)
            gk_ref[0:width, :] += nn(grad_scores, own_query) * HEAD_DIM**-0.5
            grad_q = (tn(grad_scores, keys) * HEAD_DIM**-0.5).astype(BF16)
            before = gq_ref[pl.ds(start, BLOCK), 0:PAIR_DIM]
            gq_ref[pl.ds(start, BLOCK), 0:PAIR_DIM] = jnp.where(mine, grad_q, before)
    if whole:
        gq_ref[:, PAIR_DIM : 2 * PAIR_DIM] = gk_ref[...].astype(BF16)
        gq_ref[:, 2 * PAIR_DIM :] = gv_ref[...].astype(BF16)
        for slot in range(8):
            here = slice(slot * tok, (slot + 1) * tok)
            keep_ref[here, :] = gq_ref[pl.ds(place(micro, member, 0, slot, tok), tok), :]
            give_ref[here, :] = gq_ref[pl.ds(place(micro, member, 1, slot, tok), tok), :]


def attend_back(where, mixed, own, got):
    rows_q, rows_k = 2 * own.shape[0], mixed.shape[0]
    whole = rows_q == rows_k
    keys = jax.ShapeDtypeStruct((rows_k, PAIR_DIM), F32)
    half = jax.ShapeDtypeStruct((rows_q // 2, 3 * PAIR_DIM), BF16)
    vmem = pl.BlockSpec(memory_space=pltpu.VMEM)
    return pl.pallas_call(
        attend_back_kernel,
        out_shape=(jax.ShapeDtypeStruct((rows_q, (3 if whole else 1) * PAIR_DIM), BF16),)
        + ((half, half) if whole else (keys, keys)),
        in_specs=[pl.BlockSpec(memory_space=pltpu.SMEM)] + [vmem] * 3,
        out_specs=(vmem,) * 3,
        scratch_shapes=[pltpu.VMEM(keys.shape, F32)] * (2 if whole else 0) + [pltpu.VMEM((rows_q, PAIR_DIM), BF16)],
        compiler_params=pltpu.CompilerParams(vmem_limit_bytes=56 << 20),
        cost_estimate=pl.CostEstimate(
            flops=10 * rows_q * rows_k * PAIR_DIM,
            bytes_accessed=8 * rows_k * PAIR_DIM * 4,
            transcendentals=2 * rows_q * rows_k,
        ),
    )(where, mixed, own, got)


def shards(n_dp, n_seq, inputs, teacher, valid_mask, prefix, attn_in, attn_out, mlp_in, mlp_out, norm_gains):
    n_micro, _, tok, width = inputs.shape
    rows = n_micro * tok
    dp = lax.axis_index("dp")
    seq = lax.axis_index("seq")
    me = dp * n_seq + seq
    n_dev = n_dp * n_seq
    n_far = n_seq // 8
    member = seq % 8
    micro = (seq // 8) % 2
    part = seq // 16
    n_parts = n_seq // 16
    rows_q = 16 * tok
    part_groups = [[p * 16 + g for p in range(n_parts)] for g in range(16)]
    gain_one = norm_gains[0:1]
    gain_two = norm_gains[1:2]

    def micro_first(pair):
        return jnp.where(micro == 0, pair, pair[::-1])

    def other_micro(value):
        return swap_seq(value, 8, n_seq)

    own_in = micro_first(inputs[:, 0])

    unit = attn_in.shape[0] // 3
    n_share = PAIR_DIM // unit

    def home(share):
        pair, rest = divmod(share % n_dev, n_share)
        to_dp, to_far = divmod(rest, n_far)
        return to_dp * n_seq + to_far * 8 + pair

    my_share = member * n_share + dp * n_far + seq // 8
    third_inverse = pow(3, -1, n_dev)
    thirds = [(3 * (((my_share - t) * third_inverse) % n_dev) + t) // n_dev for t in range(3)]
    own_units = attn_in.reshape(3, unit, width)
    x_got = other_micro(own_in[1])
    down_rows = lax.ppermute(mlp_out, BOTH, [(b, (b % 2) * n_seq + b // 2) for b in range(n_dev)])
    arrived = [lax.ppermute(own_units[t], BOTH, [(i, home(3 * i + t)) for i in range(n_dev)]) for t in range(3)]
    x_pair = jnp.concatenate([own_in[0], x_got], 0)
    x_pair, arrived, late_in = joint(x_pair, arrived, mlp_in)
    ffn_here = far_spread(late_in, n_seq)
    ffn_there = [swap_dp(late_in)]

    x_blocks = cube_gather(x_pair, n_seq)
    if n_parts > 1:
        whole = lax.all_gather(jnp.stack(x_blocks), "seq", axis=0, axis_index_groups=part_groups, tiled=True)
        x_blocks = [whole[i] for i in range(8 * n_parts)]

    def pick(keys, values, key):
        return jnp.where(keys[0] == key, values[0], jnp.where(keys[1] == key, values[1], values[2]))

    arrived = after(arrived, x_blocks[4])
    my_thirds = jnp.stack([pick(thirds, arrived, third) for third in range(3)])
    here = far_spread(my_thirds, n_seq)
    there = [swap_dp(v) for v in here]

    def by_share(here, there, at):
        order = [jnp.stack([v[j] for j in range(n_far)], at) for v in (here, there)]
        if n_far > 1:
            turn = seq // 8
            for bit in range(n_far.bit_length() - 1):
                index = jnp.arange(n_far) ^ (1 << bit)
                on = (turn // (1 << bit)) % 2
                order = [jnp.where(on == 1, jnp.take(v, index, axis=at), v) for v in order]
        first = jnp.where(dp == 0, order[0], order[1])
        second = jnp.where(dp == 0, order[1], order[0])
        return jnp.stack([first, second], at)

    pair_w = by_share(here, there, 1).reshape(3 * PAIR_DIM, width)

    prefix_len = jnp.where(micro == 0, prefix[0, 0], prefix[1, 0])
    where = jnp.stack([micro, member, part * rows_q, prefix_len]).astype(jnp.int32)
    x_blocks, pair_w, ffn_here, ffn_there, down_rows, late_out = joint(
        x_blocks, pair_w, ffn_here, ffn_there, down_rows, attn_out
    )
    down_here = far_spread(down_rows, n_seq)
    down_there = [swap_dp(down_rows)]
    out_rows = lax.ppermute(late_out, BOTH, [(i, home(i)) for i in range(n_dev)])
    first_in, mixed, att_keep, att_give = attend(where, x_blocks, pair_w, gain_one, rows_q)
    att_give, out_rows = joint(att_give, out_rows)
    out_here = far_spread(out_rows, n_seq)
    out_w = by_share(out_here, [swap_dp(v) for v in out_here], 0).reshape(PAIR_DIM, width)
    att_got = other_micro(att_give)

    ffn_there += [swap_dp(v) for v in after(ffn_here[1:], att_got)]
    down_there += [swap_dp(v) for v in after(down_here[1:], att_got)]
    in_rows = mlp_in.shape[0]

    def by_dp(here, there):
        return jnp.where(dp == 0, jnp.concatenate([here, there], 0), jnp.concatenate([there, here], 0))

    in_w = by_dp(*(jnp.concatenate(blocks, 0) for blocks in (ffn_here, ffn_there)))
    down_w = jnp.concatenate([by_dp(here, there) for here, there in zip(down_here, down_there)], 0)
    n_hidden = n_far * in_rows

    attended = jnp.stack([att_keep.reshape(8, tok, PAIR_DIM), att_got.reshape(8, tok, PAIR_DIM)], 1)
    attended = attended.reshape(8 * rows, PAIR_DIM)
    source = own_in.reshape(rows, width).astype(F32)
    middle = source + cube_reduce(lambda v: nn(v, out_w), attended, n_seq)[0]
    scale_two = rms_scale(middle)
    normed_two = middle * scale_two
    second_in = cube_rows((normed_two * gain_two).astype(BF16), n_seq)

    gate_up = nt(second_in, in_w)
    gate = gate_up[:, :n_hidden]
    up_part = gate_up[:, n_hidden:]
    sigmoid_gate = jax.nn.sigmoid(gate)
    silu_gate = gate * sigmoid_gate
    hidden = (silu_gate * up_part).astype(BF16)
    result = middle + cube_reduce(lambda v: nn(v, down_w), hidden, n_seq)[0]
    late_teacher, late_mask = after((teacher, valid_mask), att_got)
    target = micro_first(late_teacher[:, 0]).reshape(rows, width).astype(F32)
    row_mask = micro_first(late_mask[:, 0]).reshape(rows, 1).astype(F32)
    error = row_mask * (result - target)
    error_low = cube_rows(error.astype(BF16), n_seq)
    grad_hidden = nt(error_low, down_w)
    grad_gate = (grad_hidden * up_part * sigmoid_gate * (1.0 + gate * (1.0 - sigmoid_gate))).astype(BF16)
    grad_up = (grad_hidden * silu_gate).astype(BF16)
    grad_both = jnp.concatenate([grad_gate, grad_up], 1)
    grad_second, begun, _ = cube_reduce(lambda v: nn(v, in_w), grad_both, n_seq)

    hidden_late, both_late = after((hidden, grad_both), begun)
    down_terms = tn(hidden_late, error_low).reshape(n_far, 2, mlp_out.shape[0], width)
    in_terms = tn(both_late, second_in).reshape(n_dp, n_far, in_rows, width)
    down_got = swap_dp(jnp.where(dp == 0, down_terms[:, 1], down_terms[:, 0]).astype(BF16))
    in_got = swap_dp(jnp.where(dp == 0, in_terms[1], in_terms[0]).astype(BF16))
    down_terms = jnp.where(dp == 0, down_terms[:, 0], down_terms[:, 1])
    in_terms = jnp.where(dp == 0, in_terms[0], in_terms[1])

    grad_middle = error + norm_back(grad_second, normed_two, scale_two, gain_two)
    middle_low = cube_rows(grad_middle.astype(BF16), n_seq)
    grad_att = nt(middle_low, out_w).astype(BF16).reshape(8, 2, tok, PAIR_DIM)
    grad_keep = grad_att[:, 0].reshape(8 * tok, PAIR_DIM)
    grad_got = other_micro(grad_att[:, 1].reshape(8 * tok, PAIR_DIM))

    in_terms = in_terms + after(in_got, grad_got).astype(F32)
    in_pairs = in_terms.reshape((n_far // 2, 2) + in_terms.shape[1:])
    in_low = swap_seq(in_pairs[:, 1].astype(BF16), 8, n_seq)
    grads = attend_back(where, mixed, grad_keep, grad_got)
    if n_parts > 1:
        grad_k, grad_v = (
            lax.psum_scatter(v, "seq", scatter_dimension=0, axis_index_groups=part_groups, tiled=True).astype(BF16)
            for v in grads[1:]
        )
        grad_mixed = jnp.concatenate([grads[0], grad_k, grad_v], 1)
        first_part = lax.dynamic_slice_in_dim(first_in, part * rows_q, rows_q, 0)
        places = (member ^ jnp.array(CUBE, jnp.int32)) + 8 * micro
        by_rows = grad_mixed.reshape(16, tok, 3 * PAIR_DIM)
        mixed_keep, mixed_give = (by_rows[p].reshape(8 * tok, 3 * PAIR_DIM) for p in (places, places ^ 8))
    else:
        grad_mixed, mixed_keep, mixed_give = grads
        first_part = first_in
    mixed_give, mixed_keep, grad_mixed, in_low, first_part = joint(
        mixed_give, mixed_keep, grad_mixed, in_low, first_part
    )
    mixed_got = other_micro(mixed_give)

    mixed_rows = jnp.stack([v.reshape(8, tok, 3 * PAIR_DIM) for v in (mixed_keep, mixed_got)], 1)
    grad_first, last, _ = cube_reduce(
        lambda v: nn(v, pair_w), mixed_rows.reshape(8 * rows, 3 * PAIR_DIM), n_seq
    )
    mlp_in_grad = far_reduce(in_pairs[:, 0] + in_low.astype(F32), [grad_first], n_seq, 16)
    down_terms = down_terms + after(down_got, mixed_got).astype(F32)
    down_sum = far_reduce(down_terms, [last], n_seq)
    mlp_out_grad = lax.ppermute(
        down_sum.astype(BF16), BOTH, [((b % 2) * n_seq + b // 2, b) for b in range(n_dev)]
    )

    scale_one = rms_scale(source)
    input_grad = grad_middle + norm_back(grad_first, source * scale_one, scale_one, gain_one)
    mlp_out_grad = after(mlp_out_grad, grad_first).astype(F32)

    def share_reduce(terms, gates):
        give = jnp.where(dp == 0, terms[:, 1], terms[:, 0]).astype(BF16)
        terms = jnp.where(dp == 0, terms[:, 0], terms[:, 1]) + after(swap_dp(give), gates[0]).astype(F32)
        bits = 8
        while bits < n_seq:
            on = (seq // bits) % 2
            pairs = terms.reshape((terms.shape[0], terms.shape[1] // 2, 2) + terms.shape[2:])
            give = jnp.where(on == 0, pairs[:, :, 1], pairs[:, :, 0]).astype(BF16)
            got = after(swap_seq(give, bits, n_seq), gates[1])
            terms = jnp.where(on == 0, pairs[:, :, 0], pairs[:, :, 1]) + got.astype(F32)
            bits *= 2
        return terms[:, 0].astype(BF16)

    pair_terms = tn(grad_mixed, first_part)
    gain_term = jnp.sum(pair_terms * pair_w.astype(F32), axis=0) / gain_one[0]
    terms = jnp.concatenate([pair_terms, tn(attended, middle_low)], 0).reshape(4, n_dp, n_far, unit, width)
    terms = share_reduce(terms, [mixed_got, grad_first])
    attn_out_grad = lax.ppermute(terms[3], BOTH, [(home(i), i) for i in range(n_dev)]).astype(F32)
    returned = [
        lax.ppermute(
            jnp.where(thirds[t] == 0, terms[0], jnp.where(thirds[t] == 1, terms[1], terms[2])),
            BOTH,
            [(home(3 * i + t), i) for i in range(n_dev)],
        )
        for t in range(3)
    ]
    attn_in_grad = jnp.concatenate(returned, 0).astype(F32)

    squares = micro_first(jnp.sum((error * error).reshape(n_micro, tok * width), axis=1))
    scalars = jnp.zeros((width,), F32).at[0:2].set(squares).at[2].set(jnp.sum(row_mask))
    sums = jnp.stack([gain_term, jnp.sum(grad_second * normed_two, axis=0), scalars])
    sums = sums + swap_seq(sums, 1, n_seq)
    sums = sums + swap_dp(sums)
    bits = 2
    while bits < n_seq:
        sums = sums + after(swap_seq(sums, bits, n_seq), mixed_keep if bits < 8 else last)
        bits *= 2
    losses = sums[2, 0:2] / (width * sums[2, 2])

    def by_micro(value):
        return micro_first(value.reshape(n_micro, 1, tok, width))

    return (
        by_micro(result.astype(BF16)),
        losses,
        by_micro(input_grad),
        attn_in_grad,
        attn_out_grad,
        mlp_in_grad,
        mlp_out_grad,
        sums[0:2],
    )


def solution(mesh):
    n_dp, n_seq = mesh.shape["dp"], mesh.shape["seq"]
    placed = (
        P(None, "dp", "seq", None),
        P(None, "dp", "seq", None),
        P(None, "dp", "seq"),
        P(None, "dp"),
        P(BOTH, None),
        P(BOTH, None),
        P(BOTH, None),
        P(BOTH, None),
        P(),
    )
    return jax.shard_map(
        functools.partial(shards, n_dp, n_seq),
        mesh=mesh,
        in_specs=placed,
        out_specs=(
            P(None, "dp", "seq", None),
            P(),
            P(None, "dp", "seq", None),
            P(BOTH, None),
            P(BOTH, None),
            P(BOTH, None),
            P(BOTH, None),
            P(),
        ),
        check_vma=False,
    )
```

```python
import functools

import jax
import jax.numpy as jnp
from jax import lax
from jax.experimental import pallas as pl
from jax.experimental.pallas import tpu as pltpu
from jax.sharding import PartitionSpec as P

HEADS = 16
HEAD_DIM = 64
PAIR_DIM = 2 * HEAD_DIM
EPS = 1e-05
NEG = -1e30
F32 = jnp.float32
BF16 = jnp.bfloat16
BOTH = ("dp", "seq")
BLOCK = 256
CUBE = (0, 2, 4, 6, 1, 3, 5, 7)


def rms_scale(rows):
    return lax.rsqrt(jnp.mean(rows * rows, axis=-1, keepdims=True) + EPS)


def nt(left, right):
    return lax.dot_general(left, right, (((1,), (1,)), ((), ())), preferred_element_type=F32)


def tn(left, right):
    return lax.dot_general(left, right, (((0,), (0,)), ((), ())), preferred_element_type=F32)


def nn(left, right):
    return jnp.dot(left, right, preferred_element_type=F32)


def norm_back(grad_norm, normed, scale_rows, gain):
    scaled = grad_norm * gain
    return scale_rows * (scaled - normed * jnp.mean(scaled * normed, axis=-1, keepdims=True))


def swap_seq(value, bits, n_seq):
    return lax.ppermute(value, "seq", [(i, i ^ bits) for i in range(n_seq)])


def swap_dp(value):
    return lax.ppermute(value, "dp", [(0, 1), (1, 0)])


def cube_gather(own, n_seq):
    half = own.shape[0] // 2
    by_one = swap_seq(own, 2, n_seq)
    by_two = swap_seq(own, 4, n_seq)
    by_core = swap_seq(own, 1, n_seq)
    across = jnp.concatenate([swap_seq(by_two[:half], 2, n_seq), swap_seq(by_one[half:], 4, n_seq)], 0)
    others = [swap_seq(v, 1, n_seq) for v in (by_one, by_two, across)]
    return [own, by_one, by_two, across, by_core] + others


def cube_rows(own, n_seq):
    return jnp.concatenate(cube_gather(own, n_seq), 0)


def cube_reduce(product, left, n_seq, hold=()):
    cut = left.shape[0] // 2
    got = swap_seq(product(left[cut:]).astype(BF16), 1, n_seq)
    got, hold = joint(got, hold)
    sums = product(left[:cut]) + got.astype(F32)
    here, for_one, for_two, for_across = sums.reshape(4, cut // 4, -1)
    half = cut // 8
    low = for_across.astype(BF16)
    via_one = swap_seq(low[:half], 2, n_seq).astype(F32)
    via_two = swap_seq(low[half:], 4, n_seq).astype(F32)
    for_two = jnp.concatenate([for_two[:half] + via_one, for_two[half:]], 0)
    for_one = jnp.concatenate([for_one[:half], for_one[half:] + via_two], 0)
    from_one = swap_seq(for_one.astype(BF16), 2, n_seq).astype(F32)
    from_two = swap_seq(for_two.astype(BF16), 4, n_seq).astype(F32)
    return here + from_one + from_two, (via_one, via_two), hold


def joint(*trees):
    leaves, shape = jax.tree.flatten(trees)
    return jax.tree.unflatten(shape, lax.optimization_barrier(tuple(leaves)))


def after(value, *others):
    return joint(value, *others)[0]


def ones_of(number):
    return bin(number).count("1")


def far_spread(own, n_seq):
    here = {0: own}
    for ones in range(1, (n_seq // 8).bit_length()):
        for j in range(1, n_seq // 8):
            if ones_of(j) == ones:
                here[j] = swap_seq(here[j & (j - 1)], 8 * (j & -j), n_seq)
    return [here[j] for j in range(n_seq // 8)]


def far_reduce(terms, gates, n_seq, bits=8):
    while terms.shape[0] > 1:
        pairs = terms.reshape((terms.shape[0] // 2, 2) + terms.shape[1:])
        got = swap_seq(pairs[:, 1].astype(BF16), bits, n_seq)
        terms = pairs[:, 0] + after(got, gates[0]).astype(F32)
        gates = gates[1:] or gates
        bits *= 2
    return terms[0]


def spans(rows_q, rows_k):
    if rows_q != rows_k:
        return [(0, rows_q, rows_k)]
    half = rows_k // 2
    return [(0, half, half)] + [(start, start + BLOCK, start + BLOCK) for start in range(half, rows_q, BLOCK)]


def place(micro, member, half, slot, tok):
    bits = (slot % 4) * 2 + slot // 4
    return pl.multiple_of(((micro ^ half) * 8 + (member ^ bits)) * tok, tok)


def attend_kernel(where_ref, *refs):
    x_refs = refs[:-8]
    w_ref, gain_ref, first_ref, mixed_ref, keep_ref, give_ref, att_ref, x_ref = refs[-8:]
    micro, member, first_query, prefix_len = where_ref[0], where_ref[1], where_ref[2], where_ref[3]
    rows_q, rows_k = att_ref.shape[0], mixed_ref.shape[0]
    tok = rows_q // 16
    for piece, ref in enumerate(x_refs):
        x_ref[2 * tok * piece : 2 * tok * (piece + 1), :] = ref[...]

    @pl.loop(0, rows_k // (4 * tok))
    def _(pair):
        rows = pl.ds(pl.multiple_of(4 * tok * pair, 4 * tok), 4 * tok)
        source = x_ref[rows, :].astype(F32)
        first = (source * rms_scale(source) * gain_ref[...]).astype(BF16)
        mixed = nt(first, w_ref[...]).astype(BF16)
        for piece in range(2):
            part, slot = (2 * pair + piece) // 8, (2 * pair + piece) % 8
            for half in range(2):
                at = part * rows_q + place(micro, member, half, slot, tok)
                here = slice((2 * piece + half) * tok, (2 * piece + half + 1) * tok)
                first_ref[pl.ds(at, tok), :] = first[here]
                mixed_ref[pl.ds(at, tok), :] = mixed[here]

    att_ref[...] = jnp.zeros_like(att_ref)
    lanes = lax.broadcasted_iota(jnp.int32, (BLOCK, PAIR_DIM), 1)
    for begin, end, width in spans(rows_q, rows_k):

        @pl.loop(0, 2 * (end - begin) // BLOCK)
        def _(step, begin=begin, width=width):
            start = pl.multiple_of(begin + (step // 2) * BLOCK, BLOCK)
            at = pl.multiple_of(first_query + start, BLOCK)
            mine = (lanes // HEAD_DIM) == step % 2
            query = mixed_ref[pl.ds(at, BLOCK), 0:PAIR_DIM]
            keys = mixed_ref[0:width, PAIR_DIM : 2 * PAIR_DIM]
            values = mixed_ref[0:width, 2 * PAIR_DIM :]
            key_pos = lax.broadcasted_iota(jnp.int32, (BLOCK, width), 1)
            query_pos = at + lax.broadcasted_iota(jnp.int32, (BLOCK, width), 0)
            allowed = (key_pos <= query_pos) | (key_pos < prefix_len)
            scores = nt(jnp.where(mine, query, jnp.zeros_like(query)), keys) * HEAD_DIM**-0.5
            scores = jnp.where(allowed, scores, NEG)
            top = jnp.max(scores, axis=-1, keepdims=True)
            weights = jnp.exp(scores - top)
            total = jnp.sum(weights, axis=-1, keepdims=True)
            probs = (weights / total).astype(BF16)
            before = att_ref[pl.ds(start, BLOCK), :]
            att_ref[pl.ds(start, BLOCK), :] = jnp.where(mine, nn(probs, values).astype(BF16), before)
    for slot in range(8):
        here = slice(slot * tok, (slot + 1) * tok)
        keep_ref[here, :] = att_ref[pl.ds(place(micro, member, 0, slot, tok), tok), :]
        give_ref[here, :] = att_ref[pl.ds(place(micro, member, 1, slot, tok), tok), :]


def attend(where, blocks, weights, gain, rows_q):
    rows_k, width = blocks[0].shape[0] * len(blocks), blocks[0].shape[1]
    vmem = pl.BlockSpec(memory_space=pltpu.VMEM)
    return pl.pallas_call(
        attend_kernel,
        out_shape=(
            jax.ShapeDtypeStruct((rows_k, width), BF16),
            jax.ShapeDtypeStruct((rows_k, 3 * PAIR_DIM), BF16),
            jax.ShapeDtypeStruct((rows_q // 2, PAIR_DIM), BF16),
            jax.ShapeDtypeStruct((rows_q // 2, PAIR_DIM), BF16),
        ),
        in_specs=[pl.BlockSpec(memory_space=pltpu.SMEM)] + [vmem] * (len(blocks) + 2),
        out_specs=(vmem,) * 4,
        scratch_shapes=[pltpu.VMEM((rows_q, PAIR_DIM), BF16), pltpu.VMEM((rows_k, width), BF16)],
        compiler_params=pltpu.CompilerParams(vmem_limit_bytes=56 << 20),
        cost_estimate=pl.CostEstimate(
            flops=2 * rows_k * width * 3 * PAIR_DIM + 4 * rows_q * rows_k * PAIR_DIM,
            bytes_accessed=4 * rows_k * width,
            transcendentals=2 * rows_q * rows_k,
        ),
    )(where, *blocks, weights, gain)


def attend_back_kernel(where_ref, mixed_ref, own_ref, got_ref, gq_ref, *refs):
    micro, member, first_query, prefix_len = where_ref[0], where_ref[1], where_ref[2], where_ref[3]
    grad_ref = refs[-1]
    whole = len(refs) == 5
    keep_ref, give_ref, gk_ref, gv_ref = refs[:4] if whole else (None, None) + refs[:2]
    rows_q, rows_k = grad_ref.shape[0], mixed_ref.shape[0]
    tok = rows_q // 16
    for slot in range(8):
        here = slice(slot * tok, (slot + 1) * tok)
        grad_ref[pl.ds(place(micro, member, 0, slot, tok), tok), :] = own_ref[here, :]
        grad_ref[pl.ds(place(micro, member, 1, slot, tok), tok), :] = got_ref[here, :]
    lanes = lax.broadcasted_iota(jnp.int32, (BLOCK, PAIR_DIM), 1)
    gq_ref[...] = jnp.zeros_like(gq_ref)
    gk_ref[...] = jnp.zeros_like(gk_ref)
    gv_ref[...] = jnp.zeros_like(gv_ref)
    for begin, end, width in spans(rows_q, rows_k):

        @pl.loop(0, 2 * (end - begin) // BLOCK)
        def _(step, begin=begin, width=width):
            start = pl.multiple_of(begin + (step // 2) * BLOCK, BLOCK)
            at = pl.multiple_of(first_query + start, BLOCK)
            mine = (lanes // HEAD_DIM) == step % 2
            query = mixed_ref[pl.ds(at, BLOCK), 0:PAIR_DIM]
            grad = grad_ref[pl.ds(start, BLOCK), :]
            keys = mixed_ref[0:width, PAIR_DIM : 2 * PAIR_DIM]
            values = mixed_ref[0:width, 2 * PAIR_DIM :]
            key_pos = lax.broadcasted_iota(jnp.int32, (width, BLOCK), 0)
            query_pos = at + lax.broadcasted_iota(jnp.int32, (width, BLOCK), 1)
            allowed = (key_pos <= query_pos) | (key_pos < prefix_len)
            own_query = jnp.where(mine, query, jnp.zeros_like(query))
            own_grad = jnp.where(mine, grad, jnp.zeros_like(grad))
            scores = nt(keys, own_query) * HEAD_DIM**-0.5
            scores = jnp.where(allowed, scores, NEG)
            top = jnp.max(scores, axis=0, keepdims=True)
            weights = jnp.exp(scores - top)
            probs = weights / jnp.sum(weights, axis=0, keepdims=True)
            grad_probs = nt(values, own_grad)
            delta = jnp.sum(probs * grad_probs, axis=0, keepdims=True)
            grad_scores = (probs * (grad_probs - delta)).astype(BF16)
            gv_ref[0:width, :] += nn(probs.astype(BF16), own_grad)
            gk_ref[0:width, :] += nn(grad_scores, own_query) * HEAD_DIM**-0.5
            grad_q = (tn(grad_scores, keys) * HEAD_DIM**-0.5).astype(BF16)
            before = gq_ref[pl.ds(start, BLOCK), 0:PAIR_DIM]
            gq_ref[pl.ds(start, BLOCK), 0:PAIR_DIM] = jnp.where(mine, grad_q, before)
    if whole:
        gq_ref[:, PAIR_DIM : 2 * PAIR_DIM] = gk_ref[...].astype(BF16)
        gq_ref[:, 2 * PAIR_DIM :] = gv_ref[...].astype(BF16)
        for slot in range(8):
            here = slice(slot * tok, (slot + 1) * tok)
            keep_ref[here, :] = gq_ref[pl.ds(place(micro, member, 0, slot, tok), tok), :]
            give_ref[here, :] = gq_ref[pl.ds(place(micro, member, 1, slot, tok), tok), :]


def attend_back(where, mixed, own, got):
    rows_q, rows_k = 2 * own.shape[0], mixed.shape[0]
    whole = rows_q == rows_k
    keys = jax.ShapeDtypeStruct((rows_k, PAIR_DIM), F32)
    half = jax.ShapeDtypeStruct((rows_q // 2, 3 * PAIR_DIM), BF16)
    vmem = pl.BlockSpec(memory_space=pltpu.VMEM)
    return pl.pallas_call(
        attend_back_kernel,
        out_shape=(jax.ShapeDtypeStruct((rows_q, (3 if whole else 1) * PAIR_DIM), BF16),)
        + ((half, half) if whole else (keys, keys)),
        in_specs=[pl.BlockSpec(memory_space=pltpu.SMEM)] + [vmem] * 3,
        out_specs=(vmem,) * 3,
        scratch_shapes=[pltpu.VMEM(keys.shape, F32)] * (2 if whole else 0) + [pltpu.VMEM((rows_q, PAIR_DIM), BF16)],
        compiler_params=pltpu.CompilerParams(vmem_limit_bytes=56 << 20),
        cost_estimate=pl.CostEstimate(
            flops=10 * rows_q * rows_k * PAIR_DIM,
            bytes_accessed=8 * rows_k * PAIR_DIM * 4,
            transcendentals=2 * rows_q * rows_k,
        ),
    )(where, mixed, own, got)


def shards(n_dp, n_seq, inputs, teacher, valid_mask, prefix, attn_in, attn_out, mlp_in, mlp_out, norm_gains):
    n_micro, _, tok, width = inputs.shape
    rows = n_micro * tok
    dp = lax.axis_index("dp")
    seq = lax.axis_index("seq")
    me = dp * n_seq + seq
    n_dev = n_dp * n_seq
    n_far = n_seq // 8
    member = seq % 8
    micro = (seq // 8) % 2
    part = seq // 16
    n_parts = n_seq // 16
    rows_q = 16 * tok
    part_groups = [[p * 16 + g for p in range(n_parts)] for g in range(16)]
    gain_one = norm_gains[0:1]
    gain_two = norm_gains[1:2]

    def micro_first(pair):
        return jnp.where(micro == 0, pair, pair[::-1])

    def other_micro(value):
        return swap_seq(value, 8, n_seq)

    own_in = micro_first(inputs[:, 0])

    unit = attn_in.shape[0] // 3
    n_share = PAIR_DIM // unit

    def home(share):
        pair, rest = divmod(share % n_dev, n_share)
        to_dp, to_far = divmod(rest, n_far)
        return to_dp * n_seq + to_far * 8 + pair

    my_share = member * n_share + dp * n_far + seq // 8
    third_inverse = pow(3, -1, n_dev)
    thirds = [(3 * (((my_share - t) * third_inverse) % n_dev) + t) // n_dev for t in range(3)]
    own_units = attn_in.reshape(3, unit, width)
    x_got = other_micro(own_in[1])
    down_rows = lax.ppermute(mlp_out, BOTH, [(b, (b % 2) * n_seq + b // 2) for b in range(n_dev)])
    arrived = [lax.ppermute(own_units[t], BOTH, [(i, home(3 * i + t)) for i in range(n_dev)]) for t in range(3)]
    arrived.append(lax.ppermute(attn_out, BOTH, [(i, home(i)) for i in range(n_dev)]))
    x_pair = jnp.concatenate([own_in[0], x_got], 0)
    x_pair, arrived = joint(x_pair, arrived)

    x_blocks = cube_gather(x_pair, n_seq)
    if n_parts > 1:
        whole = lax.all_gather(jnp.stack(x_blocks), "seq", axis=0, axis_index_groups=part_groups, tiled=True)
        x_blocks = [whole[i] for i in range(8 * n_parts)]

    def pick(keys, values, key):
        return jnp.where(keys[0] == key, values[0], jnp.where(keys[1] == key, values[1], values[2]))

    arrived = after(arrived, x_blocks[4])
    my_blocks = jnp.stack([pick(thirds, arrived, third) for third in range(3)] + [arrived[3]])
    here = far_spread(my_blocks, n_seq)
    there = [swap_dp(v) for v in here]

    def by_share(here, there, at):
        order = [jnp.stack([v[j] for j in range(n_far)], at) for v in (here, there)]
        if n_far > 1:
            turn = seq // 8
            for bit in range(n_far.bit_length() - 1):
                index = jnp.arange(n_far) ^ (1 << bit)
                on = (turn // (1 << bit)) % 2
                order = [jnp.where(on == 1, jnp.take(v, index, axis=at), v) for v in order]
        first = jnp.where(dp == 0, order[0], order[1])
        second = jnp.where(dp == 0, order[1], order[0])
        return jnp.stack([first, second], at)

    head_w = by_share(here, there, 1).reshape(4 * PAIR_DIM, width)
    pair_w, out_w = head_w[: 3 * PAIR_DIM], head_w[3 * PAIR_DIM :]

    prefix_len = jnp.where(micro == 0, prefix[0, 0], prefix[1, 0])
    where = jnp.stack([micro, member, part * rows_q, prefix_len]).astype(jnp.int32)
    x_blocks, pair_w, out_w, late_in = joint(x_blocks, pair_w, out_w, mlp_in)
    ffn_here = far_spread(late_in, n_seq)
    ffn_there = [swap_dp(late_in)]
    first_in, mixed, att_keep, att_give = attend(where, x_blocks, pair_w, gain_one, rows_q)
    att_give, att_keep, ffn_here, ffn_there, down_rows = joint(att_give, att_keep, ffn_here, ffn_there, down_rows)
    down_here = far_spread(down_rows, n_seq)
    down_there = [swap_dp(down_rows)]
    att_got = other_micro(att_give)

    ffn_there += [swap_dp(v) for v in after(ffn_here[1:], att_got)]
    down_there += [swap_dp(v) for v in after(down_here[1:], att_got)]
    in_rows = mlp_in.shape[0]

    def by_dp(here, there):
        return jnp.where(dp == 0, jnp.concatenate([here, there], 0), jnp.concatenate([there, here], 0))

    in_w = by_dp(*(jnp.concatenate(blocks, 0) for blocks in (ffn_here, ffn_there)))
    down_w = jnp.concatenate([by_dp(here, there) for here, there in zip(down_here, down_there)], 0)
    n_hidden = n_far * in_rows

    attended = jnp.stack([att_keep.reshape(8, tok, PAIR_DIM), att_got.reshape(8, tok, PAIR_DIM)], 1)
    attended = attended.reshape(8 * rows, PAIR_DIM)
    source = own_in.reshape(rows, width).astype(F32)
    middle = source + cube_reduce(lambda v: nn(v, out_w), attended, n_seq)[0]
    scale_two = rms_scale(middle)
    normed_two = middle * scale_two
    second_in = cube_rows((normed_two * gain_two).astype(BF16), n_seq)

    gate_up = nt(second_in, in_w)
    gate = gate_up[:, :n_hidden]
    up_part = gate_up[:, n_hidden:]
    sigmoid_gate = jax.nn.sigmoid(gate)
    silu_gate = gate * sigmoid_gate
    hidden = (silu_gate * up_part).astype(BF16)
    result = middle + cube_reduce(lambda v: nn(v, down_w), hidden, n_seq)[0]
    late_teacher, late_mask = after((teacher, valid_mask), att_got)
    target = micro_first(late_teacher[:, 0]).reshape(rows, width).astype(F32)
    row_mask = micro_first(late_mask[:, 0]).reshape(rows, 1).astype(F32)
    error = row_mask * (result - target)
    error_low = cube_rows(error.astype(BF16), n_seq)
    grad_hidden = nt(error_low, down_w)
    grad_gate = (grad_hidden * up_part * sigmoid_gate * (1.0 + gate * (1.0 - sigmoid_gate))).astype(BF16)
    grad_up = (grad_hidden * silu_gate).astype(BF16)
    grad_both = jnp.concatenate([grad_gate, grad_up], 1)
    grad_second, begun, _ = cube_reduce(lambda v: nn(v, in_w), grad_both, n_seq)

    hidden_late, both_late = after((hidden, grad_both), begun)
    down_terms = tn(hidden_late, error_low).reshape(n_far, 2, mlp_out.shape[0], width)
    in_terms = tn(both_late, second_in).reshape(n_dp, n_far, in_rows, width)
    down_got = swap_dp(jnp.where(dp == 0, down_terms[:, 1], down_terms[:, 0]).astype(BF16))
    in_got = swap_dp(jnp.where(dp == 0, in_terms[1], in_terms[0]).astype(BF16))
    down_terms = jnp.where(dp == 0, down_terms[:, 0], down_terms[:, 1])
    in_terms = jnp.where(dp == 0, in_terms[0], in_terms[1])

    grad_middle = error + norm_back(grad_second, normed_two, scale_two, gain_two)
    middle_low = cube_rows(grad_middle.astype(BF16), n_seq)
    grad_att = nt(middle_low, out_w).astype(BF16).reshape(8, 2, tok, PAIR_DIM)
    grad_keep = grad_att[:, 0].reshape(8 * tok, PAIR_DIM)
    grad_got = other_micro(grad_att[:, 1].reshape(8 * tok, PAIR_DIM))

    in_terms = in_terms + after(in_got, grad_got).astype(F32)
    in_pairs = in_terms.reshape((n_far // 2, 2) + in_terms.shape[1:])
    half_rows = in_rows // 2
    in_low = swap_seq(in_pairs[:, 1, :half_rows].astype(BF16), 8, n_seq)
    grads = attend_back(where, mixed, grad_keep, grad_got)
    if n_parts > 1:
        grad_k, grad_v = (
            lax.psum_scatter(v, "seq", scatter_dimension=0, axis_index_groups=part_groups, tiled=True).astype(BF16)
            for v in grads[1:]
        )
        grad_mixed = jnp.concatenate([grads[0], grad_k, grad_v], 1)
        first_part = lax.dynamic_slice_in_dim(first_in, part * rows_q, rows_q, 0)
        places = (member ^ jnp.array(CUBE, jnp.int32)) + 8 * micro
        by_rows = grad_mixed.reshape(16, tok, 3 * PAIR_DIM)
        mixed_keep, mixed_give = (by_rows[p].reshape(8 * tok, 3 * PAIR_DIM) for p in (places, places ^ 8))
    else:
        grad_mixed, mixed_keep, mixed_give = grads
        first_part = first_in
    mixed_give, mixed_keep, grad_mixed, in_low, first_part = joint(
        mixed_give, mixed_keep, grad_mixed, in_low, first_part
    )
    mixed_got = other_micro(mixed_give)

    pair_terms = tn(grad_mixed, first_part)
    gain_term = jnp.sum(pair_terms * pair_w.astype(F32), axis=0) / gain_one[0]
    terms = jnp.concatenate([pair_terms, tn(attended, middle_low)], 0).reshape(4, n_dp, n_far, unit, width)
    terms_got = swap_dp(jnp.where(dp == 0, terms[:, 1], terms[:, 0]).astype(BF16))
    mixed_got, terms_got = joint(mixed_got, terms_got)
    terms = jnp.where(dp == 0, terms[:, 0], terms[:, 1]) + terms_got.astype(F32)

    mixed_rows = jnp.stack([v.reshape(8, tok, 3 * PAIR_DIM) for v in (mixed_keep, mixed_got)], 1)
    in_rest = swap_seq(after(in_pairs, mixed_got)[:, 1, half_rows:].astype(BF16), 8, n_seq)
    grad_first, last, in_rest = cube_reduce(
        lambda v: nn(v, pair_w), mixed_rows.reshape(8 * rows, 3 * PAIR_DIM), n_seq, in_rest
    )
    in_low = after(jnp.concatenate([in_low, in_rest], 1), grad_first)
    mlp_in_grad = far_reduce(in_pairs[:, 0] + in_low.astype(F32), [grad_first], n_seq, 16)
    down_terms = down_terms + after(down_got, mixed_got).astype(F32)
    down_sum = far_reduce(down_terms, [last], n_seq)
    mlp_out_grad = lax.ppermute(
        down_sum.astype(BF16), BOTH, [((b % 2) * n_seq + b // 2, b) for b in range(n_dev)]
    )

    scale_one = rms_scale(source)
    input_grad = grad_middle + norm_back(grad_first, source * scale_one, scale_one, gain_one)
    mlp_out_grad = after(mlp_out_grad, grad_first).astype(F32)

    bits = 8
    while bits < n_seq:
        on = (seq // bits) % 2
        pairs = terms.reshape((terms.shape[0], terms.shape[1] // 2, 2) + terms.shape[2:])
        give = jnp.where(on == 0, pairs[:, :, 1], pairs[:, :, 0]).astype(BF16)
        got = after(swap_seq(give, bits, n_seq), grad_first)
        terms = jnp.where(on == 0, pairs[:, :, 0], pairs[:, :, 1]) + got.astype(F32)
        bits *= 2
    terms = terms[:, 0].astype(BF16)
    attn_out_grad = lax.ppermute(terms[3], BOTH, [(home(i), i) for i in range(n_dev)]).astype(F32)
    returned = [
        lax.ppermute(
            jnp.where(thirds[t] == 0, terms[0], jnp.where(thirds[t] == 1, terms[1], terms[2])),
            BOTH,
            [(home(3 * i + t), i) for i in range(n_dev)],
        )
        for t in range(3)
    ]
    attn_in_grad = jnp.concatenate(returned, 0).astype(F32)

    squares = micro_first(jnp.sum((error * error).reshape(n_micro, tok * width), axis=1))
    scalars = jnp.zeros((width,), F32).at[0:2].set(squares).at[2].set(jnp.sum(row_mask))
    sums = jnp.stack([gain_term, jnp.sum(grad_second * normed_two, axis=0), scalars])
    sums = sums + swap_seq(sums, 1, n_seq)
    sums = sums + swap_dp(sums)
    bits = 2
    while bits < n_seq:
        sums = sums + after(swap_seq(sums, bits, n_seq), mixed_keep if bits < 8 else last)
        bits *= 2
    losses = sums[2, 0:2] / (width * sums[2, 2])

    def by_micro(value):
        return micro_first(value.reshape(n_micro, 1, tok, width))

    return (
        by_micro(result.astype(BF16)),
        losses,
        by_micro(input_grad),
        attn_in_grad,
        attn_out_grad,
        mlp_in_grad,
        mlp_out_grad,
        sums[0:2],
    )


def solution(mesh):
    n_dp, n_seq = mesh.shape["dp"], mesh.shape["seq"]
    placed = (
        P(None, "dp", "seq", None),
        P(None, "dp", "seq", None),
        P(None, "dp", "seq"),
        P(None, "dp"),
        P(BOTH, None),
        P(BOTH, None),
        P(BOTH, None),
        P(BOTH, None),
        P(),
    )
    return jax.shard_map(
        functools.partial(shards, n_dp, n_seq),
        mesh=mesh,
        in_specs=placed,
        out_specs=(
            P(None, "dp", "seq", None),
            P(),
            P(None, "dp", "seq", None),
            P(BOTH, None),
            P(BOTH, None),
            P(BOTH, None),
            P(BOTH, None),
            P(),
        ),
        check_vma=False,
    )
```

```python
import functools

import jax
import jax.numpy as jnp
from jax import lax
from jax.experimental import pallas as pl
from jax.experimental.pallas import tpu as pltpu
from jax.sharding import PartitionSpec as P

HEADS = 16
HEAD_DIM = 64
PAIR_DIM = 2 * HEAD_DIM
SCALE = HEAD_DIM**-0.5
EPS = 1e-05
NEG = -1e30
F32 = jnp.float32
BF16 = jnp.bfloat16
BOTH = ("dp", "seq")
BLOCK = 256
CUBE = (0, 2, 4, 6, 1, 3, 5, 7)


def rms_scale(rows):
    return lax.rsqrt(jnp.mean(rows * rows, axis=-1, keepdims=True) + EPS)


def nt(left, right):
    return lax.dot_general(left, right, (((1,), (1,)), ((), ())), preferred_element_type=F32)


def tn(left, right):
    return lax.dot_general(left, right, (((0,), (0,)), ((), ())), preferred_element_type=F32)


def nn(left, right):
    return jnp.dot(left, right, preferred_element_type=F32)


def norm_back(grad_norm, normed, scale_rows, gain):
    scaled = grad_norm * gain
    return scale_rows * (scaled - normed * jnp.mean(scaled * normed, axis=-1, keepdims=True))


def swap_seq(value, bits, n_seq):
    return lax.ppermute(value, "seq", [(i, i ^ bits) for i in range(n_seq)])


def swap_dp(value):
    return lax.ppermute(value, "dp", [(0, 1), (1, 0)])


def cube_gather(own, n_seq):
    half = own.shape[0] // 2
    by_one = swap_seq(own, 2, n_seq)
    by_two = swap_seq(own, 4, n_seq)
    by_core = swap_seq(own, 1, n_seq)
    across = jnp.concatenate([swap_seq(by_two[:half], 2, n_seq), swap_seq(by_one[half:], 4, n_seq)], 0)
    others = [swap_seq(v, 1, n_seq) for v in (by_one, by_two, across)]
    return [own, by_one, by_two, across, by_core] + others


def cube_rows(own, n_seq):
    return jnp.concatenate(cube_gather(own, n_seq), 0)


def cube_reduce(product, left, n_seq, hold=()):
    cut = left.shape[0] // 2
    got = swap_seq(product(left[cut:]).astype(BF16), 1, n_seq)
    got, hold = joint(got, hold)
    sums = product(left[:cut]) + got.astype(F32)
    here, for_one, for_two, for_across = sums.reshape(4, cut // 4, -1)
    half = cut // 8
    low = for_across.astype(BF16)
    via_one = swap_seq(low[:half], 2, n_seq).astype(F32)
    via_two = swap_seq(low[half:], 4, n_seq).astype(F32)
    for_two = jnp.concatenate([for_two[:half] + via_one, for_two[half:]], 0)
    for_one = jnp.concatenate([for_one[:half], for_one[half:] + via_two], 0)
    from_one = swap_seq(for_one.astype(BF16), 2, n_seq).astype(F32)
    from_two = swap_seq(for_two.astype(BF16), 4, n_seq).astype(F32)
    return here + from_one + from_two, (via_one, via_two), hold


def joint(*trees):
    leaves, shape = jax.tree.flatten(trees)
    return jax.tree.unflatten(shape, lax.optimization_barrier(tuple(leaves)))


def after(value, *others):
    return joint(value, *others)[0]


def ones_of(number):
    return bin(number).count("1")


def far_spread(own, n_seq):
    here = {0: own}
    for ones in range(1, (n_seq // 8).bit_length()):
        for j in range(1, n_seq // 8):
            if ones_of(j) == ones:
                here[j] = swap_seq(here[j & (j - 1)], 8 * (j & -j), n_seq)
    return [here[j] for j in range(n_seq // 8)]


def far_reduce(terms, gates, n_seq, bits=8):
    while terms.shape[0] > 1:
        pairs = terms.reshape((terms.shape[0] // 2, 2) + terms.shape[1:])
        got = swap_seq(pairs[:, 1].astype(BF16), bits, n_seq)
        terms = pairs[:, 0] + after(got, gates[0]).astype(F32)
        gates = gates[1:] or gates
        bits *= 2
    return terms[0]


def spans(rows_q, rows_k):
    if rows_q != rows_k:
        return [(0, rows_q, rows_k)]
    half = rows_k // 2
    return [(0, half, half)] + [(start, start + BLOCK, start + BLOCK) for start in range(half, rows_q, BLOCK)]


def place(micro, member, half, slot, tok):
    bits = (slot % 4) * 2 + slot // 4
    return pl.multiple_of(((micro ^ half) * 8 + (member ^ bits)) * tok, tok)


def attend_kernel(where_ref, *refs):
    x_refs = refs[:-8]
    w_ref, gain_ref, first_ref, mixed_ref, keep_ref, give_ref, att_ref, x_ref = refs[-8:]
    micro, member, first_query, prefix_len = where_ref[0], where_ref[1], where_ref[2], where_ref[3]
    rows_q, rows_k = att_ref.shape[0], mixed_ref.shape[0]
    tok = rows_q // 16
    for piece, ref in enumerate(x_refs):
        x_ref[2 * tok * piece : 2 * tok * (piece + 1), :] = ref[...]

    @pl.loop(0, rows_k // (4 * tok))
    def _(pair):
        rows = pl.ds(pl.multiple_of(4 * tok * pair, 4 * tok), 4 * tok)
        source = x_ref[rows, :].astype(F32)
        first = (source * rms_scale(source) * gain_ref[...]).astype(BF16)
        mixed = nt(first, w_ref[...]).astype(BF16)
        for piece in range(2):
            part, slot = (2 * pair + piece) // 8, (2 * pair + piece) % 8
            for half in range(2):
                at = part * rows_q + place(micro, member, half, slot, tok)
                here = slice((2 * piece + half) * tok, (2 * piece + half + 1) * tok)
                first_ref[pl.ds(at, tok), :] = first[here]
                mixed_ref[pl.ds(at, tok), :] = mixed[here]

    att_ref[...] = jnp.zeros_like(att_ref)
    lanes = lax.broadcasted_iota(jnp.int32, (BLOCK, PAIR_DIM), 1)
    for begin, end, width in spans(rows_q, rows_k):

        @pl.loop(0, 2 * (end - begin) // BLOCK)
        def _(step, begin=begin, width=width):
            start = pl.multiple_of(begin + (step // 2) * BLOCK, BLOCK)
            at = pl.multiple_of(first_query + start, BLOCK)
            mine = (lanes // HEAD_DIM) == step % 2
            query = mixed_ref[pl.ds(at, BLOCK), 0:PAIR_DIM]
            keys = mixed_ref[0:width, PAIR_DIM : 2 * PAIR_DIM]
            values = mixed_ref[0:width, 2 * PAIR_DIM :]
            free = begin if rows_q == rows_k else 0
            key_pos = free + lax.broadcasted_iota(jnp.int32, (BLOCK, width - free), 1)
            query_pos = at + lax.broadcasted_iota(jnp.int32, (BLOCK, width - free), 0)
            allowed = (key_pos <= query_pos) | (key_pos < prefix_len)
            scores = nt(jnp.where(mine, query * SCALE, jnp.zeros_like(query)), keys)
            masked = jnp.where(allowed, scores[:, free:], NEG)
            scores = jnp.concatenate([scores[:, :free], masked], 1) if free else masked
            top = jnp.max(scores, axis=-1, keepdims=True)
            weights = jnp.exp(scores - top)
            total = jnp.sum(weights, axis=-1, keepdims=True)
            probs = (weights * (1.0 / total)).astype(BF16)
            before = att_ref[pl.ds(start, BLOCK), :]
            att_ref[pl.ds(start, BLOCK), :] = jnp.where(mine, nn(probs, values).astype(BF16), before)
    for slot in range(8):
        here = slice(slot * tok, (slot + 1) * tok)
        keep_ref[here, :] = att_ref[pl.ds(place(micro, member, 0, slot, tok), tok), :]
        give_ref[here, :] = att_ref[pl.ds(place(micro, member, 1, slot, tok), tok), :]


def attend(where, blocks, weights, gain, rows_q):
    rows_k, width = blocks[0].shape[0] * len(blocks), blocks[0].shape[1]
    vmem = pl.BlockSpec(memory_space=pltpu.VMEM)
    return pl.pallas_call(
        attend_kernel,
        out_shape=(
            jax.ShapeDtypeStruct((rows_k, width), BF16),
            jax.ShapeDtypeStruct((rows_k, 3 * PAIR_DIM), BF16),
            jax.ShapeDtypeStruct((rows_q // 2, PAIR_DIM), BF16),
            jax.ShapeDtypeStruct((rows_q // 2, PAIR_DIM), BF16),
        ),
        in_specs=[pl.BlockSpec(memory_space=pltpu.SMEM)] + [vmem] * (len(blocks) + 2),
        out_specs=(vmem,) * 4,
        scratch_shapes=[pltpu.VMEM((rows_q, PAIR_DIM), BF16), pltpu.VMEM((rows_k, width), BF16)],
        compiler_params=pltpu.CompilerParams(vmem_limit_bytes=56 << 20),
        cost_estimate=pl.CostEstimate(
            flops=2 * rows_k * width * 3 * PAIR_DIM + 4 * rows_q * rows_k * PAIR_DIM,
            bytes_accessed=4 * rows_k * width,
            transcendentals=2 * rows_q * rows_k,
        ),
    )(where, *blocks, weights, gain)


def attend_back_kernel(where_ref, mixed_ref, own_ref, got_ref, gq_ref, *refs):
    micro, member, first_query, prefix_len = where_ref[0], where_ref[1], where_ref[2], where_ref[3]
    grad_ref = refs[-1]
    whole = len(refs) == 5
    keep_ref, give_ref, gk_ref, gv_ref = refs[:4] if whole else (None, None) + refs[:2]
    rows_q, rows_k = grad_ref.shape[0], mixed_ref.shape[0]
    tok = rows_q // 16
    for slot in range(8):
        here = slice(slot * tok, (slot + 1) * tok)
        grad_ref[pl.ds(place(micro, member, 0, slot, tok), tok), :] = own_ref[here, :]
        grad_ref[pl.ds(place(micro, member, 1, slot, tok), tok), :] = got_ref[here, :]
    lanes = lax.broadcasted_iota(jnp.int32, (BLOCK, PAIR_DIM), 1)
    gq_ref[...] = jnp.zeros_like(gq_ref)
    gk_ref[...] = jnp.zeros_like(gk_ref)
    gv_ref[...] = jnp.zeros_like(gv_ref)
    for begin, end, width in spans(rows_q, rows_k):

        @pl.loop(0, 2 * (end - begin) // BLOCK)
        def _(step, begin=begin, width=width):
            start = pl.multiple_of(begin + (step // 2) * BLOCK, BLOCK)
            at = pl.multiple_of(first_query + start, BLOCK)
            mine = (lanes // HEAD_DIM) == step % 2
            query = mixed_ref[pl.ds(at, BLOCK), 0:PAIR_DIM]
            grad = grad_ref[pl.ds(start, BLOCK), :]
            keys = mixed_ref[0:width, PAIR_DIM : 2 * PAIR_DIM]
            values = mixed_ref[0:width, 2 * PAIR_DIM :]
            free = begin if rows_q == rows_k else 0
            key_pos = free + lax.broadcasted_iota(jnp.int32, (width - free, BLOCK), 0)
            query_pos = at + lax.broadcasted_iota(jnp.int32, (width - free, BLOCK), 1)
            allowed = (key_pos <= query_pos) | (key_pos < prefix_len)
            own_query = jnp.where(mine, query * SCALE, jnp.zeros_like(query))
            own_grad = jnp.where(mine, grad, jnp.zeros_like(grad))
            scores = nt(keys, own_query)
            masked = jnp.where(allowed, scores[free:], NEG)
            scores = jnp.concatenate([scores[:free], masked], 0) if free else masked
            top = jnp.max(scores, axis=0, keepdims=True)
            weights = jnp.exp(scores - top)
            probs = weights * (1.0 / jnp.sum(weights, axis=0, keepdims=True))
            grad_probs = nt(values, own_grad)
            delta = jnp.sum(probs * grad_probs, axis=0, keepdims=True)
            grad_scores = (probs * (grad_probs - delta)).astype(BF16)
            gv_ref[0:width, :] += nn(probs.astype(BF16), own_grad)
            gk_ref[0:width, :] += nn(grad_scores, own_query)
            grad_q = (tn(grad_scores, keys) * SCALE).astype(BF16)
            before = gq_ref[pl.ds(start, BLOCK), 0:PAIR_DIM]
            gq_ref[pl.ds(start, BLOCK), 0:PAIR_DIM] = jnp.where(mine, grad_q, before)
    if whole:
        gq_ref[:, PAIR_DIM : 2 * PAIR_DIM] = gk_ref[...].astype(BF16)
        gq_ref[:, 2 * PAIR_DIM :] = gv_ref[...].astype(BF16)
        for slot in range(8):
            here = slice(slot * tok, (slot + 1) * tok)
            keep_ref[here, :] = gq_ref[pl.ds(place(micro, member, 0, slot, tok), tok), :]
            give_ref[here, :] = gq_ref[pl.ds(place(micro, member, 1, slot, tok), tok), :]


def attend_back(where, mixed, own, got):
    rows_q, rows_k = 2 * own.shape[0], mixed.shape[0]
    whole = rows_q == rows_k
    keys = jax.ShapeDtypeStruct((rows_k, PAIR_DIM), F32)
    half = jax.ShapeDtypeStruct((rows_q // 2, 3 * PAIR_DIM), BF16)
    vmem = pl.BlockSpec(memory_space=pltpu.VMEM)
    return pl.pallas_call(
        attend_back_kernel,
        out_shape=(jax.ShapeDtypeStruct((rows_q, (3 if whole else 1) * PAIR_DIM), BF16),)
        + ((half, half) if whole else (keys, keys)),
        in_specs=[pl.BlockSpec(memory_space=pltpu.SMEM)] + [vmem] * 3,
        out_specs=(vmem,) * 3,
        scratch_shapes=[pltpu.VMEM(keys.shape, F32)] * (2 if whole else 0) + [pltpu.VMEM((rows_q, PAIR_DIM), BF16)],
        compiler_params=pltpu.CompilerParams(vmem_limit_bytes=56 << 20),
        cost_estimate=pl.CostEstimate(
            flops=10 * rows_q * rows_k * PAIR_DIM,
            bytes_accessed=8 * rows_k * PAIR_DIM * 4,
            transcendentals=2 * rows_q * rows_k,
        ),
    )(where, mixed, own, got)


def shards(n_dp, n_seq, inputs, teacher, valid_mask, prefix, attn_in, attn_out, mlp_in, mlp_out, norm_gains):
    n_micro, _, tok, width = inputs.shape
    rows = n_micro * tok
    dp = lax.axis_index("dp")
    seq = lax.axis_index("seq")
    me = dp * n_seq + seq
    n_dev = n_dp * n_seq
    n_far = n_seq // 8
    member = seq % 8
    micro = (seq // 8) % 2
    part = seq // 16
    n_parts = n_seq // 16
    rows_q = 16 * tok
    part_groups = [[p * 16 + g for p in range(n_parts)] for g in range(16)]
    gain_one = norm_gains[0:1]
    gain_two = norm_gains[1:2]

    def micro_first(pair):
        return jnp.where(micro == 0, pair, pair[::-1])

    def other_micro(value):
        return swap_seq(value, 8, n_seq)

    own_in = micro_first(inputs[:, 0])

    unit = attn_in.shape[0] // 3
    n_share = PAIR_DIM // unit

    def home(share):
        pair, rest = divmod(share % n_dev, n_share)
        to_dp, to_far = divmod(rest, n_far)
        return to_dp * n_seq + to_far * 8 + pair

    my_share = member * n_share + dp * n_far + seq // 8
    third_inverse = pow(3, -1, n_dev)
    thirds = [(3 * (((my_share - t) * third_inverse) % n_dev) + t) // n_dev for t in range(3)]
    own_units = attn_in.reshape(3, unit, width)
    x_got = other_micro(own_in[1])
    down_rows = lax.ppermute(mlp_out, BOTH, [(b, (b % 2) * n_seq + b // 2) for b in range(n_dev)])
    arrived = [lax.ppermute(own_units[t], BOTH, [(i, home(3 * i + t)) for i in range(n_dev)]) for t in range(3)]
    arrived.append(lax.ppermute(attn_out, BOTH, [(i, home(i)) for i in range(n_dev)]))
    x_pair = jnp.concatenate([own_in[0], x_got], 0)
    x_pair, arrived = joint(x_pair, arrived)

    x_blocks = cube_gather(x_pair, n_seq)
    if n_parts > 1:
        whole = lax.all_gather(jnp.stack(x_blocks), "seq", axis=0, axis_index_groups=part_groups, tiled=True)
        x_blocks = [whole[i] for i in range(8 * n_parts)]

    def pick(keys, values, key):
        return jnp.where(keys[0] == key, values[0], jnp.where(keys[1] == key, values[1], values[2]))

    arrived = after(arrived, x_blocks[4])
    my_blocks = jnp.stack([pick(thirds, arrived, third) for third in range(3)] + [arrived[3]])
    here = far_spread(my_blocks, n_seq)
    there = [swap_dp(v) for v in here]

    def by_share(here, there, at):
        order = [jnp.stack([v[j] for j in range(n_far)], at) for v in (here, there)]
        if n_far > 1:
            turn = seq // 8
            for bit in range(n_far.bit_length() - 1):
                index = jnp.arange(n_far) ^ (1 << bit)
                on = (turn // (1 << bit)) % 2
                order = [jnp.where(on == 1, jnp.take(v, index, axis=at), v) for v in order]
        first = jnp.where(dp == 0, order[0], order[1])
        second = jnp.where(dp == 0, order[1], order[0])
        return jnp.stack([first, second], at)

    head_w = by_share(here, there, 1).reshape(4 * PAIR_DIM, width)
    pair_w, out_w = head_w[: 3 * PAIR_DIM], head_w[3 * PAIR_DIM :]

    prefix_len = jnp.where(micro == 0, prefix[0, 0], prefix[1, 0])
    where = jnp.stack([micro, member, part * rows_q, prefix_len]).astype(jnp.int32)
    x_blocks, pair_w, out_w, late_in = joint(x_blocks, pair_w, out_w, mlp_in)
    ffn_here = far_spread(late_in, n_seq)
    ffn_there = [swap_dp(late_in)]
    first_in, mixed, att_keep, att_give = attend(where, x_blocks, pair_w, gain_one, rows_q)
    att_keep, ffn_here, ffn_there, down_rows = joint(att_keep, ffn_here, ffn_there, down_rows)
    down_here = far_spread(down_rows, n_seq)
    down_there = [swap_dp(down_rows)]
    att_got = other_micro(att_give)

    ffn_there += [swap_dp(v) for v in after(ffn_here[1:], att_got)]
    down_there += [swap_dp(v) for v in after(down_here[1:], att_got)]
    in_rows = mlp_in.shape[0]

    def by_dp(here, there):
        return jnp.where(dp == 0, jnp.concatenate([here, there], 0), jnp.concatenate([there, here], 0))

    in_w = by_dp(*(jnp.concatenate(blocks, 0) for blocks in (ffn_here, ffn_there)))
    down_w = jnp.concatenate([by_dp(here, there) for here, there in zip(down_here, down_there)], 0)
    n_hidden = n_far * in_rows

    attended = jnp.stack([att_keep.reshape(8, tok, PAIR_DIM), att_got.reshape(8, tok, PAIR_DIM)], 1)
    attended = attended.reshape(8 * rows, PAIR_DIM)
    source = own_in.reshape(rows, width).astype(F32)
    middle = source + cube_reduce(lambda v: nn(v, out_w), attended, n_seq)[0]
    scale_two = rms_scale(middle)
    normed_two = middle * scale_two
    second_in = cube_rows((normed_two * gain_two).astype(BF16), n_seq)

    gate_up = nt(second_in, in_w)
    gate = gate_up[:, :n_hidden]
    up_part = gate_up[:, n_hidden:]
    sigmoid_gate = jax.nn.sigmoid(gate)
    silu_gate = gate * sigmoid_gate
    hidden = (silu_gate * up_part).astype(BF16)
    result = middle + cube_reduce(lambda v: nn(v, down_w), hidden, n_seq)[0]
    late_teacher, late_mask = after((teacher, valid_mask), att_got)
    target = micro_first(late_teacher[:, 0]).reshape(rows, width).astype(F32)
    row_mask = micro_first(late_mask[:, 0]).reshape(rows, 1).astype(F32)
    error = row_mask * (result - target)
    error_low = cube_rows(error.astype(BF16), n_seq)
    grad_hidden = nt(error_low, down_w)
    grad_gate = (grad_hidden * up_part * sigmoid_gate * (1.0 + gate * (1.0 - sigmoid_gate))).astype(BF16)
    grad_up = (grad_hidden * silu_gate).astype(BF16)
    grad_both = jnp.concatenate([grad_gate, grad_up], 1)
    grad_second, begun, _ = cube_reduce(lambda v: nn(v, in_w), grad_both, n_seq)

    hidden_late, both_late = after((hidden, grad_both), begun)
    down_terms = tn(hidden_late, error_low).reshape(n_far, 2, mlp_out.shape[0], width)
    in_terms = tn(both_late, second_in).reshape(n_dp, n_far, in_rows, width)
    down_got = swap_dp(jnp.where(dp == 0, down_terms[:, 1], down_terms[:, 0]).astype(BF16))
    in_got = swap_dp(jnp.where(dp == 0, in_terms[1], in_terms[0]).astype(BF16))
    down_terms = jnp.where(dp == 0, down_terms[:, 0], down_terms[:, 1])
    in_terms = jnp.where(dp == 0, in_terms[0], in_terms[1])

    grad_middle = error + norm_back(grad_second, normed_two, scale_two, gain_two)
    middle_low = cube_rows(grad_middle.astype(BF16), n_seq)
    grad_att = nt(middle_low, out_w).astype(BF16).reshape(8, 2, tok, PAIR_DIM)
    grad_keep = grad_att[:, 0].reshape(8 * tok, PAIR_DIM)
    grad_got = other_micro(grad_att[:, 1].reshape(8 * tok, PAIR_DIM))

    in_terms = in_terms + after(in_got, grad_got).astype(F32)
    in_pairs = in_terms.reshape((n_far // 2, 2) + in_terms.shape[1:])
    half_rows = 3 * in_rows // 4
    in_low = swap_seq(in_pairs[:, 1, :half_rows].astype(BF16), 8, n_seq)
    grads = attend_back(where, mixed, grad_keep, grad_got)
    if n_parts > 1:
        grad_k, grad_v = (
            lax.psum_scatter(v, "seq", scatter_dimension=0, axis_index_groups=part_groups, tiled=True).astype(BF16)
            for v in grads[1:]
        )
        grad_mixed = jnp.concatenate([grads[0], grad_k, grad_v], 1)
        first_part = lax.dynamic_slice_in_dim(first_in, part * rows_q, rows_q, 0)
        places = (member ^ jnp.array(CUBE, jnp.int32)) + 8 * micro
        by_rows = grad_mixed.reshape(16, tok, 3 * PAIR_DIM)
        mixed_keep, mixed_give = (by_rows[p].reshape(8 * tok, 3 * PAIR_DIM) for p in (places, places ^ 8))
    else:
        grad_mixed, mixed_keep, mixed_give = grads
        first_part = first_in
    mixed_give, mixed_keep, grad_mixed, in_low, first_part, down_got = joint(
        mixed_give, mixed_keep, grad_mixed, in_low, first_part, down_got
    )
    mixed_got = other_micro(mixed_give)

    pair_terms = tn(grad_mixed, first_part)
    gain_term = jnp.sum(pair_terms * pair_w.astype(F32), axis=0) / gain_one[0]
    terms = jnp.concatenate([pair_terms, tn(attended, middle_low)], 0).reshape(4, n_dp, n_far, unit, width)
    terms_got = swap_dp(jnp.where(dp == 0, terms[:, 1], terms[:, 0]).astype(BF16))
    mixed_got, terms_got = joint(mixed_got, terms_got)
    terms = jnp.where(dp == 0, terms[:, 0], terms[:, 1]) + terms_got.astype(F32)

    mixed_rows = jnp.stack([v.reshape(8, tok, 3 * PAIR_DIM) for v in (mixed_keep, mixed_got)], 1)
    in_rest = swap_seq(after(in_pairs, mixed_got)[:, 1, half_rows:].astype(BF16), 8, n_seq)
    grad_first, last, in_rest = cube_reduce(
        lambda v: nn(v, pair_w), mixed_rows.reshape(8 * rows, 3 * PAIR_DIM), n_seq, in_rest
    )
    in_low = after(jnp.concatenate([in_low, in_rest], 1), grad_first)
    mlp_in_grad = far_reduce(in_pairs[:, 0] + in_low.astype(F32), [grad_first], n_seq, 16)
    down_terms = down_terms + after(down_got, mixed_got).astype(F32)
    down_sum = far_reduce(down_terms, [last], n_seq)
    mlp_out_grad = lax.ppermute(
        down_sum.astype(BF16), BOTH, [((b % 2) * n_seq + b // 2, b) for b in range(n_dev)]
    )

    scale_one = rms_scale(source)
    input_grad = grad_middle + norm_back(grad_first, source * scale_one, scale_one, gain_one)
    mlp_out_grad = after(mlp_out_grad, grad_first).astype(F32)

    bits = 8
    while bits < n_seq:
        on = (seq // bits) % 2
        pairs = terms.reshape((terms.shape[0], terms.shape[1] // 2, 2) + terms.shape[2:])
        give = jnp.where(on == 0, pairs[:, :, 1], pairs[:, :, 0]).astype(BF16)
        got = after(swap_seq(give, bits, n_seq), grad_first)
        terms = jnp.where(on == 0, pairs[:, :, 0], pairs[:, :, 1]) + got.astype(F32)
        bits *= 2
    terms = terms[:, 0].astype(BF16)
    attn_out_grad = lax.ppermute(terms[3], BOTH, [(home(i), i) for i in range(n_dev)]).astype(F32)
    returned = [
        lax.ppermute(
            jnp.where(thirds[t] == 0, terms[0], jnp.where(thirds[t] == 1, terms[1], terms[2])),
            BOTH,
            [(home(3 * i + t), i) for i in range(n_dev)],
        )
        for t in range(3)
    ]
    attn_in_grad = jnp.concatenate(returned, 0).astype(F32)

    squares = micro_first(jnp.sum((error * error).reshape(n_micro, tok * width), axis=1))
    scalars = jnp.zeros((width,), F32).at[0:2].set(squares).at[2].set(jnp.sum(row_mask))
    sums = jnp.stack([gain_term, jnp.sum(grad_second * normed_two, axis=0), scalars])
    sums = sums + swap_seq(sums, 1, n_seq)
    sums = sums + swap_dp(sums)
    bits = 2
    while bits < n_seq:
        sums = sums + after(swap_seq(sums, bits, n_seq), mixed_keep if bits < 8 else last)
        bits *= 2
    losses = sums[2, 0:2] / (width * sums[2, 2])

    def by_micro(value):
        return micro_first(value.reshape(n_micro, 1, tok, width))

    return (
        by_micro(result.astype(BF16)),
        losses,
        by_micro(input_grad),
        attn_in_grad,
        attn_out_grad,
        mlp_in_grad,
        mlp_out_grad,
        sums[0:2],
    )


def solution(mesh):
    n_dp, n_seq = mesh.shape["dp"], mesh.shape["seq"]
    placed = (
        P(None, "dp", "seq", None),
        P(None, "dp", "seq", None),
        P(None, "dp", "seq"),
        P(None, "dp"),
        P(BOTH, None),
        P(BOTH, None),
        P(BOTH, None),
        P(BOTH, None),
        P(),
    )
    return jax.shard_map(
        functools.partial(shards, n_dp, n_seq),
        mesh=mesh,
        in_specs=placed,
        out_specs=(
            P(None, "dp", "seq", None),
            P(),
            P(None, "dp", "seq", None),
            P(BOTH, None),
            P(BOTH, None),
            P(BOTH, None),
            P(BOTH, None),
            P(),
        ),
        check_vma=False,
    )
```

```python
import functools

import jax
import jax.numpy as jnp
from jax import lax
from jax.experimental import pallas as pl
from jax.experimental.pallas import tpu as pltpu
from jax.sharding import PartitionSpec as P

HEADS = 16
HEAD_DIM = 64
PAIR_DIM = 2 * HEAD_DIM
SCALE = HEAD_DIM**-0.5
EPS = 1e-05
NEG = -1e30
F32 = jnp.float32
BF16 = jnp.bfloat16
BOTH = ("dp", "seq")
BLOCK = 256
CUBE = (0, 2, 4, 6, 1, 3, 5, 7)


def rms_scale(rows):
    return lax.rsqrt(jnp.mean(rows * rows, axis=-1, keepdims=True) + EPS)


def nt(left, right):
    return lax.dot_general(left, right, (((1,), (1,)), ((), ())), preferred_element_type=F32)


def tn(left, right):
    return lax.dot_general(left, right, (((0,), (0,)), ((), ())), preferred_element_type=F32)


def nn(left, right):
    return jnp.dot(left, right, preferred_element_type=F32)


def norm_back(grad_norm, normed, scale_rows, gain):
    scaled = grad_norm * gain
    return scale_rows * (scaled - normed * jnp.mean(scaled * normed, axis=-1, keepdims=True))


def swap_seq(value, bits, n_seq):
    return lax.ppermute(value, "seq", [(i, i ^ bits) for i in range(n_seq)])


def swap_dp(value):
    return lax.ppermute(value, "dp", [(0, 1), (1, 0)])


def cube_gather(own, n_seq):
    half = own.shape[0] // 2
    by_one = swap_seq(own, 2, n_seq)
    by_two = swap_seq(own, 4, n_seq)
    by_core = swap_seq(own, 1, n_seq)
    across = jnp.concatenate([swap_seq(by_two[:half], 2, n_seq), swap_seq(by_one[half:], 4, n_seq)], 0)
    others = [swap_seq(v, 1, n_seq) for v in (by_one, by_two, across)]
    return [own, by_one, by_two, across, by_core] + others


def cube_rows(own, n_seq):
    return jnp.concatenate(cube_gather(own, n_seq), 0)


def cube_reduce(product, left, n_seq, hold=()):
    cut = left.shape[0] // 2
    got = swap_seq(product(left[cut:]).astype(BF16), 1, n_seq)
    got, hold = joint(got, hold)
    sums = product(left[:cut]) + got.astype(F32)
    here, for_one, for_two, for_across = sums.reshape(4, cut // 4, -1)
    half = cut // 8
    low = for_across.astype(BF16)
    via_one = swap_seq(low[:half], 2, n_seq).astype(F32)
    via_two = swap_seq(low[half:], 4, n_seq).astype(F32)
    for_two = jnp.concatenate([for_two[:half] + via_one, for_two[half:]], 0)
    for_one = jnp.concatenate([for_one[:half], for_one[half:] + via_two], 0)
    from_one = swap_seq(for_one.astype(BF16), 2, n_seq).astype(F32)
    from_two = swap_seq(for_two.astype(BF16), 4, n_seq).astype(F32)
    return here + from_one + from_two, (via_one, via_two), hold


def joint(*trees):
    leaves, shape = jax.tree.flatten(trees)
    return jax.tree.unflatten(shape, lax.optimization_barrier(tuple(leaves)))


def after(value, *others):
    return joint(value, *others)[0]


def ones_of(number):
    return bin(number).count("1")


def far_spread(own, n_seq):
    here = {0: own}
    for ones in range(1, (n_seq // 8).bit_length()):
        for j in range(1, n_seq // 8):
            if ones_of(j) == ones:
                here[j] = swap_seq(here[j & (j - 1)], 8 * (j & -j), n_seq)
    return [here[j] for j in range(n_seq // 8)]


def far_reduce(terms, gates, n_seq, bits=8):
    while terms.shape[0] > 1:
        pairs = terms.reshape((terms.shape[0] // 2, 2) + terms.shape[1:])
        got = swap_seq(pairs[:, 1].astype(BF16), bits, n_seq)
        terms = pairs[:, 0] + after(got, gates[0]).astype(F32)
        gates = gates[1:] or gates
        bits *= 2
    return terms[0]


def spans(rows_q, rows_k):
    if rows_q != rows_k:
        return [(0, rows_q, rows_k)]
    half = rows_k // 2
    return [(0, half, half)] + [(start, start + BLOCK, start + BLOCK) for start in range(half, rows_q, BLOCK)]


def place(micro, member, half, slot, tok):
    bits = (slot % 4) * 2 + slot // 4
    return pl.multiple_of(((micro ^ half) * 8 + (member ^ bits)) * tok, tok)


def attend_kernel(where_ref, *refs):
    x_refs = refs[:-8]
    w_ref, gain_ref, first_ref, mixed_ref, keep_ref, give_ref, att_ref, x_ref = refs[-8:]
    micro, member, first_query, prefix_len = where_ref[0], where_ref[1], where_ref[2], where_ref[3]
    rows_q, rows_k = att_ref.shape[0], mixed_ref.shape[0]
    tok = rows_q // 16
    for piece, ref in enumerate(x_refs):
        x_ref[2 * tok * piece : 2 * tok * (piece + 1), :] = ref[...]

    @pl.loop(0, rows_k // (4 * tok))
    def _(pair):
        rows = pl.ds(pl.multiple_of(4 * tok * pair, 4 * tok), 4 * tok)
        source = x_ref[rows, :].astype(F32)
        first = (source * rms_scale(source) * gain_ref[...]).astype(BF16)
        mixed = nt(first, w_ref[...]).astype(BF16)
        for piece in range(2):
            part, slot = (2 * pair + piece) // 8, (2 * pair + piece) % 8
            for half in range(2):
                at = part * rows_q + place(micro, member, half, slot, tok)
                here = slice((2 * piece + half) * tok, (2 * piece + half + 1) * tok)
                first_ref[pl.ds(at, tok), :] = first[here]
                mixed_ref[pl.ds(at, tok), :] = mixed[here]

    att_ref[...] = jnp.zeros_like(att_ref)
    lanes = lax.broadcasted_iota(jnp.int32, (BLOCK, PAIR_DIM), 1)
    for begin, end, width in spans(rows_q, rows_k):

        @pl.loop(0, 2 * (end - begin) // BLOCK)
        def _(step, begin=begin, width=width):
            start = pl.multiple_of(begin + (step // 2) * BLOCK, BLOCK)
            at = pl.multiple_of(first_query + start, BLOCK)
            mine = (lanes // HEAD_DIM) == step % 2
            query = mixed_ref[pl.ds(at, BLOCK), 0:PAIR_DIM]
            keys = mixed_ref[0:width, PAIR_DIM : 2 * PAIR_DIM]
            values = mixed_ref[0:width, 2 * PAIR_DIM :]
            free = begin if rows_q == rows_k else 0
            key_pos = free + lax.broadcasted_iota(jnp.int32, (BLOCK, width - free), 1)
            query_pos = at + lax.broadcasted_iota(jnp.int32, (BLOCK, width - free), 0)
            allowed = (key_pos <= query_pos) | (key_pos < prefix_len)
            scores = nt(jnp.where(mine, query * SCALE, jnp.zeros_like(query)), keys)
            masked = jnp.where(allowed, scores[:, free:], NEG)
            scores = jnp.concatenate([scores[:, :free], masked], 1) if free else masked
            top = jnp.max(scores, axis=-1, keepdims=True)
            weights = jnp.exp(scores - top)
            total = jnp.sum(weights, axis=-1, keepdims=True)
            probs = (weights * (1.0 / total)).astype(BF16)
            before = att_ref[pl.ds(start, BLOCK), :]
            att_ref[pl.ds(start, BLOCK), :] = jnp.where(mine, nn(probs, values).astype(BF16), before)
    for slot in range(8):
        here = slice(slot * tok, (slot + 1) * tok)
        keep_ref[here, :] = att_ref[pl.ds(place(micro, member, 0, slot, tok), tok), :]
        give_ref[here, :] = att_ref[pl.ds(place(micro, member, 1, slot, tok), tok), :]


def attend(where, blocks, weights, gain, rows_q):
    rows_k, width = blocks[0].shape[0] * len(blocks), blocks[0].shape[1]
    vmem = pl.BlockSpec(memory_space=pltpu.VMEM)
    return pl.pallas_call(
        attend_kernel,
        out_shape=(
            jax.ShapeDtypeStruct((rows_k, width), BF16),
            jax.ShapeDtypeStruct((rows_k, 3 * PAIR_DIM), BF16),
            jax.ShapeDtypeStruct((rows_q // 2, PAIR_DIM), BF16),
            jax.ShapeDtypeStruct((rows_q // 2, PAIR_DIM), BF16),
        ),
        in_specs=[pl.BlockSpec(memory_space=pltpu.SMEM)] + [vmem] * (len(blocks) + 2),
        out_specs=(vmem,) * 4,
        scratch_shapes=[pltpu.VMEM((rows_q, PAIR_DIM), BF16), pltpu.VMEM((rows_k, width), BF16)],
        compiler_params=pltpu.CompilerParams(vmem_limit_bytes=56 << 20),
        cost_estimate=pl.CostEstimate(
            flops=2 * rows_k * width * 3 * PAIR_DIM + 4 * rows_q * rows_k * PAIR_DIM,
            bytes_accessed=4 * rows_k * width,
            transcendentals=2 * rows_q * rows_k,
        ),
    )(where, *blocks, weights, gain)


def attend_back_kernel(where_ref, mixed_ref, own_ref, got_ref, gq_ref, *refs):
    micro, member, first_query, prefix_len = where_ref[0], where_ref[1], where_ref[2], where_ref[3]
    grad_ref = refs[-1]
    whole = len(refs) == 5
    keep_ref, give_ref, gk_ref, gv_ref = refs[:4] if whole else (None, None) + refs[:2]
    rows_q, rows_k = grad_ref.shape[0], mixed_ref.shape[0]
    tok = rows_q // 16
    for slot in range(8):
        here = slice(slot * tok, (slot + 1) * tok)
        grad_ref[pl.ds(place(micro, member, 0, slot, tok), tok), :] = own_ref[here, :]
        grad_ref[pl.ds(place(micro, member, 1, slot, tok), tok), :] = got_ref[here, :]
    lanes = lax.broadcasted_iota(jnp.int32, (BLOCK, PAIR_DIM), 1)
    gq_ref[...] = jnp.zeros_like(gq_ref)
    gk_ref[...] = jnp.zeros_like(gk_ref)
    gv_ref[...] = jnp.zeros_like(gv_ref)
    for begin, end, width in spans(rows_q, rows_k):

        @pl.loop(0, 2 * (end - begin) // BLOCK)
        def _(step, begin=begin, width=width):
            start = pl.multiple_of(begin + (step // 2) * BLOCK, BLOCK)
            at = pl.multiple_of(first_query + start, BLOCK)
            mine = (lanes // HEAD_DIM) == step % 2
            query = mixed_ref[pl.ds(at, BLOCK), 0:PAIR_DIM]
            grad = grad_ref[pl.ds(start, BLOCK), :]
            keys = mixed_ref[0:width, PAIR_DIM : 2 * PAIR_DIM]
            values = mixed_ref[0:width, 2 * PAIR_DIM :]
            free = begin if rows_q == rows_k else 0
            key_pos = free + lax.broadcasted_iota(jnp.int32, (width - free, BLOCK), 0)
            query_pos = at + lax.broadcasted_iota(jnp.int32, (width - free, BLOCK), 1)
            allowed = (key_pos <= query_pos) | (key_pos < prefix_len)
            own_query = jnp.where(mine, query * SCALE, jnp.zeros_like(query))
            own_grad = jnp.where(mine, grad, jnp.zeros_like(grad))
            scores = nt(keys, own_query)
            masked = jnp.where(allowed, scores[free:], NEG)
            scores = jnp.concatenate([scores[:free], masked], 0) if free else masked
            top = jnp.max(scores, axis=0, keepdims=True)
            weights = jnp.exp(scores - top)
            probs = weights * (1.0 / jnp.sum(weights, axis=0, keepdims=True))
            grad_probs = nt(values, own_grad)
            delta = jnp.sum(probs * grad_probs, axis=0, keepdims=True)
            grad_scores = (probs * (grad_probs - delta)).astype(BF16)
            gv_ref[0:width, :] += nn(probs.astype(BF16), own_grad)
            gk_ref[0:width, :] += nn(grad_scores, own_query)
            grad_q = (tn(grad_scores, keys) * SCALE).astype(BF16)
            before = gq_ref[pl.ds(start, BLOCK), 0:PAIR_DIM]
            gq_ref[pl.ds(start, BLOCK), 0:PAIR_DIM] = jnp.where(mine, grad_q, before)
    if whole:
        gq_ref[:, PAIR_DIM : 2 * PAIR_DIM] = gk_ref[...].astype(BF16)
        gq_ref[:, 2 * PAIR_DIM :] = gv_ref[...].astype(BF16)
        for slot in range(8):
            here = slice(slot * tok, (slot + 1) * tok)
            keep_ref[here, :] = gq_ref[pl.ds(place(micro, member, 0, slot, tok), tok), :]
            give_ref[here, :] = gq_ref[pl.ds(place(micro, member, 1, slot, tok), tok), :]


def attend_back(where, mixed, own, got):
    rows_q, rows_k = 2 * own.shape[0], mixed.shape[0]
    whole = rows_q == rows_k
    keys = jax.ShapeDtypeStruct((rows_k, PAIR_DIM), F32)
    half = jax.ShapeDtypeStruct((rows_q // 2, 3 * PAIR_DIM), BF16)
    vmem = pl.BlockSpec(memory_space=pltpu.VMEM)
    return pl.pallas_call(
        attend_back_kernel,
        out_shape=(jax.ShapeDtypeStruct((rows_q, (3 if whole else 1) * PAIR_DIM), BF16),)
        + ((half, half) if whole else (keys, keys)),
        in_specs=[pl.BlockSpec(memory_space=pltpu.SMEM)] + [vmem] * 3,
        out_specs=(vmem,) * 3,
        scratch_shapes=[pltpu.VMEM(keys.shape, F32)] * (2 if whole else 0) + [pltpu.VMEM((rows_q, PAIR_DIM), BF16)],
        compiler_params=pltpu.CompilerParams(vmem_limit_bytes=56 << 20),
        cost_estimate=pl.CostEstimate(
            flops=10 * rows_q * rows_k * PAIR_DIM,
            bytes_accessed=8 * rows_k * PAIR_DIM * 4,
            transcendentals=2 * rows_q * rows_k,
        ),
    )(where, mixed, own, got)


def shards(n_dp, n_seq, inputs, teacher, valid_mask, prefix, attn_in, attn_out, mlp_in, mlp_out, norm_gains):
    n_micro, _, tok, width = inputs.shape
    rows = n_micro * tok
    dp = lax.axis_index("dp")
    seq = lax.axis_index("seq")
    me = dp * n_seq + seq
    n_dev = n_dp * n_seq
    n_far = n_seq // 8
    member = seq % 8
    micro = (seq // 8) % 2
    part = seq // 16
    n_parts = n_seq // 16
    rows_q = 16 * tok
    part_groups = [[p * 16 + g for p in range(n_parts)] for g in range(16)]
    gain_one = norm_gains[0:1]
    gain_two = norm_gains[1:2]

    def micro_first(pair):
        return jnp.where(micro == 0, pair, pair[::-1])

    def other_micro(value):
        return swap_seq(value, 8, n_seq)

    own_in = micro_first(inputs[:, 0])

    unit = attn_in.shape[0] // 3
    n_share = PAIR_DIM // unit

    def home(share):
        pair, rest = divmod(share % n_dev, n_share)
        to_dp, to_far = divmod(rest, n_far)
        return to_dp * n_seq + to_far * 8 + pair

    my_share = member * n_share + dp * n_far + seq // 8
    third_inverse = pow(3, -1, n_dev)
    thirds = [(3 * (((my_share - t) * third_inverse) % n_dev) + t) // n_dev for t in range(3)]
    own_units = attn_in.reshape(3, unit, width)
    x_got = other_micro(own_in[1])
    down_rows = lax.ppermute(mlp_out, BOTH, [(b, (b % 2) * n_seq + b // 2) for b in range(n_dev)])
    arrived = [lax.ppermute(own_units[t], BOTH, [(i, home(3 * i + t)) for i in range(n_dev)]) for t in range(3)]
    arrived.append(lax.ppermute(attn_out, BOTH, [(i, home(i)) for i in range(n_dev)]))
    x_pair = jnp.concatenate([own_in[0], x_got], 0)
    x_pair, arrived = joint(x_pair, arrived)

    x_blocks = cube_gather(x_pair, n_seq)
    if n_parts > 1:
        whole = lax.all_gather(jnp.stack(x_blocks), "seq", axis=0, axis_index_groups=part_groups, tiled=True)
        x_blocks = [whole[i] for i in range(8 * n_parts)]

    def pick(keys, values, key):
        return jnp.where(keys[0] == key, values[0], jnp.where(keys[1] == key, values[1], values[2]))

    arrived = after(arrived, x_blocks[4])
    my_blocks = jnp.stack([pick(thirds, arrived, third) for third in range(3)] + [arrived[3]])
    here = far_spread(my_blocks, n_seq)
    there = [swap_dp(v) for v in here]

    def by_share(here, there, at):
        order = [jnp.stack([v[j] for j in range(n_far)], at) for v in (here, there)]
        if n_far > 1:
            turn = seq // 8
            for bit in range(n_far.bit_length() - 1):
                index = jnp.arange(n_far) ^ (1 << bit)
                on = (turn // (1 << bit)) % 2
                order = [jnp.where(on == 1, jnp.take(v, index, axis=at), v) for v in order]
        first = jnp.where(dp == 0, order[0], order[1])
        second = jnp.where(dp == 0, order[1], order[0])
        return jnp.stack([first, second], at)

    head_w = by_share(here, there, 1).reshape(4 * PAIR_DIM, width)
    pair_w, out_w = head_w[: 3 * PAIR_DIM], head_w[3 * PAIR_DIM :]

    prefix_len = jnp.where(micro == 0, prefix[0, 0], prefix[1, 0])
    where = jnp.stack([micro, member, part * rows_q, prefix_len]).astype(jnp.int32)
    x_blocks, pair_w, out_w, late_in = joint(x_blocks, pair_w, out_w, mlp_in)
    ffn_here = far_spread(late_in, n_seq)
    ffn_there = [swap_dp(late_in)]
    first_in, mixed, att_keep, att_give = attend(where, x_blocks, pair_w, gain_one, rows_q)
    att_keep, ffn_here, ffn_there, down_rows = joint(att_keep, ffn_here, ffn_there, down_rows)
    down_here = far_spread(down_rows, n_seq)
    down_there = [swap_dp(down_rows)]
    att_got = other_micro(att_give)

    ffn_there += [swap_dp(v) for v in after(ffn_here[1:], att_got)]
    down_there += [swap_dp(v) for v in after(down_here[1:], att_got)]
    in_rows = mlp_in.shape[0]

    def by_dp(here, there):
        return jnp.where(dp == 0, jnp.concatenate([here, there], 0), jnp.concatenate([there, here], 0))

    in_w = by_dp(*(jnp.concatenate(blocks, 0) for blocks in (ffn_here, ffn_there)))
    down_w = jnp.concatenate([by_dp(here, there) for here, there in zip(down_here, down_there)], 0)
    n_hidden = n_far * in_rows

    attended = jnp.stack([att_keep.reshape(8, tok, PAIR_DIM), att_got.reshape(8, tok, PAIR_DIM)], 1)
    attended = attended.reshape(8 * rows, PAIR_DIM)
    source = own_in.reshape(rows, width).astype(F32)
    middle = source + cube_reduce(lambda v: nn(v, out_w), attended, n_seq)[0]
    scale_two = rms_scale(middle)
    normed_two = middle * scale_two
    second_in = cube_rows((normed_two * gain_two).astype(BF16), n_seq)

    gate_up = nt(second_in, in_w)
    gate = gate_up[:, :n_hidden]
    up_part = gate_up[:, n_hidden:]
    sigmoid_gate = jax.nn.sigmoid(gate)
    silu_gate = gate * sigmoid_gate
    hidden = (silu_gate * up_part).astype(BF16)
    result = middle + cube_reduce(lambda v: nn(v, down_w), hidden, n_seq)[0]
    late_teacher, late_mask = after((teacher, valid_mask), att_got)
    target = micro_first(late_teacher[:, 0]).reshape(rows, width).astype(F32)
    row_mask = micro_first(late_mask[:, 0]).reshape(rows, 1).astype(F32)
    error = row_mask * (result - target)
    error_low = cube_rows(error.astype(BF16), n_seq)
    grad_hidden = nt(error_low, down_w)
    grad_gate = (grad_hidden * up_part * sigmoid_gate * (1.0 + gate * (1.0 - sigmoid_gate))).astype(BF16)
    grad_up = (grad_hidden * silu_gate).astype(BF16)
    grad_both = jnp.concatenate([grad_gate, grad_up], 1)
    grad_second, begun, _ = cube_reduce(lambda v: nn(v, in_w), grad_both, n_seq)

    hidden_late, both_late = after((hidden, grad_both), begun)
    down_terms = tn(hidden_late, error_low).reshape(n_far, 2, mlp_out.shape[0], width)
    in_terms = tn(both_late, second_in).reshape(n_dp, n_far, in_rows, width)
    down_got = swap_dp(jnp.where(dp == 0, down_terms[:, 1], down_terms[:, 0]).astype(BF16))
    in_got = swap_dp(jnp.where(dp == 0, in_terms[1], in_terms[0]).astype(BF16))
    down_terms = jnp.where(dp == 0, down_terms[:, 0], down_terms[:, 1])
    in_terms = jnp.where(dp == 0, in_terms[0], in_terms[1])

    grad_middle = error + norm_back(grad_second, normed_two, scale_two, gain_two)
    middle_low = cube_rows(grad_middle.astype(BF16), n_seq)
    grad_att = nt(middle_low, out_w).astype(BF16).reshape(8, 2, tok, PAIR_DIM)
    grad_keep = grad_att[:, 0].reshape(8 * tok, PAIR_DIM)
    grad_got = other_micro(grad_att[:, 1].reshape(8 * tok, PAIR_DIM))

    in_terms = in_terms + after(in_got, grad_got).astype(F32)
    in_pairs = in_terms.reshape((n_far // 2, 2) + in_terms.shape[1:])
    half_rows = 7 * in_rows // 8
    in_low = swap_seq(in_pairs[:, 1, :half_rows].astype(BF16), 8, n_seq)
    grads = attend_back(where, mixed, grad_keep, grad_got)
    if n_parts > 1:
        grad_k, grad_v = (
            lax.psum_scatter(v, "seq", scatter_dimension=0, axis_index_groups=part_groups, tiled=True).astype(BF16)
            for v in grads[1:]
        )
        grad_mixed = jnp.concatenate([grads[0], grad_k, grad_v], 1)
        first_part = lax.dynamic_slice_in_dim(first_in, part * rows_q, rows_q, 0)
        places = (member ^ jnp.array(CUBE, jnp.int32)) + 8 * micro
        by_rows = grad_mixed.reshape(16, tok, 3 * PAIR_DIM)
        mixed_keep, mixed_give = (by_rows[p].reshape(8 * tok, 3 * PAIR_DIM) for p in (places, places ^ 8))
    else:
        grad_mixed, mixed_keep, mixed_give = grads
        first_part = first_in
    mixed_give, mixed_keep, grad_mixed, in_low, first_part, down_got = joint(
        mixed_give, mixed_keep, grad_mixed, in_low, first_part, down_got
    )
    mixed_got = other_micro(mixed_give)

    pair_terms = tn(grad_mixed, first_part)
    gain_term = jnp.sum(pair_terms * pair_w.astype(F32), axis=0) / gain_one[0]
    terms = jnp.concatenate([pair_terms, tn(attended, middle_low)], 0).reshape(4, n_dp, n_far, unit, width)
    terms_got = swap_dp(jnp.where(dp == 0, terms[:, 1], terms[:, 0]).astype(BF16))
    mixed_got, terms_got = joint(mixed_got, terms_got)
    terms = jnp.where(dp == 0, terms[:, 0], terms[:, 1]) + terms_got.astype(F32)

    mixed_rows = jnp.stack([v.reshape(8, tok, 3 * PAIR_DIM) for v in (mixed_keep, mixed_got)], 1)
    in_rest = swap_seq(after(in_pairs, mixed_got)[:, 1, half_rows:].astype(BF16), 8, n_seq)
    grad_first, last, in_rest = cube_reduce(
        lambda v: nn(v, pair_w), mixed_rows.reshape(8 * rows, 3 * PAIR_DIM), n_seq, in_rest
    )
    in_low = after(jnp.concatenate([in_low, in_rest], 1), grad_first)
    mlp_in_grad = far_reduce(in_pairs[:, 0] + in_low.astype(F32), [grad_first], n_seq, 16)
    down_terms = down_terms + after(down_got, mixed_got).astype(F32)
    down_sum = far_reduce(down_terms, [last], n_seq)
    mlp_out_grad = lax.ppermute(
        down_sum.astype(BF16), BOTH, [((b % 2) * n_seq + b // 2, b) for b in range(n_dev)]
    )

    scale_one = rms_scale(source)
    input_grad = grad_middle + norm_back(grad_first, source * scale_one, scale_one, gain_one)
    mlp_out_grad = after(mlp_out_grad, grad_first).astype(F32)

    bits = 8
    while bits < n_seq:
        on = (seq // bits) % 2
        pairs = terms.reshape((terms.shape[0], terms.shape[1] // 2, 2) + terms.shape[2:])
        give = jnp.where(on == 0, pairs[:, :, 1], pairs[:, :, 0]).astype(BF16)
        got = after(swap_seq(give, bits, n_seq), grad_first)
        terms = jnp.where(on == 0, pairs[:, :, 0], pairs[:, :, 1]) + got.astype(F32)
        bits *= 2
    terms = terms[:, 0].astype(BF16)
    attn_out_grad = lax.ppermute(terms[3], BOTH, [(home(i), i) for i in range(n_dev)]).astype(F32)
    returned = [
        lax.ppermute(
            jnp.where(thirds[t] == 0, terms[0], jnp.where(thirds[t] == 1, terms[1], terms[2])),
            BOTH,
            [(home(3 * i + t), i) for i in range(n_dev)],
        )
        for t in range(3)
    ]
    attn_in_grad = jnp.concatenate(returned, 0).astype(F32)

    squares = micro_first(jnp.sum((error * error).reshape(n_micro, tok * width), axis=1))
    scalars = jnp.zeros((width,), F32).at[0:2].set(squares).at[2].set(jnp.sum(row_mask))
    sums = jnp.stack([gain_term, jnp.sum(grad_second * normed_two, axis=0), scalars])
    sums = sums + swap_seq(sums, 1, n_seq)
    sums = sums + swap_dp(sums)
    bits = 2
    while bits < n_seq:
        sums = sums + after(swap_seq(sums, bits, n_seq), mixed_keep if bits < 8 else last)
        bits *= 2
    losses = sums[2, 0:2] / (width * sums[2, 2])

    def by_micro(value):
        return micro_first(value.reshape(n_micro, 1, tok, width))

    return (
        by_micro(result.astype(BF16)),
        losses,
        by_micro(input_grad),
        attn_in_grad,
        attn_out_grad,
        mlp_in_grad,
        mlp_out_grad,
        sums[0:2],
    )


def solution(mesh):
    n_dp, n_seq = mesh.shape["dp"], mesh.shape["seq"]
    placed = (
        P(None, "dp", "seq", None),
        P(None, "dp", "seq", None),
        P(None, "dp", "seq"),
        P(None, "dp"),
        P(BOTH, None),
        P(BOTH, None),
        P(BOTH, None),
        P(BOTH, None),
        P(),
    )
    return jax.shard_map(
        functools.partial(shards, n_dp, n_seq),
        mesh=mesh,
        in_specs=placed,
        out_specs=(
            P(None, "dp", "seq", None),
            P(),
            P(None, "dp", "seq", None),
            P(BOTH, None),
            P(BOTH, None),
            P(BOTH, None),
            P(BOTH, None),
            P(),
        ),
        check_vma=False,
    )
```

```python
import functools

import jax
import jax.numpy as jnp
from jax import lax
from jax.experimental import pallas as pl
from jax.experimental.pallas import tpu as pltpu
from jax.sharding import PartitionSpec as P

HEADS = 16
HEAD_DIM = 64
PAIR_DIM = 2 * HEAD_DIM
SCALE = HEAD_DIM**-0.5
EPS = 1e-05
NEG = -1e30
F32 = jnp.float32
BF16 = jnp.bfloat16
BOTH = ("dp", "seq")
BLOCK = 256
CUBE = (0, 2, 4, 6, 1, 3, 5, 7)


def rms_scale(rows):
    return lax.rsqrt(jnp.mean(rows * rows, axis=-1, keepdims=True) + EPS)


def nt(left, right):
    return lax.dot_general(left, right, (((1,), (1,)), ((), ())), preferred_element_type=F32)


def tn(left, right):
    return lax.dot_general(left, right, (((0,), (0,)), ((), ())), preferred_element_type=F32)


def nn(left, right):
    return jnp.dot(left, right, preferred_element_type=F32)


def norm_back(grad_norm, normed, scale_rows, gain):
    scaled = grad_norm * gain
    return scale_rows * (scaled - normed * jnp.mean(scaled * normed, axis=-1, keepdims=True))


def swap_seq(value, bits, n_seq):
    return lax.ppermute(value, "seq", [(i, i ^ bits) for i in range(n_seq)])


def swap_dp(value):
    return lax.ppermute(value, "dp", [(0, 1), (1, 0)])


def cube_gather(own, n_seq):
    half = own.shape[0] // 2
    by_one = swap_seq(own, 2, n_seq)
    by_two = swap_seq(own, 4, n_seq)
    by_core = swap_seq(own, 1, n_seq)
    across = jnp.concatenate([swap_seq(by_two[:half], 2, n_seq), swap_seq(by_one[half:], 4, n_seq)], 0)
    others = [swap_seq(v, 1, n_seq) for v in (by_one, by_two, across)]
    return [own, by_one, by_two, across, by_core] + others


def cube_rows(own, n_seq):
    return jnp.concatenate(cube_gather(own, n_seq), 0)


def cube_reduce(product, left, n_seq, hold=()):
    cut = left.shape[0] // 2
    got = swap_seq(product(left[cut:]).astype(BF16), 1, n_seq)
    got, hold = joint(got, hold)
    sums = product(left[:cut]) + got.astype(F32)
    here, for_one, for_two, for_across = sums.reshape(4, cut // 4, -1)
    half = cut // 8
    low = for_across.astype(BF16)
    via_one = swap_seq(low[:half], 2, n_seq).astype(F32)
    via_two = swap_seq(low[half:], 4, n_seq).astype(F32)
    for_two = jnp.concatenate([for_two[:half] + via_one, for_two[half:]], 0)
    for_one = jnp.concatenate([for_one[:half], for_one[half:] + via_two], 0)
    from_one = swap_seq(for_one.astype(BF16), 2, n_seq).astype(F32)
    from_two = swap_seq(for_two.astype(BF16), 4, n_seq).astype(F32)
    return here + from_one + from_two, (via_one, via_two), hold


def joint(*trees):
    leaves, shape = jax.tree.flatten(trees)
    return jax.tree.unflatten(shape, lax.optimization_barrier(tuple(leaves)))


def after(value, *others):
    return joint(value, *others)[0]


def ones_of(number):
    return bin(number).count("1")


def far_spread(own, n_seq):
    here = {0: own}
    for ones in range(1, (n_seq // 8).bit_length()):
        for j in range(1, n_seq // 8):
            if ones_of(j) == ones:
                here[j] = swap_seq(here[j & (j - 1)], 8 * (j & -j), n_seq)
    return [here[j] for j in range(n_seq // 8)]


def far_reduce(terms, gates, n_seq, bits=8):
    while terms.shape[0] > 1:
        pairs = terms.reshape((terms.shape[0] // 2, 2) + terms.shape[1:])
        got = swap_seq(pairs[:, 1].astype(BF16), bits, n_seq)
        terms = pairs[:, 0] + after(got, gates[0]).astype(F32)
        gates = gates[1:] or gates
        bits *= 2
    return terms[0]


def spans(rows_q, rows_k):
    if rows_q != rows_k:
        return [(0, rows_q, rows_k)]
    half = rows_k // 2
    return [(0, half, half)] + [(start, start + BLOCK, start + BLOCK) for start in range(half, rows_q, BLOCK)]


def place(micro, member, half, slot, tok):
    bits = (slot % 4) * 2 + slot // 4
    return pl.multiple_of(((micro ^ half) * 8 + (member ^ bits)) * tok, tok)


def attend_kernel(where_ref, *refs):
    x_refs = refs[:-8]
    w_ref, gain_ref, first_ref, mixed_ref, keep_ref, give_ref, att_ref, x_ref = refs[-8:]
    micro, member, first_query, prefix_len = where_ref[0], where_ref[1], where_ref[2], where_ref[3]
    rows_q, rows_k = att_ref.shape[0], mixed_ref.shape[0]
    tok = rows_q // 16
    for piece, ref in enumerate(x_refs):
        x_ref[2 * tok * piece : 2 * tok * (piece + 1), :] = ref[...]

    @pl.loop(0, rows_k // (4 * tok))
    def _(pair):
        rows = pl.ds(pl.multiple_of(4 * tok * pair, 4 * tok), 4 * tok)
        source = x_ref[rows, :].astype(F32)
        first = (source * rms_scale(source) * gain_ref[...]).astype(BF16)
        mixed = nt(first, w_ref[...]).astype(BF16)
        for piece in range(2):
            part, slot = (2 * pair + piece) // 8, (2 * pair + piece) % 8
            for half in range(2):
                at = part * rows_q + place(micro, member, half, slot, tok)
                here = slice((2 * piece + half) * tok, (2 * piece + half + 1) * tok)
                first_ref[pl.ds(at, tok), :] = first[here]
                mixed_ref[pl.ds(at, tok), :] = mixed[here]

    att_ref[...] = jnp.zeros_like(att_ref)
    lanes = lax.broadcasted_iota(jnp.int32, (BLOCK, PAIR_DIM), 1)
    for begin, end, width in spans(rows_q, rows_k):

        @pl.loop(0, 2 * (end - begin) // BLOCK)
        def _(step, begin=begin, width=width):
            start = pl.multiple_of(begin + (step // 2) * BLOCK, BLOCK)
            at = pl.multiple_of(first_query + start, BLOCK)
            mine = (lanes // HEAD_DIM) == step % 2
            query = mixed_ref[pl.ds(at, BLOCK), 0:PAIR_DIM]
            keys = mixed_ref[0:width, PAIR_DIM : 2 * PAIR_DIM]
            values = mixed_ref[0:width, 2 * PAIR_DIM :]
            free = begin if rows_q == rows_k else 0
            key_pos = free + lax.broadcasted_iota(jnp.int32, (BLOCK, width - free), 1)
            query_pos = at + lax.broadcasted_iota(jnp.int32, (BLOCK, width - free), 0)
            allowed = (key_pos <= query_pos) | (key_pos < prefix_len)
            scores = nt(jnp.where(mine, query * SCALE, jnp.zeros_like(query)), keys)
            masked = jnp.where(allowed, scores[:, free:], NEG)
            scores = jnp.concatenate([scores[:, :free], masked], 1) if free else masked
            top = jnp.max(scores, axis=-1, keepdims=True)
            weights = jnp.exp(scores - top)
            total = jnp.sum(weights, axis=-1, keepdims=True)
            probs = (weights * (1.0 / total)).astype(BF16)
            before = att_ref[pl.ds(start, BLOCK), :]
            att_ref[pl.ds(start, BLOCK), :] = jnp.where(mine, nn(probs, values).astype(BF16), before)
    for slot in range(8):
        here = slice(slot * tok, (slot + 1) * tok)
        keep_ref[here, :] = att_ref[pl.ds(place(micro, member, 0, slot, tok), tok), :]
        give_ref[here, :] = att_ref[pl.ds(place(micro, member, 1, slot, tok), tok), :]


def attend(where, blocks, weights, gain, rows_q):
    rows_k, width = blocks[0].shape[0] * len(blocks), blocks[0].shape[1]
    vmem = pl.BlockSpec(memory_space=pltpu.VMEM)
    return pl.pallas_call(
        attend_kernel,
        out_shape=(
            jax.ShapeDtypeStruct((rows_k, width), BF16),
            jax.ShapeDtypeStruct((rows_k, 3 * PAIR_DIM), BF16),
            jax.ShapeDtypeStruct((rows_q // 2, PAIR_DIM), BF16),
            jax.ShapeDtypeStruct((rows_q // 2, PAIR_DIM), BF16),
        ),
        in_specs=[pl.BlockSpec(memory_space=pltpu.SMEM)] + [vmem] * (len(blocks) + 2),
        out_specs=(vmem,) * 4,
        scratch_shapes=[pltpu.VMEM((rows_q, PAIR_DIM), BF16), pltpu.VMEM((rows_k, width), BF16)],
        compiler_params=pltpu.CompilerParams(vmem_limit_bytes=56 << 20),
        cost_estimate=pl.CostEstimate(
            flops=2 * rows_k * width * 3 * PAIR_DIM + 4 * rows_q * rows_k * PAIR_DIM,
            bytes_accessed=4 * rows_k * width,
            transcendentals=2 * rows_q * rows_k,
        ),
    )(where, *blocks, weights, gain)


def attend_back_kernel(where_ref, mixed_ref, own_ref, got_ref, gq_ref, *refs):
    micro, member, first_query, prefix_len = where_ref[0], where_ref[1], where_ref[2], where_ref[3]
    grad_ref = refs[-1]
    whole = len(refs) == 5
    keep_ref, give_ref, gk_ref, gv_ref = refs[:4] if whole else (None, None) + refs[:2]
    rows_q, rows_k = grad_ref.shape[0], mixed_ref.shape[0]
    tok = rows_q // 16
    for slot in range(8):
        here = slice(slot * tok, (slot + 1) * tok)
        grad_ref[pl.ds(place(micro, member, 0, slot, tok), tok), :] = own_ref[here, :]
        grad_ref[pl.ds(place(micro, member, 1, slot, tok), tok), :] = got_ref[here, :]
    lanes = lax.broadcasted_iota(jnp.int32, (BLOCK, PAIR_DIM), 1)
    gq_ref[...] = jnp.zeros_like(gq_ref)
    gk_ref[...] = jnp.zeros_like(gk_ref)
    gv_ref[...] = jnp.zeros_like(gv_ref)
    for begin, end, width in spans(rows_q, rows_k):

        @pl.loop(0, 2 * (end - begin) // BLOCK)
        def _(step, begin=begin, width=width):
            start = pl.multiple_of(begin + (step // 2) * BLOCK, BLOCK)
            at = pl.multiple_of(first_query + start, BLOCK)
            mine = (lanes // HEAD_DIM) == step % 2
            query = mixed_ref[pl.ds(at, BLOCK), 0:PAIR_DIM]
            grad = grad_ref[pl.ds(start, BLOCK), :]
            keys = mixed_ref[0:width, PAIR_DIM : 2 * PAIR_DIM]
            values = mixed_ref[0:width, 2 * PAIR_DIM :]
            free = begin if rows_q == rows_k else 0
            key_pos = free + lax.broadcasted_iota(jnp.int32, (width - free, BLOCK), 0)
            query_pos = at + lax.broadcasted_iota(jnp.int32, (width - free, BLOCK), 1)
            allowed = (key_pos <= query_pos) | (key_pos < prefix_len)
            own_query = jnp.where(mine, query * SCALE, jnp.zeros_like(query))
            own_grad = jnp.where(mine, grad, jnp.zeros_like(grad))
            scores = nt(keys, own_query)
            masked = jnp.where(allowed, scores[free:], NEG)
            scores = jnp.concatenate([scores[:free], masked], 0) if free else masked
            top = jnp.max(scores, axis=0, keepdims=True)
            weights = jnp.exp(scores - top)
            probs = weights * (1.0 / jnp.sum(weights, axis=0, keepdims=True))
            grad_probs = nt(values, own_grad)
            delta = jnp.sum(probs * grad_probs, axis=0, keepdims=True)
            grad_scores = (probs * (grad_probs - delta)).astype(BF16)
            gv_ref[0:width, :] += nn(probs.astype(BF16), own_grad)
            gk_ref[0:width, :] += nn(grad_scores, own_query)
            grad_q = (tn(grad_scores, keys) * SCALE).astype(BF16)
            before = gq_ref[pl.ds(start, BLOCK), 0:PAIR_DIM]
            gq_ref[pl.ds(start, BLOCK), 0:PAIR_DIM] = jnp.where(mine, grad_q, before)
    if whole:
        gq_ref[:, PAIR_DIM : 2 * PAIR_DIM] = gk_ref[...].astype(BF16)
        gq_ref[:, 2 * PAIR_DIM :] = gv_ref[...].astype(BF16)
        for slot in range(8):
            here = slice(slot * tok, (slot + 1) * tok)
            keep_ref[here, :] = gq_ref[pl.ds(place(micro, member, 0, slot, tok), tok), :]
            give_ref[here, :] = gq_ref[pl.ds(place(micro, member, 1, slot, tok), tok), :]


def attend_back(where, mixed, own, got):
    rows_q, rows_k = 2 * own.shape[0], mixed.shape[0]
    whole = rows_q == rows_k
    keys = jax.ShapeDtypeStruct((rows_k, PAIR_DIM), F32)
    half = jax.ShapeDtypeStruct((rows_q // 2, 3 * PAIR_DIM), BF16)
    vmem = pl.BlockSpec(memory_space=pltpu.VMEM)
    return pl.pallas_call(
        attend_back_kernel,
        out_shape=(jax.ShapeDtypeStruct((rows_q, (3 if whole else 1) * PAIR_DIM), BF16),)
        + ((half, half) if whole else (keys, keys)),
        in_specs=[pl.BlockSpec(memory_space=pltpu.SMEM)] + [vmem] * 3,
        out_specs=(vmem,) * 3,
        scratch_shapes=[pltpu.VMEM(keys.shape, F32)] * (2 if whole else 0) + [pltpu.VMEM((rows_q, PAIR_DIM), BF16)],
        compiler_params=pltpu.CompilerParams(vmem_limit_bytes=56 << 20),
        cost_estimate=pl.CostEstimate(
            flops=10 * rows_q * rows_k * PAIR_DIM,
            bytes_accessed=8 * rows_k * PAIR_DIM * 4,
            transcendentals=2 * rows_q * rows_k,
        ),
    )(where, mixed, own, got)


def shards(n_dp, n_seq, inputs, teacher, valid_mask, prefix, attn_in, attn_out, mlp_in, mlp_out, norm_gains):
    n_micro, _, tok, width = inputs.shape
    rows = n_micro * tok
    dp = lax.axis_index("dp")
    seq = lax.axis_index("seq")
    me = dp * n_seq + seq
    n_dev = n_dp * n_seq
    n_far = n_seq // 8
    member = seq % 8
    micro = (seq // 8) % 2
    part = seq // 16
    n_parts = n_seq // 16
    rows_q = 16 * tok
    part_groups = [[p * 16 + g for p in range(n_parts)] for g in range(16)]
    gain_one = norm_gains[0:1]
    gain_two = norm_gains[1:2]

    def micro_first(pair):
        return jnp.where(micro == 0, pair, pair[::-1])

    def other_micro(value):
        return swap_seq(value, 8, n_seq)

    own_in = micro_first(inputs[:, 0])

    unit = attn_in.shape[0] // 3
    n_share = PAIR_DIM // unit

    def home(share):
        pair, rest = divmod(share % n_dev, n_share)
        to_dp, to_far = divmod(rest, n_far)
        return to_dp * n_seq + to_far * 8 + pair

    my_share = member * n_share + dp * n_far + seq // 8
    third_inverse = pow(3, -1, n_dev)
    thirds = [(3 * (((my_share - t) * third_inverse) % n_dev) + t) // n_dev for t in range(3)]
    own_units = attn_in.reshape(3, unit, width)
    x_got = other_micro(own_in[1])
    down_rows = lax.ppermute(mlp_out, BOTH, [(b, (b % 2) * n_seq + b // 2) for b in range(n_dev)])
    arrived = [lax.ppermute(own_units[t], BOTH, [(i, home(3 * i + t)) for i in range(n_dev)]) for t in range(3)]
    arrived.append(lax.ppermute(attn_out, BOTH, [(i, home(i)) for i in range(n_dev)]))
    x_pair = jnp.concatenate([own_in[0], x_got], 0)
    x_pair, arrived = joint(x_pair, arrived)

    x_blocks = cube_gather(x_pair, n_seq)
    if n_parts > 1:
        whole = lax.all_gather(jnp.stack(x_blocks), "seq", axis=0, axis_index_groups=part_groups, tiled=True)
        x_blocks = [whole[i] for i in range(8 * n_parts)]

    def pick(keys, values, key):
        return jnp.where(keys[0] == key, values[0], jnp.where(keys[1] == key, values[1], values[2]))

    arrived = after(arrived, x_blocks[4])
    my_blocks = jnp.stack([pick(thirds, arrived, third) for third in range(3)] + [arrived[3]])
    here = far_spread(my_blocks, n_seq)
    there = [swap_dp(v) for v in here]

    def by_share(here, there, at):
        order = [jnp.stack([v[j] for j in range(n_far)], at) for v in (here, there)]
        if n_far > 1:
            turn = seq // 8
            for bit in range(n_far.bit_length() - 1):
                index = jnp.arange(n_far) ^ (1 << bit)
                on = (turn // (1 << bit)) % 2
                order = [jnp.where(on == 1, jnp.take(v, index, axis=at), v) for v in order]
        first = jnp.where(dp == 0, order[0], order[1])
        second = jnp.where(dp == 0, order[1], order[0])
        return jnp.stack([first, second], at)

    head_w = by_share(here, there, 1).reshape(4 * PAIR_DIM, width)
    pair_w, out_w = head_w[: 3 * PAIR_DIM], head_w[3 * PAIR_DIM :]

    prefix_len = jnp.where(micro == 0, prefix[0, 0], prefix[1, 0])
    where = jnp.stack([micro, member, part * rows_q, prefix_len]).astype(jnp.int32)
    x_blocks, pair_w, out_w, late_in = joint(x_blocks, pair_w, out_w, mlp_in)
    ffn_here = far_spread(late_in, n_seq)
    ffn_there = [swap_dp(late_in)]
    first_in, mixed, att_keep, att_give = attend(where, x_blocks, pair_w, gain_one, rows_q)
    att_keep, ffn_here, ffn_there, down_rows = joint(att_keep, ffn_here, ffn_there, down_rows)
    down_here = far_spread(down_rows, n_seq)
    down_there = [swap_dp(down_rows)]
    att_got = other_micro(att_give)

    ffn_there += [swap_dp(v) for v in after(ffn_here[1:], att_got)]
    down_there += [swap_dp(v) for v in after(down_here[1:], att_got)]
    in_rows = mlp_in.shape[0]

    def by_dp(here, there):
        return jnp.where(dp == 0, jnp.concatenate([here, there], 0), jnp.concatenate([there, here], 0))

    in_w = by_dp(*(jnp.concatenate(blocks, 0) for blocks in (ffn_here, ffn_there)))
    down_w = jnp.concatenate([by_dp(here, there) for here, there in zip(down_here, down_there)], 0)
    n_hidden = n_far * in_rows

    attended = jnp.stack([att_keep.reshape(8, tok, PAIR_DIM), att_got.reshape(8, tok, PAIR_DIM)], 1)
    attended = attended.reshape(8 * rows, PAIR_DIM)
    source = own_in.reshape(rows, width).astype(F32)
    middle = source + cube_reduce(lambda v: nn(v, out_w), attended, n_seq)[0]
    scale_two = rms_scale(middle)
    normed_two = middle * scale_two
    second_in = cube_rows((normed_two * gain_two).astype(BF16), n_seq)

    gate_up = nt(second_in, in_w)
    gate = gate_up[:, :n_hidden]
    up_part = gate_up[:, n_hidden:]
    sigmoid_gate = jax.nn.sigmoid(gate)
    silu_gate = gate * sigmoid_gate
    hidden = (silu_gate * up_part).astype(BF16)
    result = middle + cube_reduce(lambda v: nn(v, down_w), hidden, n_seq)[0]
    late_teacher, late_mask = after((teacher, valid_mask), att_got)
    target = micro_first(late_teacher[:, 0]).reshape(rows, width).astype(F32)
    row_mask = micro_first(late_mask[:, 0]).reshape(rows, 1).astype(F32)
    error = row_mask * (result - target)
    error_low = cube_rows(error.astype(BF16), n_seq)
    grad_hidden = nt(error_low, down_w)
    grad_gate = (grad_hidden * up_part * sigmoid_gate * (1.0 + gate * (1.0 - sigmoid_gate))).astype(BF16)
    grad_up = (grad_hidden * silu_gate).astype(BF16)
    grad_both = jnp.concatenate([grad_gate, grad_up], 1)
    grad_second, begun, _ = cube_reduce(lambda v: nn(v, in_w), grad_both, n_seq)

    hidden_late, both_late = after((hidden, grad_both), begun)
    down_terms = tn(hidden_late, error_low).reshape(n_far, 2, mlp_out.shape[0], width)
    in_terms = tn(both_late, second_in).reshape(n_dp, n_far, in_rows, width)
    down_got = swap_dp(jnp.where(dp == 0, down_terms[:, 1], down_terms[:, 0]).astype(BF16))
    in_got = swap_dp(jnp.where(dp == 0, in_terms[1], in_terms[0]).astype(BF16))
    down_terms = jnp.where(dp == 0, down_terms[:, 0], down_terms[:, 1])
    in_terms = jnp.where(dp == 0, in_terms[0], in_terms[1])

    grad_middle = error + norm_back(grad_second, normed_two, scale_two, gain_two)
    middle_low = cube_rows(grad_middle.astype(BF16), n_seq)
    grad_att = nt(middle_low, out_w).astype(BF16).reshape(8, 2, tok, PAIR_DIM)
    grad_keep = grad_att[:, 0].reshape(8 * tok, PAIR_DIM)
    grad_got = other_micro(grad_att[:, 1].reshape(8 * tok, PAIR_DIM))

    in_terms = in_terms + after(in_got, grad_got).astype(F32)
    in_pairs = in_terms.reshape((n_far // 2, 2) + in_terms.shape[1:])
    half_rows = 7 * in_rows // 8
    in_low = swap_seq(in_pairs[:, 1, :half_rows].astype(BF16), 8, n_seq)
    grads = attend_back(where, mixed, grad_keep, grad_got)
    if n_parts > 1:
        grad_k, grad_v = (
            lax.psum_scatter(v, "seq", scatter_dimension=0, axis_index_groups=part_groups, tiled=True).astype(BF16)
            for v in grads[1:]
        )
        grad_mixed = jnp.concatenate([grads[0], grad_k, grad_v], 1)
        first_part = lax.dynamic_slice_in_dim(first_in, part * rows_q, rows_q, 0)
        places = (member ^ jnp.array(CUBE, jnp.int32)) + 8 * micro
        by_rows = grad_mixed.reshape(16, tok, 3 * PAIR_DIM)
        mixed_keep, mixed_give = (by_rows[p].reshape(8 * tok, 3 * PAIR_DIM) for p in (places, places ^ 8))
    else:
        grad_mixed, mixed_keep, mixed_give = grads
        first_part = first_in
    mixed_give, mixed_keep, grad_mixed, in_low, first_part, down_got = joint(
        mixed_give, mixed_keep, grad_mixed, in_low, first_part, down_got
    )
    mixed_got = other_micro(mixed_give)

    pair_terms = tn(grad_mixed, first_part)
    gain_term = jnp.sum(pair_terms * pair_w.astype(F32), axis=0) / gain_one[0]
    terms = jnp.concatenate([pair_terms, tn(attended, middle_low)], 0).reshape(4, n_dp, n_far, unit, width)
    terms_got = swap_dp(jnp.where(dp == 0, terms[:, 1], terms[:, 0]).astype(BF16))
    mixed_got, terms_got = joint(mixed_got, terms_got)
    terms = jnp.where(dp == 0, terms[:, 0], terms[:, 1]) + terms_got.astype(F32)

    mixed_rows = jnp.stack([v.reshape(8, tok, 3 * PAIR_DIM) for v in (mixed_keep, mixed_got)], 1)
    in_rest = swap_seq(after(in_pairs, mixed_got)[:, 1, half_rows:].astype(BF16), 8, n_seq)
    grad_first, last, in_rest = cube_reduce(
        lambda v: nn(v, pair_w), mixed_rows.reshape(8 * rows, 3 * PAIR_DIM), n_seq, in_rest
    )
    in_low = after(jnp.concatenate([in_low, in_rest], 1), grad_first)
    mlp_in_grad = far_reduce(in_pairs[:, 0] + in_low.astype(F32), [grad_first], n_seq, 16)
    down_terms = down_terms + after(down_got, mixed_got).astype(F32)
    down_sum = far_reduce(down_terms, [last], n_seq)
    mlp_out_grad = lax.ppermute(
        down_sum.astype(BF16), BOTH, [((b % 2) * n_seq + b // 2, b) for b in range(n_dev)]
    )

    scale_one = rms_scale(source)
    input_grad = grad_middle + norm_back(grad_first, source * scale_one, scale_one, gain_one)
    mlp_out_grad = after(mlp_out_grad, grad_first).astype(F32)

    bits = 8
    while bits < n_seq:
        on = (seq // bits) % 2
        pairs = terms.reshape((terms.shape[0], terms.shape[1] // 2, 2) + terms.shape[2:])
        give = jnp.where(on == 0, pairs[:, :, 1], pairs[:, :, 0]).astype(BF16)
        got = after(swap_seq(give, bits, n_seq), last)
        terms = jnp.where(on == 0, pairs[:, :, 0], pairs[:, :, 1]) + got.astype(F32)
        bits *= 2
    terms = terms[:, 0].astype(BF16)
    attn_out_grad = lax.ppermute(terms[3], BOTH, [(home(i), i) for i in range(n_dev)]).astype(F32)
    returned = [
        lax.ppermute(
            jnp.where(thirds[t] == 0, terms[0], jnp.where(thirds[t] == 1, terms[1], terms[2])),
            BOTH,
            [(home(3 * i + t), i) for i in range(n_dev)],
        )
        for t in range(3)
    ]
    attn_in_grad = jnp.concatenate(returned, 0).astype(F32)

    squares = micro_first(jnp.sum((error * error).reshape(n_micro, tok * width), axis=1))
    scalars = jnp.zeros((width,), F32).at[0:2].set(squares).at[2].set(jnp.sum(row_mask))
    sums = jnp.stack([gain_term, jnp.sum(grad_second * normed_two, axis=0), scalars])
    sums = sums + swap_seq(sums, 1, n_seq)
    sums = sums + swap_dp(sums)
    bits = 2
    while bits < n_seq:
        sums = sums + after(swap_seq(sums, bits, n_seq), mixed_keep if bits < 8 else last)
        bits *= 2
    losses = sums[2, 0:2] / (width * sums[2, 2])

    def by_micro(value):
        return micro_first(value.reshape(n_micro, 1, tok, width))

    return (
        by_micro(result.astype(BF16)),
        losses,
        by_micro(input_grad),
        attn_in_grad,
        attn_out_grad,
        mlp_in_grad,
        mlp_out_grad,
        sums[0:2],
    )


def solution(mesh):
    n_dp, n_seq = mesh.shape["dp"], mesh.shape["seq"]
    placed = (
        P(None, "dp", "seq", None),
        P(None, "dp", "seq", None),
        P(None, "dp", "seq"),
        P(None, "dp"),
        P(BOTH, None),
        P(BOTH, None),
        P(BOTH, None),
        P(BOTH, None),
        P(),
    )
    return jax.shard_map(
        functools.partial(shards, n_dp, n_seq),
        mesh=mesh,
        in_specs=placed,
        out_specs=(
            P(None, "dp", "seq", None),
            P(),
            P(None, "dp", "seq", None),
            P(BOTH, None),
            P(BOTH, None),
            P(BOTH, None),
            P(BOTH, None),
            P(),
        ),
        check_vma=False,
    )
```

```python
import functools

import jax
import jax.numpy as jnp
from jax import lax
from jax.experimental import pallas as pl
from jax.experimental.pallas import tpu as pltpu
from jax.sharding import PartitionSpec as P

HEADS = 16
HEAD_DIM = 64
PAIR_DIM = 2 * HEAD_DIM
SCALE = HEAD_DIM**-0.5
EPS = 1e-05
NEG = -1e30
F32 = jnp.float32
BF16 = jnp.bfloat16
BOTH = ("dp", "seq")
BLOCK = 256
CUBE = (0, 2, 4, 6, 1, 3, 5, 7)


def rms_scale(rows):
    return lax.rsqrt(jnp.mean(rows * rows, axis=-1, keepdims=True) + EPS)


def nt(left, right):
    return lax.dot_general(left, right, (((1,), (1,)), ((), ())), preferred_element_type=F32)


def tn(left, right):
    return lax.dot_general(left, right, (((0,), (0,)), ((), ())), preferred_element_type=F32)


def nn(left, right):
    return jnp.dot(left, right, preferred_element_type=F32)


def norm_back(grad_norm, normed, scale_rows, gain):
    scaled = grad_norm * gain
    return scale_rows * (scaled - normed * jnp.mean(scaled * normed, axis=-1, keepdims=True))


def swap_seq(value, bits, n_seq):
    return lax.ppermute(value, "seq", [(i, i ^ bits) for i in range(n_seq)])


def swap_dp(value):
    return lax.ppermute(value, "dp", [(0, 1), (1, 0)])


def cube_gather(own, n_seq):
    half = own.shape[0] // 2
    by_one = swap_seq(own, 2, n_seq)
    by_two = swap_seq(own, 4, n_seq)
    by_core = swap_seq(own, 1, n_seq)
    across = jnp.concatenate([swap_seq(by_two[:half], 2, n_seq), swap_seq(by_one[half:], 4, n_seq)], 0)
    others = [swap_seq(v, 1, n_seq) for v in (by_one, by_two, across)]
    return [own, by_one, by_two, across, by_core] + others


def cube_rows(own, n_seq):
    return jnp.concatenate(cube_gather(own, n_seq), 0)


def cube_reduce(product, left, n_seq, hold=()):
    cut = left.shape[0] // 2
    got = swap_seq(product(left[cut:]).astype(BF16), 1, n_seq)
    got, hold = joint(got, hold)
    sums = product(left[:cut]) + got.astype(F32)
    here, for_one, for_two, for_across = sums.reshape(4, cut // 4, -1)
    half = cut // 8
    low = for_across.astype(BF16)
    via_one = swap_seq(low[:half], 2, n_seq).astype(F32)
    via_two = swap_seq(low[half:], 4, n_seq).astype(F32)
    for_two = jnp.concatenate([for_two[:half] + via_one, for_two[half:]], 0)
    for_one = jnp.concatenate([for_one[:half], for_one[half:] + via_two], 0)
    from_one = swap_seq(for_one.astype(BF16), 2, n_seq).astype(F32)
    from_two = swap_seq(for_two.astype(BF16), 4, n_seq).astype(F32)
    return here + from_one + from_two, (via_one, via_two), hold


def joint(*trees):
    leaves, shape = jax.tree.flatten(trees)
    return jax.tree.unflatten(shape, lax.optimization_barrier(tuple(leaves)))


def after(value, *others):
    return joint(value, *others)[0]


def ones_of(number):
    return bin(number).count("1")


def far_spread(own, n_seq):
    here = {0: own}
    for ones in range(1, (n_seq // 8).bit_length()):
        for j in range(1, n_seq // 8):
            if ones_of(j) == ones:
                here[j] = swap_seq(here[j & (j - 1)], 8 * (j & -j), n_seq)
    return [here[j] for j in range(n_seq // 8)]


def far_reduce(terms, gates, n_seq, bits=8):
    while terms.shape[0] > 1:
        pairs = terms.reshape((terms.shape[0] // 2, 2) + terms.shape[1:])
        got = swap_seq(pairs[:, 1].astype(BF16), bits, n_seq)
        terms = pairs[:, 0] + after(got, gates[0]).astype(F32)
        gates = gates[1:] or gates
        bits *= 2
    return terms[0]


def spans(rows_q, rows_k):
    if rows_q != rows_k:
        return [(0, rows_q, rows_k)]
    half = rows_k // 2
    return [(0, half, half)] + [(start, start + BLOCK, start + BLOCK) for start in range(half, rows_q, BLOCK)]


def place(micro, member, half, slot, tok):
    bits = (slot % 4) * 2 + slot // 4
    return pl.multiple_of(((micro ^ half) * 8 + (member ^ bits)) * tok, tok)


def attend_kernel(where_ref, *refs):
    x_refs = refs[:-8]
    w_ref, gain_ref, first_ref, mixed_ref, keep_ref, give_ref, att_ref, x_ref = refs[-8:]
    micro, member, first_query, prefix_len = where_ref[0], where_ref[1], where_ref[2], where_ref[3]
    rows_q, rows_k = att_ref.shape[0], mixed_ref.shape[0]
    tok = rows_q // 16
    for piece, ref in enumerate(x_refs):
        x_ref[2 * tok * piece : 2 * tok * (piece + 1), :] = ref[...]

    @pl.loop(0, rows_k // (4 * tok))
    def _(pair):
        rows = pl.ds(pl.multiple_of(4 * tok * pair, 4 * tok), 4 * tok)
        source = x_ref[rows, :].astype(F32)
        first = (source * rms_scale(source) * gain_ref[...]).astype(BF16)
        mixed = nt(first, w_ref[...]).astype(BF16)
        for piece in range(2):
            part, slot = (2 * pair + piece) // 8, (2 * pair + piece) % 8
            for half in range(2):
                at = part * rows_q + place(micro, member, half, slot, tok)
                here = slice((2 * piece + half) * tok, (2 * piece + half + 1) * tok)
                first_ref[pl.ds(at, tok), :] = first[here]
                mixed_ref[pl.ds(at, tok), :] = mixed[here]

    lanes = lax.broadcasted_iota(jnp.int32, (BLOCK, PAIR_DIM), 1)
    for begin, end, width in spans(rows_q, rows_k):

        @pl.loop(0, (end - begin) // BLOCK)
        def _(step, begin=begin, width=width):
            start = pl.multiple_of(begin + step * BLOCK, BLOCK)
            at = pl.multiple_of(first_query + start, BLOCK)
            query = mixed_ref[pl.ds(at, BLOCK), 0:PAIR_DIM] * SCALE
            keys = mixed_ref[0:width, PAIR_DIM : 2 * PAIR_DIM]
            values = mixed_ref[0:width, 2 * PAIR_DIM :]
            free = begin if rows_q == rows_k else 0
            key_pos = free + lax.broadcasted_iota(jnp.int32, (BLOCK, width - free), 1)
            query_pos = at + lax.broadcasted_iota(jnp.int32, (BLOCK, width - free), 0)
            allowed = (key_pos <= query_pos) | (key_pos < prefix_len)
            outs = []
            for head in range(2):
                scores = nt(jnp.where((lanes // HEAD_DIM) == head, query, jnp.zeros_like(query)), keys)
                masked = jnp.where(allowed, scores[:, free:], NEG)
                scores = jnp.concatenate([scores[:, :free], masked], 1) if free else masked
                weights = jnp.exp(scores - jnp.max(scores, axis=-1, keepdims=True))
                total = jnp.sum(weights, axis=-1, keepdims=True)
                outs.append(nn((weights * (1.0 / total)).astype(BF16), values))
            att_ref[pl.ds(start, BLOCK), :] = jnp.where(lanes < HEAD_DIM, outs[0], outs[1]).astype(BF16)

    for slot in range(8):
        here = slice(slot * tok, (slot + 1) * tok)
        keep_ref[here, :] = att_ref[pl.ds(place(micro, member, 0, slot, tok), tok), :]
        give_ref[here, :] = att_ref[pl.ds(place(micro, member, 1, slot, tok), tok), :]


def attend(where, blocks, weights, gain, rows_q):
    rows_k, width = blocks[0].shape[0] * len(blocks), blocks[0].shape[1]
    vmem = pl.BlockSpec(memory_space=pltpu.VMEM)
    return pl.pallas_call(
        attend_kernel,
        out_shape=(
            jax.ShapeDtypeStruct((rows_k, width), BF16),
            jax.ShapeDtypeStruct((rows_k, 3 * PAIR_DIM), BF16),
            jax.ShapeDtypeStruct((rows_q // 2, PAIR_DIM), BF16),
            jax.ShapeDtypeStruct((rows_q // 2, PAIR_DIM), BF16),
        ),
        in_specs=[pl.BlockSpec(memory_space=pltpu.SMEM)] + [vmem] * (len(blocks) + 2),
        out_specs=(vmem,) * 4,
        scratch_shapes=[pltpu.VMEM((rows_q, PAIR_DIM), BF16), pltpu.VMEM((rows_k, width), BF16)],
        compiler_params=pltpu.CompilerParams(vmem_limit_bytes=56 << 20),
        cost_estimate=pl.CostEstimate(
            flops=2 * rows_k * width * 3 * PAIR_DIM + 4 * rows_q * rows_k * PAIR_DIM,
            bytes_accessed=4 * rows_k * width,
            transcendentals=2 * rows_q * rows_k,
        ),
    )(where, *blocks, weights, gain)


def attend_back_kernel(where_ref, mixed_ref, own_ref, got_ref, gq_ref, *refs):
    micro, member, first_query, prefix_len = where_ref[0], where_ref[1], where_ref[2], where_ref[3]
    grad_ref = refs[-1]
    whole = len(refs) == 5
    keep_ref, give_ref, gk_ref, gv_ref = refs[:4] if whole else (None, None) + refs[:2]
    rows_q, rows_k = grad_ref.shape[0], mixed_ref.shape[0]
    tok = rows_q // 16
    for slot in range(8):
        here = slice(slot * tok, (slot + 1) * tok)
        grad_ref[pl.ds(place(micro, member, 0, slot, tok), tok), :] = own_ref[here, :]
        grad_ref[pl.ds(place(micro, member, 1, slot, tok), tok), :] = got_ref[here, :]
    lanes = lax.broadcasted_iota(jnp.int32, (BLOCK, PAIR_DIM), 1)
    gq_ref[...] = jnp.zeros_like(gq_ref)
    gk_ref[...] = jnp.zeros_like(gk_ref)
    gv_ref[...] = jnp.zeros_like(gv_ref)
    for begin, end, width in spans(rows_q, rows_k):

        @pl.loop(0, 2 * (end - begin) // BLOCK)
        def _(step, begin=begin, width=width):
            start = pl.multiple_of(begin + (step // 2) * BLOCK, BLOCK)
            at = pl.multiple_of(first_query + start, BLOCK)
            mine = (lanes // HEAD_DIM) == step % 2
            query = mixed_ref[pl.ds(at, BLOCK), 0:PAIR_DIM]
            grad = grad_ref[pl.ds(start, BLOCK), :]
            keys = mixed_ref[0:width, PAIR_DIM : 2 * PAIR_DIM]
            values = mixed_ref[0:width, 2 * PAIR_DIM :]
            free = begin if rows_q == rows_k else 0
            key_pos = free + lax.broadcasted_iota(jnp.int32, (width - free, BLOCK), 0)
            query_pos = at + lax.broadcasted_iota(jnp.int32, (width - free, BLOCK), 1)
            allowed = (key_pos <= query_pos) | (key_pos < prefix_len)
            own_query = jnp.where(mine, query * SCALE, jnp.zeros_like(query))
            own_grad = jnp.where(mine, grad, jnp.zeros_like(grad))
            scores = nt(keys, own_query)
            masked = jnp.where(allowed, scores[free:], NEG)
            scores = jnp.concatenate([scores[:free], masked], 0) if free else masked
            top = jnp.max(scores, axis=0, keepdims=True)
            weights = jnp.exp(scores - top)
            probs = weights * (1.0 / jnp.sum(weights, axis=0, keepdims=True))
            grad_probs = nt(values, own_grad)
            delta = jnp.sum(probs * grad_probs, axis=0, keepdims=True)
            grad_scores = (probs * (grad_probs - delta)).astype(BF16)
            gv_ref[0:width, :] += nn(probs.astype(BF16), own_grad)
            gk_ref[0:width, :] += nn(grad_scores, own_query)
            grad_q = (tn(grad_scores, keys) * SCALE).astype(BF16)
            before = gq_ref[pl.ds(start, BLOCK), 0:PAIR_DIM]
            gq_ref[pl.ds(start, BLOCK), 0:PAIR_DIM] = jnp.where(mine, grad_q, before)
    if whole:
        gq_ref[:, PAIR_DIM : 2 * PAIR_DIM] = gk_ref[...].astype(BF16)
        gq_ref[:, 2 * PAIR_DIM :] = gv_ref[...].astype(BF16)
        for slot in range(8):
            here = slice(slot * tok, (slot + 1) * tok)
            keep_ref[here, :] = gq_ref[pl.ds(place(micro, member, 0, slot, tok), tok), :]
            give_ref[here, :] = gq_ref[pl.ds(place(micro, member, 1, slot, tok), tok), :]


def attend_back(where, mixed, own, got):
    rows_q, rows_k = 2 * own.shape[0], mixed.shape[0]
    whole = rows_q == rows_k
    keys = jax.ShapeDtypeStruct((rows_k, PAIR_DIM), F32)
    half = jax.ShapeDtypeStruct((rows_q // 2, 3 * PAIR_DIM), BF16)
    vmem = pl.BlockSpec(memory_space=pltpu.VMEM)
    return pl.pallas_call(
        attend_back_kernel,
        out_shape=(jax.ShapeDtypeStruct((rows_q, (3 if whole else 1) * PAIR_DIM), BF16),)
        + ((half, half) if whole else (keys, keys)),
        in_specs=[pl.BlockSpec(memory_space=pltpu.SMEM)] + [vmem] * 3,
        out_specs=(vmem,) * 3,
        scratch_shapes=[pltpu.VMEM(keys.shape, F32)] * (2 if whole else 0) + [pltpu.VMEM((rows_q, PAIR_DIM), BF16)],
        compiler_params=pltpu.CompilerParams(vmem_limit_bytes=56 << 20),
        cost_estimate=pl.CostEstimate(
            flops=10 * rows_q * rows_k * PAIR_DIM,
            bytes_accessed=8 * rows_k * PAIR_DIM * 4,
            transcendentals=2 * rows_q * rows_k,
        ),
    )(where, mixed, own, got)


def shards(n_dp, n_seq, inputs, teacher, valid_mask, prefix, attn_in, attn_out, mlp_in, mlp_out, norm_gains):
    n_micro, _, tok, width = inputs.shape
    rows = n_micro * tok
    dp = lax.axis_index("dp")
    seq = lax.axis_index("seq")
    me = dp * n_seq + seq
    n_dev = n_dp * n_seq
    n_far = n_seq // 8
    member = seq % 8
    micro = (seq // 8) % 2
    part = seq // 16
    n_parts = n_seq // 16
    rows_q = 16 * tok
    part_groups = [[p * 16 + g for p in range(n_parts)] for g in range(16)]
    gain_one = norm_gains[0:1]
    gain_two = norm_gains[1:2]

    def micro_first(pair):
        return jnp.where(micro == 0, pair, pair[::-1])

    def other_micro(value):
        return swap_seq(value, 8, n_seq)

    own_in = micro_first(inputs[:, 0])

    unit = attn_in.shape[0] // 3
    n_share = PAIR_DIM // unit

    def home(share):
        pair, rest = divmod(share % n_dev, n_share)
        to_dp, to_far = divmod(rest, n_far)
        return to_dp * n_seq + to_far * 8 + pair

    my_share = member * n_share + dp * n_far + seq // 8
    third_inverse = pow(3, -1, n_dev)
    thirds = [(3 * (((my_share - t) * third_inverse) % n_dev) + t) // n_dev for t in range(3)]
    own_units = attn_in.reshape(3, unit, width)
    x_got = other_micro(own_in[1])
    down_rows = lax.ppermute(mlp_out, BOTH, [(b, (b % 2) * n_seq + b // 2) for b in range(n_dev)])
    arrived = [lax.ppermute(own_units[t], BOTH, [(i, home(3 * i + t)) for i in range(n_dev)]) for t in range(3)]
    arrived.append(lax.ppermute(attn_out, BOTH, [(i, home(i)) for i in range(n_dev)]))
    x_pair = jnp.concatenate([own_in[0], x_got], 0)
    x_pair, arrived = joint(x_pair, arrived)

    x_blocks = cube_gather(x_pair, n_seq)
    if n_parts > 1:
        whole = lax.all_gather(jnp.stack(x_blocks), "seq", axis=0, axis_index_groups=part_groups, tiled=True)
        x_blocks = [whole[i] for i in range(8 * n_parts)]

    def pick(keys, values, key):
        return jnp.where(keys[0] == key, values[0], jnp.where(keys[1] == key, values[1], values[2]))

    arrived = after(arrived, x_blocks[4])
    my_blocks = jnp.stack([pick(thirds, arrived, third) for third in range(3)] + [arrived[3]])
    here = far_spread(my_blocks, n_seq)
    there = [swap_dp(v) for v in here]

    def by_share(here, there, at):
        order = [jnp.stack([v[j] for j in range(n_far)], at) for v in (here, there)]
        if n_far > 1:
            turn = seq // 8
            for bit in range(n_far.bit_length() - 1):
                index = jnp.arange(n_far) ^ (1 << bit)
                on = (turn // (1 << bit)) % 2
                order = [jnp.where(on == 1, jnp.take(v, index, axis=at), v) for v in order]
        first = jnp.where(dp == 0, order[0], order[1])
        second = jnp.where(dp == 0, order[1], order[0])
        return jnp.stack([first, second], at)

    head_w = by_share(here, there, 1).reshape(4 * PAIR_DIM, width)
    pair_w, out_w = head_w[: 3 * PAIR_DIM], head_w[3 * PAIR_DIM :]

    prefix_len = jnp.where(micro == 0, prefix[0, 0], prefix[1, 0])
    where = jnp.stack([micro, member, part * rows_q, prefix_len]).astype(jnp.int32)
    x_blocks, pair_w, out_w, late_in = joint(x_blocks, pair_w, out_w, mlp_in)
    ffn_here = far_spread(late_in, n_seq)
    ffn_there = [swap_dp(late_in)]
    first_in, mixed, att_keep, att_give = attend(where, x_blocks, pair_w, gain_one, rows_q)
    att_keep, ffn_here, ffn_there, down_rows = joint(att_keep, ffn_here, ffn_there, down_rows)
    down_here = far_spread(down_rows, n_seq)
    down_there = [swap_dp(down_rows)]
    att_got = other_micro(att_give)

    ffn_there += [swap_dp(v) for v in after(ffn_here[1:], att_got)]
    down_there += [swap_dp(v) for v in after(down_here[1:], att_got)]
    in_rows = mlp_in.shape[0]

    def by_dp(here, there):
        return jnp.where(dp == 0, jnp.concatenate([here, there], 0), jnp.concatenate([there, here], 0))

    in_w = by_dp(*(jnp.concatenate(blocks, 0) for blocks in (ffn_here, ffn_there)))
    down_w = jnp.concatenate([by_dp(here, there) for here, there in zip(down_here, down_there)], 0)
    n_hidden = n_far * in_rows

    attended = jnp.stack([att_keep.reshape(8, tok, PAIR_DIM), att_got.reshape(8, tok, PAIR_DIM)], 1)
    attended = attended.reshape(8 * rows, PAIR_DIM)
    source = own_in.reshape(rows, width).astype(F32)
    middle = source + cube_reduce(lambda v: nn(v, out_w), attended, n_seq)[0]
    scale_two = rms_scale(middle)
    normed_two = middle * scale_two
    second_in = cube_rows((normed_two * gain_two).astype(BF16), n_seq)

    gate_up = nt(second_in, in_w)
    gate = gate_up[:, :n_hidden]
    up_part = gate_up[:, n_hidden:]
    sigmoid_gate = jax.nn.sigmoid(gate)
    silu_gate = gate * sigmoid_gate
    hidden = (silu_gate * up_part).astype(BF16)
    result = middle + cube_reduce(lambda v: nn(v, down_w), hidden, n_seq)[0]
    late_teacher, late_mask = after((teacher, valid_mask), att_got)
    target = micro_first(late_teacher[:, 0]).reshape(rows, width).astype(F32)
    row_mask = micro_first(late_mask[:, 0]).reshape(rows, 1).astype(F32)
    error = row_mask * (result - target)
    error_low = cube_rows(error.astype(BF16), n_seq)
    grad_hidden = nt(error_low, down_w)
    grad_gate = (grad_hidden * up_part * sigmoid_gate * (1.0 + gate * (1.0 - sigmoid_gate))).astype(BF16)
    grad_up = (grad_hidden * silu_gate).astype(BF16)
    grad_both = jnp.concatenate([grad_gate, grad_up], 1)
    grad_second, begun, _ = cube_reduce(lambda v: nn(v, in_w), grad_both, n_seq)

    hidden_late, both_late = after((hidden, grad_both), begun)
    down_terms = tn(hidden_late, error_low).reshape(n_far, 2, mlp_out.shape[0], width)
    in_terms = tn(both_late, second_in).reshape(n_dp, n_far, in_rows, width)
    down_got = swap_dp(jnp.where(dp == 0, down_terms[:, 1], down_terms[:, 0]).astype(BF16))
    in_got = swap_dp(jnp.where(dp == 0, in_terms[1], in_terms[0]).astype(BF16))
    down_terms = jnp.where(dp == 0, down_terms[:, 0], down_terms[:, 1])
    in_terms = jnp.where(dp == 0, in_terms[0], in_terms[1])

    grad_middle = error + norm_back(grad_second, normed_two, scale_two, gain_two)
    middle_low = cube_rows(grad_middle.astype(BF16), n_seq)
    grad_att = nt(middle_low, out_w).astype(BF16).reshape(8, 2, tok, PAIR_DIM)
    grad_keep = grad_att[:, 0].reshape(8 * tok, PAIR_DIM)
    grad_got = other_micro(grad_att[:, 1].reshape(8 * tok, PAIR_DIM))

    in_terms = in_terms + after(in_got, grad_got).astype(F32)
    in_pairs = in_terms.reshape((n_far // 2, 2) + in_terms.shape[1:])
    half_rows = 7 * in_rows // 8
    in_low = swap_seq(in_pairs[:, 1, :half_rows].astype(BF16), 8, n_seq)
    grads = attend_back(where, mixed, grad_keep, grad_got)
    if n_parts > 1:
        grad_k, grad_v = (
            lax.psum_scatter(v, "seq", scatter_dimension=0, axis_index_groups=part_groups, tiled=True).astype(BF16)
            for v in grads[1:]
        )
        grad_mixed = jnp.concatenate([grads[0], grad_k, grad_v], 1)
        first_part = lax.dynamic_slice_in_dim(first_in, part * rows_q, rows_q, 0)
        places = (member ^ jnp.array(CUBE, jnp.int32)) + 8 * micro
        by_rows = grad_mixed.reshape(16, tok, 3 * PAIR_DIM)
        mixed_keep, mixed_give = (by_rows[p].reshape(8 * tok, 3 * PAIR_DIM) for p in (places, places ^ 8))
    else:
        grad_mixed, mixed_keep, mixed_give = grads
        first_part = first_in
    mixed_give, mixed_keep, grad_mixed, in_low, first_part, down_got = joint(
        mixed_give, mixed_keep, grad_mixed, in_low, first_part, down_got
    )
    mixed_got = other_micro(mixed_give)

    pair_terms = tn(grad_mixed, first_part)
    gain_term = jnp.sum(pair_terms * pair_w.astype(F32), axis=0) / gain_one[0]
    terms = jnp.concatenate([pair_terms, tn(attended, middle_low)], 0).reshape(4, n_dp, n_far, unit, width)
    terms_got = swap_dp(jnp.where(dp == 0, terms[:, 1], terms[:, 0]).astype(BF16))
    mixed_got, terms_got = joint(mixed_got, terms_got)
    terms = jnp.where(dp == 0, terms[:, 0], terms[:, 1]) + terms_got.astype(F32)

    mixed_rows = jnp.stack([v.reshape(8, tok, 3 * PAIR_DIM) for v in (mixed_keep, mixed_got)], 1)
    in_rest = swap_seq(after(in_pairs, mixed_got)[:, 1, half_rows:].astype(BF16), 8, n_seq)
    grad_first, last, in_rest = cube_reduce(
        lambda v: nn(v, pair_w), mixed_rows.reshape(8 * rows, 3 * PAIR_DIM), n_seq, in_rest
    )
    in_low = after(jnp.concatenate([in_low, in_rest], 1), grad_first)
    mlp_in_grad = far_reduce(in_pairs[:, 0] + in_low.astype(F32), [grad_first], n_seq, 16)
    down_terms = down_terms + after(down_got, mixed_got).astype(F32)
    down_sum = far_reduce(down_terms, [last], n_seq)
    mlp_out_grad = lax.ppermute(
        down_sum.astype(BF16), BOTH, [((b % 2) * n_seq + b // 2, b) for b in range(n_dev)]
    )

    scale_one = rms_scale(source)
    input_grad = grad_middle + norm_back(grad_first, source * scale_one, scale_one, gain_one)
    mlp_out_grad = after(mlp_out_grad, grad_first).astype(F32)

    bits = 8
    while bits < n_seq:
        on = (seq // bits) % 2
        pairs = terms.reshape((terms.shape[0], terms.shape[1] // 2, 2) + terms.shape[2:])
        give = jnp.where(on == 0, pairs[:, :, 1], pairs[:, :, 0]).astype(BF16)
        got = after(swap_seq(give, bits, n_seq), last)
        terms = jnp.where(on == 0, pairs[:, :, 0], pairs[:, :, 1]) + got.astype(F32)
        bits *= 2
    terms = terms[:, 0].astype(BF16)
    attn_out_grad = lax.ppermute(terms[3], BOTH, [(home(i), i) for i in range(n_dev)]).astype(F32)
    returned = [
        lax.ppermute(
            jnp.where(thirds[t] == 0, terms[0], jnp.where(thirds[t] == 1, terms[1], terms[2])),
            BOTH,
            [(home(3 * i + t), i) for i in range(n_dev)],
        )
        for t in range(3)
    ]
    attn_in_grad = jnp.concatenate(returned, 0).astype(F32)

    squares = micro_first(jnp.sum((error * error).reshape(n_micro, tok * width), axis=1))
    scalars = jnp.zeros((width,), F32).at[0:2].set(squares).at[2].set(jnp.sum(row_mask))
    sums = jnp.stack([gain_term, jnp.sum(grad_second * normed_two, axis=0), scalars])
    sums = sums + swap_seq(sums, 1, n_seq)
    sums = sums + swap_dp(sums)
    bits = 2
    while bits < n_seq:
        sums = sums + after(swap_seq(sums, bits, n_seq), mixed_keep if bits < 8 else last)
        bits *= 2
    losses = sums[2, 0:2] / (width * sums[2, 2])

    def by_micro(value):
        return micro_first(value.reshape(n_micro, 1, tok, width))

    return (
        by_micro(result.astype(BF16)),
        losses,
        by_micro(input_grad),
        attn_in_grad,
        attn_out_grad,
        mlp_in_grad,
        mlp_out_grad,
        sums[0:2],
    )


def solution(mesh):
    n_dp, n_seq = mesh.shape["dp"], mesh.shape["seq"]
    placed = (
        P(None, "dp", "seq", None),
        P(None, "dp", "seq", None),
        P(None, "dp", "seq"),
        P(None, "dp"),
        P(BOTH, None),
        P(BOTH, None),
        P(BOTH, None),
        P(BOTH, None),
        P(),
    )
    return jax.shard_map(
        functools.partial(shards, n_dp, n_seq),
        mesh=mesh,
        in_specs=placed,
        out_specs=(
            P(None, "dp", "seq", None),
            P(),
            P(None, "dp", "seq", None),
            P(BOTH, None),
            P(BOTH, None),
            P(BOTH, None),
            P(BOTH, None),
            P(),
        ),
        check_vma=False,
    )
```
